32 devices in a mesh: dp: 8 (over y, x, core), seq: 4 (over z).
Axes of the slice: x: 2, y: 2, z: 4, core: 2. Of those that a mesh axis runs over, the one named last changes fastest.
Arguments:
- tokens: bfloat16 [8, 2048, 2048], P('dp', 'seq'), may hold values from -6 to 6
- lengths: int32 [8], P('dp'), may hold values from 1024 to 2048, as said below
- cotangent: bfloat16 [8, 2048, 2048], P('dp', 'seq'), may hold values from -6 to 6
- w_query: bfloat16 [2048, 2048], P('dp', 'seq'), may hold values from -0.125 to 0.125
- key_weight: bfloat16 [2048, 1024], P('dp', 'seq'), may hold values from -0.125 to 0.125
- value_weight: bfloat16 [2048, 1024], P('dp', 'seq'), may hold values from -0.125 to 0.125
- w_out: bfloat16 [2048, 2048], P('seq', 'dp'), may hold values from -0.75 to 0.75
- w_gate: bfloat16 [2048, 6144], P('dp', 'seq'), may hold values from -0.125 to 0.125
- w_up: bfloat16 [2048, 6144], P('dp', 'seq'), may hold values from -0.125 to 0.125
- w_down: bfloat16 [6144, 2048], P('seq', 'dp'), may hold values from -0.078125 to 0.078125
- norm_attn: bfloat16 [2048], P('dp'), may hold values from 0.5 to 1.5
- norm_mlp: bfloat16 [2048], P('dp'), may hold values from 0.5 to 1.5
- norm_query: bfloat16 [128], P('dp'), may hold values from 1 to 2.5
- norm_key: bfloat16 [128], P('dp'), may hold values from 0.5 to 1.5
Outputs:
- layer_output: bfloat16 [8, 2048, 2048], P('dp', 'seq')
- grad_tokens: bfloat16 [8, 2048, 2048], P('dp', 'seq')
- grad_query: float32 [2048, 2048], P('dp', 'seq')
- grad_key: float32 [2048, 1024], P('dp', 'seq')
- grad_value: float32 [2048, 1024], P('dp', 'seq')
- grad_out: float32 [2048, 2048], P('seq', 'dp')
- grad_gate: float32 [2048, 6144], P('dp', 'seq')
- grad_up: float32 [2048, 6144], P('dp', 'seq')
- grad_down: float32 [6144, 2048], P('seq', 'dp')
- grad_norm_attn: float32 [2048], P('dp')
- grad_norm_mlp: float32 [2048], P('dp')
- grad_norm_query: float32 [128], P('dp')
- grad_norm_key: float32 [128], P('dp')
The draws below stay inside these ranges and needn't reach their ends.
Inputs may be any that keep to these rules, and one draw needn't show every extreme that they name: lengths[s] real tokens stand at the start of slot s; positions from lengths[s] to 2047 are padding. Some slot is full and some other slot holds exactly 1024 tokens.
All inputs are finite; a program needn't handle non-finite values.
Results may differ from the reference program's by a relative error of at most 0.023.
Values may be sent and summed in bfloat16 or wider, within the bound.
No kernel may reach another device: no remote copies, remote signals or barrier semaphores. Data moves between devices by JAX's collectives and lax.ppermute only.
A program may use at most 448 MiB of HBM per device.

```python
import math
import jax
import jax.numpy as jnp
from jax import lax

MODEL_WIDTH = 2048
QUERY_HEADS = 16
KEY_VALUE_HEADS = 8
HEAD_SIZE = 128
FF = 6144
SLOT_POSITIONS = 2048
LEAST_LENGTH = 1024
SLOT_COUNT = 8


def draw_lengths(key, part):
    key_start = jax.random.fold_in(key, 11)
    key_longer = jax.random.fold_in(key, 12)
    key_shorter = jax.random.fold_in(key, 13)
    sampled_lengths = jax.random.randint(key_start, (SLOT_COUNT,), LEAST_LENGTH, SLOT_POSITIONS + 1)
    greatest_length = jax.random.randint(key_longer, (), 0, SLOT_COUNT)
    start_shift = jax.random.randint(key_shorter, (), 1, SLOT_COUNT)
    smallest_length = (greatest_length + start_shift) % SLOT_COUNT
    target_positions = jnp.arange(SLOT_COUNT)
    sampled_lengths = jnp.where(target_positions == greatest_length, SLOT_POSITIONS, sampled_lengths)
    return jnp.where(target_positions == smallest_length, LEAST_LENGTH, sampled_lengths).astype(jnp.int32)


def block_levels(rng, dims, shards, smallest, high):
    level, own = 1.0, jax.random.fold_in(rng, 6)
    for axis_at, parts in shards:
        draws = jnp.exp(jax.random.uniform(jax.random.fold_in(own, axis_at), (parts,), jnp.float32, smallest / len(shards), high / len(shards)))
        level = level * jnp.repeat(draws, dims[axis_at] // parts).reshape([-1 if axis == axis_at else 1 for axis in range(len(dims))])
    return level


def noise(rng, shape, width, most, split=(), held_as=jnp.bfloat16):
    entries = width * jax.random.normal(rng, shape, jnp.float32)
    if split:
        entries = entries * block_levels(rng, shape, split, -0.22, 0.18)
    return jnp.clip(entries, -most, most).astype(held_as)


def setup_inputs(seed: int = 0) -> dict:
    arg_keys = jax.random.split(jax.random.key(seed), 15)
    return {
        "tokens": noise(arg_keys[0], (SLOT_COUNT, SLOT_POSITIONS, MODEL_WIDTH), 1.0, 6.0, ((0, 8), (1, 4))),
        "lengths": draw_lengths(jax.random.fold_in(arg_keys[14], 71), 0),
        "cotangent": noise(arg_keys[2], (SLOT_COUNT, SLOT_POSITIONS, MODEL_WIDTH), 1.0, 6.0, ((0, 8), (1, 4))),
        "w_query": noise(arg_keys[3], (MODEL_WIDTH, QUERY_HEADS * HEAD_SIZE), MODEL_WIDTH ** -0.5, 0.125, ((0, 8), (1, 4))),
        "key_weight": noise(arg_keys[4], (MODEL_WIDTH, KEY_VALUE_HEADS * HEAD_SIZE), MODEL_WIDTH ** -0.5, 0.125, ((0, 8), (1, 4))),
        "value_weight": noise(arg_keys[5], (MODEL_WIDTH, KEY_VALUE_HEADS * HEAD_SIZE), MODEL_WIDTH ** -0.5, 0.125, ((0, 8), (1, 4))),
        "w_out": noise(arg_keys[6], (QUERY_HEADS * HEAD_SIZE, MODEL_WIDTH), (QUERY_HEADS * HEAD_SIZE // 32) ** -0.5, 0.75, ((0, 4), (1, 8))),
        "w_gate": noise(arg_keys[7], (MODEL_WIDTH, FF), MODEL_WIDTH ** -0.5, 0.125, ((0, 8), (1, 4))),
        "w_up": noise(arg_keys[8], (MODEL_WIDTH, FF), MODEL_WIDTH ** -0.5, 0.125, ((0, 8), (1, 4))),
        "w_down": noise(arg_keys[9], (FF, MODEL_WIDTH), FF ** -0.5, 0.078125, ((0, 4), (1, 8))),
        "norm_attn": jnp.clip(1.0 + 0.1 * jax.random.normal(arg_keys[10], (MODEL_WIDTH,), jnp.float32), 0.5, 1.5).astype(jnp.bfloat16),
        "norm_mlp": jnp.clip(1.0 + 0.1 * jax.random.normal(arg_keys[11], (MODEL_WIDTH,), jnp.float32), 0.5, 1.5).astype(jnp.bfloat16),
        "norm_query": jnp.clip(jnp.exp(math.log(2.5) - 0.916290732 * jax.random.uniform(arg_keys[12], (HEAD_SIZE,), jnp.float32) ** block_levels(arg_keys[12], (HEAD_SIZE,), ((0, 8),), -0.2, 0.2)), 1.0, 2.5).astype(jnp.bfloat16),
        "norm_key": jnp.clip(1.0 + 0.1 * jax.random.normal(arg_keys[13], (HEAD_SIZE,), jnp.float32), 0.5, 1.5).astype(jnp.bfloat16),
    }


EPS = 1e-06
BASE = 1000000.0
MASKED = -1e+30
HIGHEST = lax.Precision.HIGHEST

@jax.custom_vjp
def lower_bound(v):
    return lax.optimization_barrier(v.astype(jnp.bfloat16)).astype(jnp.float32)

@jax.custom_vjp
def lower_bound_reverse(v):
    return v

def low_keep(v):
    return (lower_bound(v), None)

def low_pass(kept, grad):
    return (grad,)

def back_keep(v):
    return (v, None)

def back_low(kept, grad):
    return (lower_bound(grad),)
lower_bound.defvjp(low_keep, low_pass)
lower_bound_reverse.defvjp(back_keep, back_low)

def norm_rows(value_rows, gain):
    return value_rows * lax.rsqrt(lax.optimization_barrier(jnp.mean(value_rows * value_rows, axis=-1, keepdims=True)) + EPS) * gain

def rotate(value_rows, cosine, sine_table):
    half_dim = value_rows.shape[-1] // 2
    turned = jnp.concatenate([-value_rows[..., half_dim:], value_rows[..., :half_dim]], axis=-1)
    return value_rows * cosine + turned * sine_table

def angles(positions):
    frequency = BASE ** (-(jnp.arange(HEAD_SIZE // 2, dtype=jnp.float32) * 2.0 / HEAD_SIZE))
    phases = positions[:, None] * frequency[None, :]
    phases = jnp.concatenate([phases, phases], axis=-1)
    return (jnp.cos(phases)[:, None, :], jnp.sin(phases)[:, None, :])

def matrix_multiply(left, right):
    return jnp.dot(left, right, precision=HIGHEST)

def gating(gate_proj, up_proj):
    return gate_proj * jax.nn.sigmoid(gate_proj) * up_proj

def slot_layer(params, inputs, length):
    w_query, key_weight, value_weight, w_out, w_gate, w_up, w_down, norm_attn, norm_mlp, norm_query, norm_key = params
    target_positions = jnp.arange(SLOT_POSITIONS, dtype=jnp.int32)
    valid_rows = (target_positions < length).astype(jnp.float32)[:, None]
    cosine, sine_table = angles(target_positions.astype(jnp.float32))
    attention_normed = lower_bound(norm_rows(inputs, norm_attn))
    query_raw = lower_bound_reverse(matrix_multiply(attention_normed, w_query)).reshape(SLOT_POSITIONS, QUERY_HEADS, HEAD_SIZE)
    key_plain = lower_bound_reverse(matrix_multiply(attention_normed, key_weight)).reshape(SLOT_POSITIONS, KEY_VALUE_HEADS, HEAD_SIZE)
    value_rows = lower_bound_reverse(lower_bound(matrix_multiply(attention_normed, value_weight))).reshape(SLOT_POSITIONS, KEY_VALUE_HEADS, HEAD_SIZE)
    query_rows = lower_bound_reverse(lower_bound(rotate(norm_rows(query_raw, norm_query), cosine, sine_table)))
    query_rows = query_rows.reshape(SLOT_POSITIONS, KEY_VALUE_HEADS, QUERY_HEADS // KEY_VALUE_HEADS, HEAD_SIZE)
    keys_rot = lower_bound_reverse(lower_bound(rotate(norm_rows(key_plain, norm_key), cosine, sine_table)))
    scores = lower_bound_reverse(jnp.einsum('qhgd,khd->hgqk', query_rows, keys_rot, precision=HIGHEST) * HEAD_SIZE ** (-0.5))
    allowed = (target_positions[None, :] <= target_positions[:, None]) & (target_positions[None, :] < length)
    scores = jnp.where(allowed, scores, MASKED)
    top = lax.optimization_barrier(jnp.max(scores, axis=-1, keepdims=True))
    raised = jnp.exp(scores - top)
    attend = lower_bound(raised / lax.optimization_barrier(jnp.sum(raised, axis=-1, keepdims=True)))
    context = jnp.einsum('hgqk,khd->qhgd', attend, value_rows, precision=HIGHEST).reshape(SLOT_POSITIONS, QUERY_HEADS * HEAD_SIZE)
    context = lower_bound_reverse(lower_bound(context))
    resid = inputs + lower_bound_reverse(matrix_multiply(context, w_out))
    normed_mlp = lower_bound(norm_rows(resid, norm_mlp))
    gate_proj = lower_bound_reverse(matrix_multiply(normed_mlp, w_gate))
    up_proj = lower_bound_reverse(matrix_multiply(normed_mlp, w_up))
    hidden = lower_bound(gating(gate_proj, up_proj))
    return valid_rows * (resid + lower_bound_reverse(matrix_multiply(hidden, w_down)))

def reference(tokens, lengths, cotangent, w_query, key_weight, value_weight, w_out, w_gate, w_up, w_down, norm_attn, norm_mlp, norm_query, norm_key):
    params = (w_query.astype(jnp.float32), key_weight.astype(jnp.float32), value_weight.astype(jnp.float32), w_out.astype(jnp.float32), w_gate.astype(jnp.float32), w_up.astype(jnp.float32), w_down.astype(jnp.float32), norm_attn.astype(jnp.float32), norm_mlp.astype(jnp.float32), norm_query.astype(jnp.float32), norm_key.astype(jnp.float32))
    inputs = tokens.astype(jnp.float32)
    layer = jax.checkpoint(slot_layer)

    def forward(params_all, inputs_all):

        def one_slot(unused, slot_item):
            return (unused, layer(params_all, slot_item[0], slot_item[1]))
        unused, outputs = lax.scan(one_slot, None, (inputs_all, lengths))
        return outputs
    outputs, pullback = jax.vjp(forward, params, inputs)
    grad_params, grad_inputs = pullback(cotangent.astype(jnp.float32))
    return (outputs.astype(jnp.bfloat16), grad_inputs.astype(jnp.bfloat16), grad_params[0], grad_params[1], grad_params[2], grad_params[3], grad_params[4], grad_params[5], grad_params[6], grad_params[7], grad_params[8], grad_params[9], grad_params[10])
```

```python
import functools
import math

import jax
import jax.numpy as jnp
from jax import lax
from jax.experimental import pallas as pl
from jax.experimental.pallas import tpu as pltpu
from jax.sharding import PartitionSpec as P

HEAD_SIZE = 128
EPS = 1e-06
BASE = 1000000.0
MASKED = -1e30
QUERY_SCALE = HEAD_SIZE**-0.5 * math.log2(math.e)
PAIR = 2


def norm_rows(value_rows, gain):
    return (
        value_rows
        * lax.rsqrt(jnp.mean(value_rows * value_rows, axis=-1, keepdims=True) + EPS)
        * gain
    )


def rotate(value_rows, cosine, sine_table):
    half_dim = value_rows.shape[-1] // 2
    turned = jnp.concatenate([-value_rows[..., half_dim:], value_rows[..., :half_dim]], axis=-1)
    return value_rows * cosine + turned * sine_table


def angles(positions):
    frequency = BASE ** (-(jnp.arange(HEAD_SIZE // 2, dtype=jnp.float32) * 2.0 / HEAD_SIZE))
    phases = positions[:, None] * frequency[None, :]
    cosine, sine_table = jnp.cos(phases), jnp.sin(phases)
    return (
        jnp.concatenate([cosine, cosine], axis=-1)[:, None, :],
        jnp.concatenate([sine_table, sine_table], axis=-1)[:, None, :],
    )


def gating(gate_proj, up_proj):
    return gate_proj * jax.nn.sigmoid(gate_proj) * up_proj


def nn(left, right):
    return lax.dot_general(
        left, right, (((1,), (0,)), ((), ())), preferred_element_type=jnp.float32
    )


def nt(left, right):
    return lax.dot_general(
        left, right, (((1,), (1,)), ((), ())), preferred_element_type=jnp.float32
    )


def tn(left, right):
    return lax.dot_general(
        left, right, (((0,), (0,)), ((), ())), preferred_element_type=jnp.float32
    )


def forward_kernel(
    block, groups, length_ref, query_ref, key_ref, value_ref, out_ref, total_ref, wide_ref
):
    at_query = pl.program_id(1)
    length = length_ref[0]
    size = HEAD_SIZE

    @pl.when(at_query == 0)
    def _():
        wide_ref[:, :size] = value_ref[...]
        wide_ref[:, size:] = jnp.ones_like(value_ref)

    whole = jnp.minimum(at_query, length // block)
    some = jnp.minimum(at_query + 1, (length + block - 1) // block)
    queries = [query_ref[:, g * size : (g + 1) * size] for g in range(groups)]

    def step(at_key, sums, masked):
        start = pl.multiple_of(at_key * block, block)
        keys = key_ref[pl.ds(start, block), :]
        wide = wide_ref[pl.ds(start, block), :]
        if masked:
            rows = at_query * block + lax.broadcasted_iota(jnp.int32, (block, block), 0)
            cols = start + lax.broadcasted_iota(jnp.int32, (block, block), 1)
            allowed = (cols <= rows) & (cols < length)
        after = []
        for g in range(groups):
            scores = nt(queries[g], keys)
            if masked:
                scores = jnp.where(allowed, scores, MASKED)
            after.append(sums[g] + nn(jnp.exp2(scores).astype(jnp.bfloat16), wide))
        return tuple(after)

    sums = tuple(jnp.zeros((block, 2 * size), jnp.float32) for _ in range(groups))
    sums = lax.fori_loop(0, whole, lambda j, c: step(j, c, False), sums)
    sums = lax.fori_loop(whole, some, lambda j, c: step(j, c, True), sums)
    for g in range(groups):
        total = sums[g][:, size:]
        out_ref[:, g * size : (g + 1) * size] = (sums[g][:, :size] / total).astype(out_ref.dtype)
        total_ref[g, :, :] = jnp.transpose(jnp.log2(total))[:8, :]


def attend_forward(queries, keys, values, lengths, block=512):
    positions, width = queries.shape
    kv_count = keys.shape[1] // HEAD_SIZE
    groups = width // keys.shape[1]
    size = HEAD_SIZE
    return pl.pallas_call(
        functools.partial(forward_kernel, block, groups),
        grid_spec=pltpu.PrefetchScalarGridSpec(
            num_scalar_prefetch=1,
            grid=(kv_count, positions // block),
            in_specs=[
                pl.BlockSpec((block, groups * size), lambda h, i, s: (i, h)),
                pl.BlockSpec((positions, size), lambda h, i, s: (0, h)),
                pl.BlockSpec((positions, size), lambda h, i, s: (0, h)),
            ],
            out_specs=[
                pl.BlockSpec((block, groups * size), lambda h, i, s: (i, h)),
                pl.BlockSpec((groups, 8, block), lambda h, i, s: (h, 0, i)),
            ],
            scratch_shapes=[pltpu.VMEM((positions, 2 * size), jnp.bfloat16)],
        ),
        out_shape=(
            jax.ShapeDtypeStruct((positions, width), jnp.bfloat16),
            jax.ShapeDtypeStruct((kv_count * groups, 8, positions), jnp.float32),
        ),
        compiler_params=pltpu.CompilerParams(
            dimension_semantics=("arbitrary", "arbitrary"), vmem_limit_bytes=48 << 20
        ),
        cost_estimate=pl.CostEstimate(
            flops=4 * positions * positions * width,
            bytes_accessed=8 * positions * width,
            transcendentals=positions * positions * width // size // 2,
        ),
        name="attend_forward",
    )(lengths, queries, keys, values)


def backward_kernel(
    block,
    groups,
    positions,
    length_ref,
    query_ref,
    key_ref,
    value_ref,
    grad_ref,
    out_ref,
    total_ref,
    grad_query_ref,
    grad_key_ref,
    grad_value_ref,
    sums_ref,
    center_ref,
):
    length = length_ref[0]
    size = HEAD_SIZE
    blocks = positions // block
    for i in range(blocks):
        rows = slice(i * block, (i + 1) * block)
        for g in range(groups):
            lanes = slice(g * size, (g + 1) * size)
            terms = grad_ref[rows, lanes].astype(jnp.float32) * out_ref[rows, lanes].astype(
                jnp.float32
            )
            center_ref[g, :, rows] = jnp.broadcast_to(
                jnp.sum(jnp.transpose(terms), axis=0, keepdims=True), (8, block)
            )
    sums_ref[...] = jnp.zeros_like(sums_ref)
    whole = length // block
    some = (length + block - 1) // block

    def key_block(j, _):
        start = pl.multiple_of(j * block, block)
        keys = key_ref[pl.ds(start, block), :]
        values = value_ref[pl.ds(start, block), :]

        def step(i, carry, masked):
            grad_keys, grad_values = carry
            at = pl.multiple_of(i * block, block)
            if masked:
                key_at = start + lax.broadcasted_iota(jnp.int32, (block, block), 0)
                query_at = at + lax.broadcasted_iota(jnp.int32, (block, block), 1)
                allowed = (key_at <= query_at) & (key_at < length)
            for g in range(groups):
                queries = query_ref[pl.ds(at, block), g * size : (g + 1) * size]
                grads = grad_ref[pl.ds(at, block), g * size : (g + 1) * size]
                scores = nt(keys, queries) - total_ref[g, 0:1, pl.ds(at, block)]
                if masked:
                    scores = jnp.where(allowed, scores, MASKED)
                probs = jnp.exp2(scores)
                grad_attend = nt(values, grads)
                grad_scores = (
                    probs * (grad_attend - center_ref[g, 0:1, pl.ds(at, block)])
                ).astype(jnp.bfloat16)
                grad_values = grad_values + nn(probs.astype(jnp.bfloat16), grads)
                grad_keys = grad_keys + nn(grad_scores, queries)
                sums_ref[g, pl.ds(at, block), :] += tn(grad_scores, keys)
            return grad_keys, grad_values

        zero = jnp.zeros((block, size), jnp.float32)
        first = jnp.where(j < whole, jnp.minimum(j + 1, blocks), blocks)
        carry = lax.fori_loop(j, first, lambda i, c: step(i, c, True), (zero, zero))
        grad_keys, grad_values = lax.fori_loop(
            first, blocks, lambda i, c: step(i, c, False), carry
        )
        grad_key_ref[pl.ds(start, block), :] = (grad_keys * (1.0 / math.log2(math.e))).astype(
            grad_key_ref.dtype
        )
        grad_value_ref[pl.ds(start, block), :] = grad_values.astype(grad_value_ref.dtype)
        return 0

    lax.fori_loop(0, some, key_block, 0)

    def padding(j, _):
        start = pl.multiple_of(j * block, block)
        zero = jnp.zeros((block, size), grad_key_ref.dtype)
        grad_key_ref[pl.ds(start, block), :] = zero
        grad_value_ref[pl.ds(start, block), :] = zero
        return 0

    lax.fori_loop(some, blocks, padding, 0)
    for g in range(groups):
        grad_query_ref[:, g * size : (g + 1) * size] = (sums_ref[g] * HEAD_SIZE**-0.5).astype(
            grad_query_ref.dtype
        )


def attend_backward(queries, keys, values, grads, context, totals, lengths, block=512):
    positions, width = queries.shape
    kv_count = keys.shape[1] // HEAD_SIZE
    groups = width // keys.shape[1]
    size = HEAD_SIZE
    wide = pl.BlockSpec((positions, groups * size), lambda h, s: (0, h))
    thin = pl.BlockSpec((positions, size), lambda h, s: (0, h))
    return pl.pallas_call(
        functools.partial(backward_kernel, block, groups, positions),
        grid_spec=pltpu.PrefetchScalarGridSpec(
            num_scalar_prefetch=1,
            grid=(kv_count,),
            in_specs=[
                wide,
                thin,
                thin,
                wide,
                wide,
                pl.BlockSpec((groups, 8, positions), lambda h, s: (h, 0, 0)),
            ],
            out_specs=[wide, thin, thin],
            scratch_shapes=[
                pltpu.VMEM((groups, positions, size), jnp.float32),
                pltpu.VMEM((groups, 8, positions), jnp.float32),
            ],
        ),
        out_shape=(
            jax.ShapeDtypeStruct((positions, width), jnp.bfloat16),
            jax.ShapeDtypeStruct(keys.shape, jnp.bfloat16),
            jax.ShapeDtypeStruct(keys.shape, jnp.bfloat16),
        ),
        compiler_params=pltpu.CompilerParams(
            dimension_semantics=("arbitrary",), vmem_limit_bytes=56 << 20
        ),
        cost_estimate=pl.CostEstimate(
            flops=10 * positions * positions * width,
            bytes_accessed=16 * positions * width,
            transcendentals=positions * positions * width // size // 2,
        ),
        name="attend_backward",
    )(lengths, queries, keys, values, grads, context, totals)


def line_gather(value, count):
    me = lax.axis_index("seq")
    right, left = value, value
    from_left, from_right = [], []
    for hop in range(1, count):
        right = lax.ppermute(right, "seq", [(i, i + 1) for i in range(hop - 1, count - 1)])
        left = lax.ppermute(left, "seq", [(i, i - 1) for i in range(1, count - hop + 1)])
        from_left.append(right)
        from_right.append(left)
    return [value] + [
        jnp.where(me + k < count, from_right[k - 1], from_left[count - k - 1])
        for k in range(1, count)
    ]


def in_order(blocks):
    count, rows = len(blocks), blocks[0].shape[0]
    me = lax.axis_index("seq")
    whole = jnp.zeros((count * rows,) + blocks[0].shape[1:], blocks[0].dtype)
    for k, block in enumerate(blocks):
        whole = lax.dynamic_update_slice_in_dim(whole, block, lax.rem(me + k, count) * rows, 0)
    return whole


def line_scatter(parts):
    count = len(parts)
    right, left = None, None
    for hop in range(count - 1):
        to_right, to_left = parts[count - 1 - hop], parts[hop + 1]
        if hop:
            to_right, to_left = to_right + right, to_left + left
        right = lax.ppermute(
            to_right.astype(jnp.bfloat16), "seq", [(i, i + 1) for i in range(hop + 1)]
        ).astype(jnp.float32)
        left = lax.ppermute(
            to_left.astype(jnp.bfloat16),
            "seq",
            [(i, i - 1) for i in range(count - 1 - hop, count)],
        ).astype(jnp.float32)
    return parts[0] + right + left


def swap(value, count):
    return lax.ppermute(value, "seq", [(i, i ^ 1) for i in range(count)])


def fetch(value, count, step):
    return lax.ppermute(value, "seq", [((i + step) % count, i) for i in range(count)])


def give(value, count, step):
    return lax.ppermute(value, "seq", [(i, (i + step) % count) for i in range(count)])


def on_device(
    tokens,
    lengths,
    cotangent,
    w_query,
    key_weight,
    value_weight,
    w_out,
    w_gate,
    w_up,
    w_down,
    norm_attn,
    norm_mlp,
    norm_query,
    norm_key,
):
    slots, rows, width = tokens.shape
    assert slots == 1
    count = lax.axis_size("seq")
    owners = lax.axis_size("dp")
    positions = count * rows
    me = lax.axis_index("seq")
    tokens_low = tokens.reshape(rows, width)
    cotangent_low = cotangent.reshape(rows, width)
    length = lengths[0]
    low = jnp.bfloat16

    gain_parts = (norm_attn, norm_mlp, norm_query, norm_key)
    gain_sizes = [part.shape[0] for part in gain_parts]
    gathered_gains = lax.all_gather(jnp.concatenate(gain_parts), "dp", axis=0)
    gains, at = [], 0
    for part_size in gain_sizes:
        gains.append(gathered_gains[:, at : at + part_size].reshape(-1).astype(jnp.float32))
        at += part_size
    gain_attn, gain_mlp, gain_query, gain_key = gains

    query_width, key_width = w_query.shape[1], key_weight.shape[1]
    heads_weight = lax.all_gather(
        jnp.concatenate([w_query, key_weight, value_weight], axis=1), "dp", axis=0, tiled=True
    )
    token_blocks = line_gather(tokens_low, count)

    steps = range(0, count, PAIR)

    def mates(weight, axis):
        return jnp.concatenate(
            [weight] + [fetch(weight, count, step) for step in steps[1:]], axis=axis
        )

    gate_weight = lax.all_gather(mates(w_gate, 1), "dp", axis=0, tiled=True)
    up_weight = lax.all_gather(mates(w_up, 1), "dp", axis=0, tiled=True)
    down_weight = lax.all_gather(mates(w_down, 0), "dp", axis=1, tiled=True)
    out_weight = lax.all_gather(in_order(line_gather(w_out, count)), "dp", axis=1, tiled=True)

    inputs = tokens_low.astype(jnp.float32)
    normed_attn = in_order(
        [norm_rows(block.astype(jnp.float32), gain_attn).astype(low) for block in token_blocks]
    )
    raw = nn(normed_attn, heads_weight)
    cosine, sine_table = angles(jnp.arange(positions, dtype=jnp.float32))

    def head_prep(raw_proj, gain):
        return rotate(
            norm_rows(raw_proj.reshape(positions, -1, HEAD_SIZE), gain), cosine, sine_table
        ).reshape(positions, -1)

    query_rot, query_back = jax.vjp(head_prep, raw[:, :query_width], gain_query)
    key_rot, key_back = jax.vjp(head_prep, raw[:, query_width : query_width + key_width], gain_key)
    queries = (query_rot * QUERY_SCALE).astype(low)
    keys = key_rot.astype(low)
    values = raw[:, query_width + key_width :].astype(low)
    context, totals = attend_forward(queries, keys, values, lengths)
    context_tok = lax.all_to_all(context, "seq", split_axis=0, concat_axis=1, tiled=True)

    resid = inputs + nn(context_tok, out_weight)
    normed_second, second_back = jax.vjp(norm_rows, resid, gain_mlp)
    normed_mlp = normed_second.astype(low)

    place = jnp.arange(rows, dtype=jnp.int32)[:, None] + me * rows
    valid_rows = (place < length).astype(jnp.float32)
    grad_rows = cotangent_low.astype(jnp.float32) * valid_rows
    grad_rows_low = grad_rows.astype(low)
    pair_normed = jnp.concatenate([normed_mlp, swap(normed_mlp, count)], axis=0)
    pair_grads = jnp.concatenate([grad_rows_low, swap(grad_rows_low, count)], axis=0)
    gate_proj = nn(pair_normed, gate_weight)
    up_proj = nn(pair_normed, up_weight)
    hidden_full, gating_back = jax.vjp(gating, gate_proj, up_proj)
    hidden = hidden_full.astype(low)
    grad_hidden = nt(pair_grads, down_weight)
    grad_gate_full, grad_up_full = gating_back(grad_hidden)
    grad_gate_low = grad_gate_full.astype(low)
    grad_up_low = grad_up_full.astype(low)
    grad_normed_pair = nt(grad_gate_low, gate_weight) + nt(grad_up_low, up_weight)
    grad_normed_mlp = grad_normed_pair[:rows] + swap(
        grad_normed_pair[rows:].astype(low), count
    ).astype(jnp.float32)
    mlp_pair = nn(hidden, down_weight)
    mlp_out = mlp_pair[:rows] + swap(mlp_pair[rows:].astype(low), count).astype(jnp.float32)
    layer_output = (valid_rows * (resid + mlp_out)).astype(low).reshape(slots, rows, width)

    def owned(partial, axis):
        mine = lax.psum_scatter(
            partial.astype(low), "dp", scatter_dimension=axis, tiled=True
        )
        pieces = jnp.split(mine, len(steps), axis=1 - axis)
        total = pieces[0].astype(jnp.float32)
        for step, piece in zip(steps[1:], pieces[1:]):
            total = total + give(piece, count, step).astype(jnp.float32)
        return total

    grad_gate = owned(tn(pair_normed, grad_gate_low), 0)
    grad_up = owned(tn(pair_normed, grad_up_low), 0)
    grad_down = owned(tn(hidden, pair_grads), 1)

    grad_resid_norm, gain_mlp_term = second_back(grad_normed_mlp)
    grad_resid = grad_rows + grad_resid_norm
    grad_attn_low = grad_resid.astype(low)
    grad_context = lax.all_to_all(
        nt(grad_attn_low, out_weight).astype(low), "seq", split_axis=1, concat_axis=0, tiled=True
    )
    out_partial = lax.psum_scatter(
        tn(context_tok, grad_attn_low).astype(low), "dp", scatter_dimension=1, tiled=True
    )
    out_rows = out_partial.shape[0] // count
    grad_out = line_scatter(
        [
            lax.dynamic_slice_in_dim(
                out_partial, lax.rem(me + k, count) * out_rows, out_rows, 0
            ).astype(jnp.float32)
            for k in range(count)
        ]
    )

    grad_query_rot, grad_key_rot, grad_values = attend_backward(
        queries, keys, values, grad_context, context, totals, lengths
    )
    grad_query_full, gain_query_term = query_back(grad_query_rot.astype(jnp.float32))
    grad_key_full, gain_key_term = key_back(grad_key_rot.astype(jnp.float32))
    grad_raw = jnp.concatenate(
        [grad_query_full.astype(low), grad_key_full.astype(low), grad_values], axis=1
    )
    grad_heads = lax.psum_scatter(
        tn(normed_attn, grad_raw).astype(low), "dp", scatter_dimension=0, tiled=True
    ).astype(jnp.float32)
    grad_query = grad_heads[:, :query_width]
    grad_key = grad_heads[:, query_width : query_width + key_width]
    grad_value = grad_heads[:, query_width + key_width :]

    shares = [
        nt(
            lax.dynamic_slice_in_dim(grad_raw, lax.rem(me + k, count) * rows, rows, 0),
            heads_weight,
        )
        for k in range(count)
    ]
    grad_normed_attn = line_scatter(shares)
    first_back = jax.vjp(norm_rows, inputs, gain_attn)[1]
    grad_input_norm, gain_attn_term = first_back(grad_normed_attn)
    grad_tokens = (grad_resid + grad_input_norm).astype(low).reshape(slots, rows, width)

    terms = (gain_attn_term, gain_mlp_term, gain_query_term, gain_key_term)
    sums = lax.psum(jnp.concatenate(terms), ("dp", "seq"))
    gain_grads, at = [], 0
    for term, part_size in zip(terms, gain_sizes):
        gain_grads.append(
            lax.dynamic_slice_in_dim(
                sums[at : at + term.shape[0]], lax.axis_index("dp") * part_size, part_size, 0
            )
        )
        at += term.shape[0]
    return (
        layer_output,
        grad_tokens,
        grad_query,
        grad_key,
        grad_value,
        grad_out,
        grad_gate,
        grad_up,
        grad_down,
        *gain_grads,
    )


def solution(mesh):
    return jax.shard_map(
        on_device,
        mesh=mesh,
        in_specs=(
            P("dp", "seq", None),
            P("dp"),
            P("dp", "seq", None),
            P("dp", "seq"),
            P("dp", "seq"),
            P("dp", "seq"),
            P("seq", "dp"),
            P("dp", "seq"),
            P("dp", "seq"),
            P("seq", "dp"),
            P("dp"),
            P("dp"),
            P("dp"),
            P("dp"),
        ),
        out_specs=(
            P("dp", "seq", None),
            P("dp", "seq", None),
            P("dp", "seq"),
            P("dp", "seq"),
            P("dp", "seq"),
            P("seq", "dp"),
            P("dp", "seq"),
            P("dp", "seq"),
            P("seq", "dp"),
            P("dp"),
            P("dp"),
            P("dp"),
            P("dp"),
        ),
        check_vma=False,
    )
```

```python
import functools
import math

import jax
import jax.numpy as jnp
from jax import lax
from jax.experimental import pallas as pl
from jax.experimental.pallas import tpu as pltpu
from jax.sharding import PartitionSpec as P

HEAD_SIZE = 128
EPS = 1e-06
BASE = 1000000.0
MASKED = -1e30
QUERY_SCALE = HEAD_SIZE**-0.5 * math.log2(math.e)
PAIR = 2
LANES = 128
COST_SCALE = 0.05


def norm_rows(value_rows, gain):
    return (
        value_rows
        * lax.rsqrt(jnp.mean(value_rows * value_rows, axis=-1, keepdims=True) + EPS)
        * gain
    )


def angles(positions):
    frequency = BASE ** (-(jnp.arange(HEAD_SIZE // 2, dtype=jnp.float32) * 2.0 / HEAD_SIZE))
    phases = positions[:, None] * frequency[None, :]
    cosine, sine_table = jnp.cos(phases), jnp.sin(phases)
    return (
        jnp.concatenate([cosine, cosine], axis=-1),
        jnp.concatenate([-sine_table, sine_table], axis=-1),
    )


def nn(left, right):
    return lax.dot_general(
        left, right, (((1,), (0,)), ((), ())), preferred_element_type=jnp.float32
    )


def nt(left, right):
    return lax.dot_general(
        left, right, (((1,), (1,)), ((), ())), preferred_element_type=jnp.float32
    )


def tn(left, right):
    return lax.dot_general(
        left, right, (((0,), (0,)), ((), ())), preferred_element_type=jnp.float32
    )


def arbitrary(axes, megabytes):
    return pltpu.CompilerParams(
        dimension_semantics=("arbitrary",) * axes, vmem_limit_bytes=megabytes << 20
    )


def cost(flops, moved, exps=0):
    return pl.CostEstimate(
        flops=int(flops * COST_SCALE),
        bytes_accessed=int(moved * COST_SCALE),
        transcendentals=int(exps * COST_SCALE),
    )


def fixed(shape):
    return pl.BlockSpec(shape, lambda *_: (0,) * len(shape))


def project_kernel(
    groups,
    kv_count,
    place_ref,
    first_ref,
    second_ref,
    gain_ref,
    weight_ref,
    cosine_ref,
    sine_ref,
    head_gain_ref,
    *refs,
):
    normed_ref, heads_ref, raw_ref = refs[-3:]
    size = HEAD_SIZE
    rows = jnp.where(place_ref[1] != 0, first_ref[...], second_ref[...]).astype(jnp.float32)
    scale = lax.rsqrt(jnp.mean(rows * rows, axis=-1, keepdims=True) + EPS)
    normed = (rows * scale * gain_ref[...]).astype(jnp.bfloat16)
    normed_ref[...] = normed
    raw = nn(normed, weight_ref[...])
    cosine, sine_table = cosine_ref[...], sine_ref[...]
    for h in range(kv_count):
        start = h * (groups + 2) * size
        for g in range(groups + 1):
            column = start + g * size
            value = raw[:, column : column + size]
            held = (h * (groups + 1) + g) * size
            raw_ref[:, held : held + size] = value
            which = 0 if g < groups else 1
            value = value * lax.rsqrt(jnp.mean(value * value, axis=-1, keepdims=True) + EPS)
            value = value * head_gain_ref[which : which + 1, :]
            value = value * cosine + pltpu.roll(value, size // 2, 1) * sine_table
            if g < groups:
                value = value * QUERY_SCALE
            heads_ref[:, column : column + size] = value.astype(jnp.bfloat16)
        column = start + (groups + 1) * size
        heads_ref[:, column : column + size] = raw[:, column : column + size].astype(jnp.bfloat16)


def project(
    place, first, second, gain, weight, cosine, sine_table, head_gains, groups, before, count
):
    rows, width = first.shape
    positions = count * rows
    columns = weight.shape[1]
    kv_count = columns // ((groups + 2) * HEAD_SIZE)
    held = kv_count * (groups + 1) * HEAD_SIZE
    block = min(256, rows)
    parts = rows // block
    same = lambda i, s: (0, 0)
    here = lambda i, s: (i, 0)
    there = lambda i, s: (s[0] * parts + i, 0)
    in_specs = [
        pl.BlockSpec((block, width), here),
        pl.BlockSpec((block, width), here),
        pl.BlockSpec((1, width), same),
        pl.BlockSpec((width, columns), same),
        pl.BlockSpec((block, HEAD_SIZE), there),
        pl.BlockSpec((block, HEAD_SIZE), there),
        pl.BlockSpec((2, HEAD_SIZE), same),
    ]
    args = [first, second, gain, weight, cosine, sine_table, head_gains]
    aliases = {}
    if before is not None:
        in_specs += [pl.BlockSpec(memory_space=pl.ANY)] * 3
        aliases = {len(args) + 1 + k: k for k in range(3)}
        args += list(before)
    return pl.pallas_call(
        functools.partial(project_kernel, groups, kv_count),
        grid_spec=pltpu.PrefetchScalarGridSpec(
            num_scalar_prefetch=1,
            grid=(parts,),
            in_specs=in_specs,
            out_specs=[
                pl.BlockSpec((block, width), there),
                pl.BlockSpec((block, columns), there),
                pl.BlockSpec((block, held), there),
            ],
        ),
        out_shape=(
            jax.ShapeDtypeStruct((positions, width), jnp.bfloat16),
            jax.ShapeDtypeStruct((positions, columns), jnp.bfloat16),
            jax.ShapeDtypeStruct((positions, held), jnp.float32),
        ),
        input_output_aliases=aliases,
        compiler_params=arbitrary(1, 40),
        cost_estimate=cost(2 * rows * width * columns, 2 * width * columns + 12 * rows * width),
        name="project",
    )(place, *args)


def forward_kernel(block, groups, place_ref, heads_ref, out_ref, total_ref, wide_ref):
    at_query = pl.program_id(1)
    length = place_ref[0]
    size = HEAD_SIZE
    key_lanes = slice(groups * size, (groups + 1) * size)

    @pl.when(at_query == 0)
    def _():
        wide_ref[:, :size] = heads_ref[:, (groups + 1) * size :]
        wide_ref[:, size:] = jnp.ones((wide_ref.shape[0], size), wide_ref.dtype)

    whole = jnp.minimum(at_query, length // block)
    some = jnp.minimum(at_query + 1, (length + block - 1) // block)
    here = pl.ds(pl.multiple_of(at_query * block, block), block)
    queries = [heads_ref[here, g * size : (g + 1) * size] for g in range(groups)]

    def step(at_key, sums, masked):
        start = pl.multiple_of(at_key * block, block)
        keys = heads_ref[pl.ds(start, block), key_lanes]
        wide = wide_ref[pl.ds(start, block), :]
        if masked:
            rows = at_query * block + lax.broadcasted_iota(jnp.int32, (block, block), 0)
            cols = start + lax.broadcasted_iota(jnp.int32, (block, block), 1)
            allowed = (cols <= rows) & (cols < length)
        after = []
        for g in range(groups):
            scores = nt(queries[g], keys)
            if masked:
                scores = jnp.where(allowed, scores, MASKED)
            after.append(sums[g] + nn(jnp.exp2(scores).astype(jnp.bfloat16), wide))
        return tuple(after)

    sums = tuple(jnp.zeros((block, 2 * size), jnp.float32) for _ in range(groups))
    sums = lax.fori_loop(0, whole, lambda j, c: step(j, c, False), sums)
    sums = lax.fori_loop(whole, some, lambda j, c: step(j, c, True), sums)
    for g in range(groups):
        total = sums[g][:, size:]
        out_ref[:, g * size : (g + 1) * size] = (sums[g][:, :size] / total).astype(out_ref.dtype)
        total_ref[g, :, :] = jnp.transpose(jnp.log2(total))[:8, :]


def attend_forward(place, heads, groups, count):
    positions = heads.shape[0]
    rows = positions // count
    block = min(512, rows)
    parts = rows // block
    group_width = (groups + 2) * HEAD_SIZE
    kv_count = heads.shape[1] // group_width
    size = HEAD_SIZE
    width = kv_count * groups * size
    return pl.pallas_call(
        functools.partial(forward_kernel, block, groups),
        grid_spec=pltpu.PrefetchScalarGridSpec(
            num_scalar_prefetch=1,
            grid=(kv_count, positions // block),
            in_specs=[pl.BlockSpec((positions, group_width), lambda h, i, s: (0, h))],
            out_specs=[
                pl.BlockSpec(
                    (None, block, groups * size),
                    lambda h, i, s: (
                        lax.rem(i // parts + count - s[1], count),
                        lax.rem(i, parts),
                        h,
                    ),
                ),
                pl.BlockSpec((groups, 8, block), lambda h, i, s: (h, 0, i)),
            ],
            scratch_shapes=[pltpu.VMEM((positions, 2 * size), jnp.bfloat16)],
        ),
        out_shape=(
            jax.ShapeDtypeStruct((count, rows, width), jnp.bfloat16),
            jax.ShapeDtypeStruct((kv_count * groups, 8, positions), jnp.float32),
        ),
        compiler_params=arbitrary(2, 48),
        cost_estimate=cost(
            4 * positions * positions * width,
            8 * positions * width,
            positions * positions * width // size // 2,
        ),
        name="attend_forward",
    )(place, heads)


def backward_kernel(
    block,
    groups,
    positions,
    count,
    place_ref,
    heads_ref,
    raw_ref,
    cosine_ref,
    sine_ref,
    head_gain_ref,
    out_ref,
    total_ref,
    *refs,
):
    piece_refs = refs[:count]
    grad_raw_ref, gain_ref, query_sums_ref, key_sums_ref, center_ref, grad_ref = refs[count:]
    length = place_ref[0]
    size = HEAD_SIZE
    rows_each = positions // count
    blocks = positions // block
    key_lanes = slice(groups * size, (groups + 1) * size)
    value_lanes = slice((groups + 1) * size, (groups + 2) * size)
    for k in range(count):
        place = lax.rem(place_ref[1] + k, count) * rows_each
        piece_ref = piece_refs[(count - k) % count]
        grad_ref[pl.ds(pl.multiple_of(place, rows_each), rows_each), :] = piece_ref[...]
        for g in range(groups):
            lanes = slice(g * size, (g + 1) * size)
            terms = piece_ref[:, lanes].astype(jnp.float32) * out_ref[k, :, lanes].astype(
                jnp.float32
            )
            center_ref[g, :, pl.ds(pl.multiple_of(place, rows_each), rows_each)] = (
                jnp.broadcast_to(
                    jnp.sum(jnp.transpose(terms), axis=0, keepdims=True), (8, rows_each)
                )
            )
    query_sums_ref[...] = jnp.zeros_like(query_sums_ref)
    whole = length // block
    some = (length + block - 1) // block

    def key_block(j, _):
        start = pl.multiple_of(j * block, block)
        keys = heads_ref[pl.ds(start, block), key_lanes]
        values = heads_ref[pl.ds(start, block), value_lanes]

        def step(i, carry, masked):
            grad_keys, grad_values = carry
            at = pl.multiple_of(i * block, block)
            if masked:
                key_at = start + lax.broadcasted_iota(jnp.int32, (block, block), 0)
                query_at = at + lax.broadcasted_iota(jnp.int32, (block, block), 1)
                allowed = (key_at <= query_at) & (key_at < length)
            for g in range(groups):
                queries = heads_ref[pl.ds(at, block), g * size : (g + 1) * size]
                grads = grad_ref[pl.ds(at, block), g * size : (g + 1) * size]
                scores = nt(keys, queries) - total_ref[g, 0:1, pl.ds(at, block)]
                if masked:
                    scores = jnp.where(allowed, scores, MASKED)
                probs = jnp.exp2(scores)
                grad_attend = nt(values, grads)
                grad_scores = (
                    probs * (grad_attend - center_ref[g, 0:1, pl.ds(at, block)])
                ).astype(jnp.bfloat16)
                grad_values = grad_values + nn(probs.astype(jnp.bfloat16), grads)
                grad_keys = grad_keys + nn(grad_scores, queries)
                query_sums_ref[g, pl.ds(at, block), :] += tn(grad_scores, keys)
            return grad_keys, grad_values

        zero = jnp.zeros((block, size), jnp.float32)
        first = jnp.where(j < whole, jnp.minimum(j + 1, blocks), blocks)
        carry = lax.fori_loop(j, first, lambda i, c: step(i, c, True), (zero, zero))
        grad_keys, grad_values = lax.fori_loop(
            first, blocks, lambda i, c: step(i, c, False), carry
        )
        key_sums_ref[pl.ds(start, block), :] = grad_keys
        grad_raw_ref[pl.ds(start, block), value_lanes] = grad_values.astype(grad_raw_ref.dtype)
        return 0

    lax.fori_loop(0, some, key_block, 0)

    def padding(j, _):
        start = pl.multiple_of(j * block, block)
        key_sums_ref[pl.ds(start, block), :] = jnp.zeros((block, size), jnp.float32)
        grad_raw_ref[pl.ds(start, block), value_lanes] = jnp.zeros(
            (block, size), grad_raw_ref.dtype
        )
        return 0

    lax.fori_loop(some, blocks, padding, 0)

    def head_back(i, carry):
        rows = pl.ds(pl.multiple_of(i * block, block), block)
        cosine, sine_table = cosine_ref[rows, :], sine_ref[rows, :]
        sums = list(carry)
        for g in range(groups + 1):
            lanes = slice(g * size, (g + 1) * size)
            if g < groups:
                grad = query_sums_ref[g, rows, :] * size**-0.5
            else:
                grad = key_sums_ref[rows, :] * (1.0 / math.log2(math.e))
            which = 0 if g < groups else 1
            grad = grad.astype(jnp.bfloat16).astype(jnp.float32)
            grad = grad * cosine - pltpu.roll(grad, size // 2, 1) * sine_table
            value = raw_ref[rows, lanes]
            scale = lax.rsqrt(jnp.mean(value * value, axis=-1, keepdims=True) + EPS)
            unit = value * scale
            sums[which] = sums[which] + jnp.sum(grad * unit, axis=0, keepdims=True)
            grad = grad * head_gain_ref[which : which + 1, :]
            inner = jnp.mean(grad * unit, axis=-1, keepdims=True)
            grad_raw_ref[rows, lanes] = (scale * (grad - unit * inner)).astype(grad_raw_ref.dtype)
        return tuple(sums)

    zero = jnp.zeros((1, size), jnp.float32)
    sums = lax.fori_loop(0, blocks, head_back, (zero, zero))
    gain_ref[0, 0:1, :] = sums[0]
    gain_ref[0, 1:2, :] = sums[1]


def attend_backward(
    place, heads, raw, cosine, sine_table, head_gains, groups, context, totals, pieces
):
    count = len(pieces)
    positions = heads.shape[0]
    rows = positions // count
    block = min(512, positions)
    size = HEAD_SIZE
    kv_count = heads.shape[1] // ((groups + 2) * size)

    def of_group(lines, columns):
        return pl.BlockSpec((lines, columns * size), lambda h, s: (0, h))

    width = kv_count * groups * size
    return pl.pallas_call(
        functools.partial(backward_kernel, block, groups, positions, count),
        grid_spec=pltpu.PrefetchScalarGridSpec(
            num_scalar_prefetch=1,
            grid=(kv_count,),
            in_specs=[
                of_group(positions, groups + 2),
                of_group(positions, groups + 1),
                fixed(cosine.shape),
                fixed(sine_table.shape),
                fixed(head_gains.shape),
                pl.BlockSpec((count, rows, groups * size), lambda h, s: (0, 0, h)),
                pl.BlockSpec((groups, 8, positions), lambda h, s: (h, 0, 0)),
            ]
            + [of_group(rows, groups)] * count,
            out_specs=[
                of_group(positions, groups + 2),
                pl.BlockSpec((1, 2, size), lambda h, s: (h, 0, 0)),
            ],
            scratch_shapes=[
                pltpu.VMEM((groups, positions, size), jnp.float32),
                pltpu.VMEM((positions, size), jnp.float32),
                pltpu.VMEM((groups, 8, positions), jnp.float32),
                pltpu.VMEM((positions, groups * size), jnp.bfloat16),
            ],
        ),
        out_shape=(
            jax.ShapeDtypeStruct(heads.shape, jnp.bfloat16),
            jax.ShapeDtypeStruct((kv_count, 2, size), jnp.float32),
        ),
        compiler_params=arbitrary(1, 56),
        cost_estimate=cost(
            positions * positions * width,
            2 * positions * width,
            positions * positions * width // size // 20,
        ),
        name="attend_backward",
    )(
        place,
        heads,
        raw,
        cosine,
        sine_table,
        head_gains,
        context,
        totals,
        *pieces,
    )


def tile_of(hidden_units):
    return next(t for t in (512, 384, 256, 128) if hidden_units % t == 0)


def separate(both, tile):
    pieces = [both[:, at : at + tile] for at in range(0, both.shape[1], tile)]
    return jnp.concatenate(pieces[0::2], axis=1), jnp.concatenate(pieces[1::2], axis=1)


def out_norm_kernel(count, weight_ref, rows_ref, gain_ref, *refs):
    resid_ref, normed_ref = refs[count:]
    part = refs[0].shape[-1]
    resid = rows_ref[...].astype(jnp.float32)
    for k in range(count):
        at = (count - k) % count * part
        resid = resid + nn(refs[k][...], weight_ref[at : at + part, :])
    resid_ref[...] = resid
    normed_ref[...] = norm_rows(resid, gain_ref[...]).astype(normed_ref.dtype)


def out_norm(pieces, weight, tokens, gain):
    count = len(pieces)
    rows, part = pieces[0].shape
    width = weight.shape[1]
    block = min(256, rows)
    across = pl.BlockSpec((block, width), lambda i: (i, 0))
    return pl.pallas_call(
        functools.partial(out_norm_kernel, count),
        grid=(rows // block,),
        in_specs=[fixed(weight.shape), across, fixed(gain.shape)]
        + [pl.BlockSpec((block, part), lambda i: (i, 0))] * count,
        out_specs=[across, across],
        out_shape=(
            jax.ShapeDtypeStruct((rows, width), jnp.float32),
            jax.ShapeDtypeStruct((rows, width), jnp.bfloat16),
        ),
        compiler_params=arbitrary(1, 48),
        cost_estimate=cost(2 * rows * count * part * width, 2 * weight.size + 10 * rows * width),
        name="out_norm",
    )(weight, tokens, gain, *pieces)


def hidden_kernel(tile, own_ref, away_ref, weight_ref, *refs):
    both_ref, hidden_ref = refs[-2:]
    rows = own_ref.shape[0]
    for half, rows_ref in enumerate((own_ref, away_ref)):
        here = slice(half * rows, (half + 1) * rows)
        both = nn(rows_ref[...], weight_ref[...])
        both_ref[here, :] = both
        gate, up = both[:, :tile], both[:, tile:]
        hidden_ref[here, :] = (gate * jax.nn.sigmoid(gate) * up).astype(hidden_ref.dtype)


def hidden_units(own, away, weight, tile, at, total, before):
    rows, width = own.shape
    columns = weight.shape[1]
    tiles = columns // (2 * tile)
    in_specs = [
        fixed(own.shape),
        fixed(away.shape),
        pl.BlockSpec((width, 2 * tile), lambda j: (0, j)),
    ]
    args, aliases = [own, away, weight], {}
    if before is not None:
        in_specs.append(pl.BlockSpec(memory_space=pl.ANY))
        args.append(before)
        aliases = {3: 1}
    return pl.pallas_call(
        functools.partial(hidden_kernel, tile),
        grid=(tiles,),
        in_specs=in_specs,
        out_specs=[
            pl.BlockSpec((2 * rows, 2 * tile), lambda j: (0, j)),
            pl.BlockSpec((2 * rows, tile), lambda j: (0, at * tiles + j)),
        ],
        out_shape=(
            jax.ShapeDtypeStruct((2 * rows, columns), jnp.float32),
            jax.ShapeDtypeStruct((2 * rows, total), jnp.bfloat16),
        ),
        input_output_aliases=aliases,
        compiler_params=arbitrary(1, 56),
        cost_estimate=cost(4 * rows * width * columns, 2 * width * columns + 10 * rows * columns),
        name="hidden_units",
    )(*args)


def hidden_back_kernel(tile, own_ref, away_ref, down_ref, both_ref, out_ref):
    rows = own_ref.shape[0]
    for half, grads_ref in enumerate((own_ref, away_ref)):
        here = slice(half * rows, (half + 1) * rows)
        grad_hidden = nt(grads_ref[...], down_ref[...])
        gate, up = both_ref[here, :tile], both_ref[here, tile:]
        sigmoid = jax.nn.sigmoid(gate)
        silu = gate * sigmoid
        out_ref[here, :tile] = (grad_hidden * up * (sigmoid + silu * (1.0 - sigmoid))).astype(
            out_ref.dtype
        )
        out_ref[here, tile:] = (grad_hidden * silu).astype(out_ref.dtype)


def hidden_back(own, away, down, both, tile):
    rows, width = own.shape
    columns = both.shape[1]
    pair = pl.BlockSpec((2 * rows, 2 * tile), lambda j: (0, j))
    return pl.pallas_call(
        functools.partial(hidden_back_kernel, tile),
        grid=(columns // (2 * tile),),
        in_specs=[
            fixed(own.shape),
            fixed(away.shape),
            pl.BlockSpec((tile, width), lambda j: (j, 0)),
            pair,
        ],
        out_specs=pair,
        out_shape=jax.ShapeDtypeStruct((2 * rows, columns), jnp.bfloat16),
        compiler_params=arbitrary(1, 56),
        cost_estimate=cost(2 * rows * width * columns, width * columns + 12 * rows * columns),
        name="hidden_back",
    )(own, away, down, both)


def unit_grads_kernel(own_ref, away_ref, grads_ref, out_ref):
    rows = own_ref.shape[0]
    out_ref[...] = (
        tn(own_ref[...], grads_ref[:rows, :]) + tn(away_ref[...], grads_ref[rows:, :])
    ).astype(out_ref.dtype)


def unit_grads(own, away, grads):
    rows, width = own.shape
    columns = grads.shape[1]
    tile = tile_of(columns)
    return pl.pallas_call(
        unit_grads_kernel,
        grid=(columns // tile,),
        in_specs=[
            fixed(own.shape),
            fixed(away.shape),
            pl.BlockSpec((2 * rows, tile), lambda j: (0, j)),
        ],
        out_specs=pl.BlockSpec((width, tile), lambda j: (0, j)),
        out_shape=jax.ShapeDtypeStruct((width, columns), jnp.bfloat16),
        compiler_params=arbitrary(1, 56),
        cost_estimate=cost(4 * rows * width * columns, 2 * width * columns + 4 * rows * columns),
        name="unit_grads",
    )(own, away, grads)


def down_grads_kernel(hidden_ref, own_ref, away_ref, out_ref):
    rows = own_ref.shape[0]
    out_ref[...] = (
        tn(hidden_ref[:rows, :], own_ref[...]) + tn(hidden_ref[rows:, :], away_ref[...])
    ).astype(out_ref.dtype)


def down_grads(hidden, own, away):
    rows, width = own.shape
    units = hidden.shape[1]
    tile = tile_of(units)
    return pl.pallas_call(
        down_grads_kernel,
        grid=(units // tile,),
        in_specs=[
            pl.BlockSpec((2 * rows, tile), lambda j: (0, j)),
            fixed(own.shape),
            fixed(away.shape),
        ],
        out_specs=pl.BlockSpec((tile, width), lambda j: (j, 0)),
        out_shape=jax.ShapeDtypeStruct((units, width), jnp.bfloat16),
        compiler_params=arbitrary(1, 56),
        cost_estimate=cost(4 * rows * width * units, 2 * width * units + 4 * rows * units),
        name="down_grads",
    )(hidden, own, away)


def grad_normed_kernel(parts, *refs):
    grads, weights = refs[:parts], refs[parts : 2 * parts]
    own_ref, away_ref = refs[2 * parts :]
    rows = own_ref.shape[0]
    for half, out_ref in enumerate((own_ref, away_ref)):
        here = slice(half * rows, (half + 1) * rows)
        total = nt(grads[0][here, :], weights[0][...])
        for grad_ref, weight_ref in zip(grads[1:], weights[1:]):
            total = total + nt(grad_ref[here, :], weight_ref[...])
        out_ref[...] = total.astype(out_ref.dtype)


def grad_normed(grads, weights):
    rows = grads[0].shape[0] // 2
    width = weights[0].shape[0]
    tile = tile_of(width)
    return pl.pallas_call(
        functools.partial(grad_normed_kernel, len(grads)),
        grid=(width // tile,),
        in_specs=[fixed(grad.shape) for grad in grads]
        + [pl.BlockSpec((tile, weight.shape[1]), lambda j: (j, 0)) for weight in weights],
        out_specs=[pl.BlockSpec((rows, tile), lambda j: (0, j))] * 2,
        out_shape=(
            jax.ShapeDtypeStruct((rows, width), jnp.float32),
            jax.ShapeDtypeStruct((rows, width), jnp.bfloat16),
        ),
        compiler_params=arbitrary(1, 60),
        cost_estimate=cost(
            sum(2 * grad.size * width for grad in grads),
            sum(2 * grad.size + 2 * weight.size for grad, weight in zip(grads, weights)),
        ),
        name="grad_normed",
    )(*grads, *weights)


def mlp_out_kernel(hidden_ref, *refs):
    own_ref, away_ref = refs[-2:]
    rows = own_ref.shape[0]
    for half, out_ref in enumerate((own_ref, away_ref)):
        here = slice(half * rows, (half + 1) * rows)
        at, total = 0, None
        for down_ref in refs[:-2]:
            units = down_ref.shape[0]
            part = nn(hidden_ref[here, at : at + units], down_ref[...])
            total = part if total is None else total + part
            at += units
        out_ref[...] = total.astype(out_ref.dtype)


def mlp_out(hidden, downs):
    rows = hidden.shape[0] // 2
    width = downs[0].shape[1]
    tile = tile_of(width)
    return pl.pallas_call(
        mlp_out_kernel,
        grid=(width // tile,),
        in_specs=[fixed(hidden.shape)]
        + [pl.BlockSpec((down.shape[0], tile), lambda j: (0, j)) for down in downs],
        out_specs=[pl.BlockSpec((rows, tile), lambda j: (0, j))] * 2,
        out_shape=(
            jax.ShapeDtypeStruct((rows, width), jnp.float32),
            jax.ShapeDtypeStruct((rows, width), jnp.bfloat16),
        ),
        compiler_params=arbitrary(1, 56),
        cost_estimate=cost(2 * hidden.size * width, 4 * hidden.size + 6 * rows * width),
        name="mlp_out",
    )(hidden, *downs)


def resid_back_kernel(
    place_ref,
    own_ref,
    away_ref,
    resid_ref,
    cotangent_ref,
    gain_ref,
    weight_ref,
    grad_ref,
    low_ref,
    sums_ref,
    *piece_refs,
):
    block = own_ref.shape[0]
    part = piece_refs[0].shape[-1]
    first = place_ref[1] + pl.program_id(0) * block
    at = first + lax.broadcasted_iota(jnp.int32, (block, 1), 0)
    valid = (at < place_ref[0]).astype(jnp.float32)
    grads = own_ref[...] + away_ref[...].astype(jnp.float32)
    back, sums = norm_back(resid_ref[...], gain_ref[...], grads)
    grad_resid = valid * cotangent_ref[...].astype(jnp.float32) + back
    grad_ref[...] = grad_resid
    low = grad_resid.astype(jnp.bfloat16)
    low_ref[...] = low
    for k, piece_ref in enumerate(piece_refs):
        piece_ref[...] = nt(low, weight_ref[k * part : (k + 1) * part, :]).astype(piece_ref.dtype)

    @pl.when(pl.program_id(0) == 0)
    def _():
        sums_ref[...] = jnp.zeros_like(sums_ref)

    sums_ref[...] += sums


def resid_back(own, away, resid, cotangent, gain, weight, length, start, count):
    rows, width = own.shape
    part = weight.shape[0] // count
    block = min(256, rows)
    across = pl.BlockSpec((block, width), lambda i, s: (i, 0))
    return pl.pallas_call(
        resid_back_kernel,
        grid_spec=pltpu.PrefetchScalarGridSpec(
            num_scalar_prefetch=1,
            grid=(rows // block,),
            in_specs=[across] * 4 + [fixed(gain.shape), fixed(weight.shape)],
            out_specs=[across, across, fixed(gain.shape)]
            + [pl.BlockSpec((block, part), lambda i, s: (i, 0))] * count,
        ),
        out_shape=(
            jax.ShapeDtypeStruct((rows, width), jnp.float32),
            jax.ShapeDtypeStruct((rows, width), jnp.bfloat16),
            jax.ShapeDtypeStruct(gain.shape, jnp.float32),
        )
        + (jax.ShapeDtypeStruct((rows, part), jnp.bfloat16),) * count,
        compiler_params=arbitrary(1, 56),
        cost_estimate=cost(2 * rows * weight.size, 2 * weight.size + 20 * rows * width),
        name="resid_back",
    )(jnp.stack([length, start]), own, away, resid, cotangent, gain, weight)


def out_grads_kernel(count, grads_ref, *refs):
    out_ref = refs[count]
    part = refs[0].shape[-1]
    for k in range(count):
        at = (count - k) % count * part
        out_ref[at : at + part, :] = tn(refs[k][...], grads_ref[...]).astype(out_ref.dtype)


def out_grads(pieces, grads):
    count = len(pieces)
    rows, part = pieces[0].shape
    width = grads.shape[1]
    tile = tile_of(width)
    return pl.pallas_call(
        functools.partial(out_grads_kernel, count),
        grid=(width // tile,),
        in_specs=[pl.BlockSpec((rows, tile), lambda j: (0, j))]
        + [fixed(piece.shape) for piece in pieces],
        out_specs=pl.BlockSpec((count * part, tile), lambda j: (0, j)),
        out_shape=jax.ShapeDtypeStruct((count * part, width), jnp.bfloat16),
        compiler_params=arbitrary(1, 48),
        cost_estimate=cost(
            2 * rows * count * part * width, 2 * count * part * (rows + width) + 2 * rows * width
        ),
        name="out_grads",
    )(grads, *pieces)


def pack_heads_kernel(groups, query_ref, key_ref, value_ref, gain_ref, out_ref):
    size = HEAD_SIZE
    at = 0
    for h in range(key_ref.shape[1] // size):
        for ref, start, columns in (
            (query_ref, h * groups * size, groups * size),
            (key_ref, h * size, size),
            (value_ref, h * size, size),
        ):
            out_ref[:, at : at + columns] = ref[:, start : start + columns]
            at += columns
    out_ref[:, at:] = gain_ref[...]


def pack_heads(query, key, value, gain, groups):
    rows = query.shape[0]
    columns = query.shape[1] + key.shape[1] + value.shape[1] + gain.shape[1]
    args = (query, key, value, gain)
    return pl.pallas_call(
        functools.partial(pack_heads_kernel, groups),
        grid=(1,),
        in_specs=[fixed(arg.shape) for arg in args],
        out_specs=fixed((rows, columns)),
        out_shape=jax.ShapeDtypeStruct((rows, columns), jnp.bfloat16),
        compiler_params=arbitrary(1, 16),
        cost_estimate=cost(0, 4 * rows * columns),
        name="pack_heads",
    )(*args)


def pack_units_kernel(tile, gate_ref, up_ref, out_ref):
    for at in range(0, gate_ref.shape[1], tile):
        out_ref[:, 2 * at : 2 * at + tile] = gate_ref[:, at : at + tile]
        out_ref[:, 2 * at + tile : 2 * at + 2 * tile] = up_ref[:, at : at + tile]


def pack_units(gate, up, tile):
    rows, columns = gate.shape
    return pl.pallas_call(
        functools.partial(pack_units_kernel, tile),
        grid=(1,),
        in_specs=[fixed(gate.shape), fixed(up.shape)],
        out_specs=fixed((rows, 2 * columns)),
        out_shape=jax.ShapeDtypeStruct((rows, 2 * columns), jnp.bfloat16),
        compiler_params=arbitrary(1, 16),
        cost_estimate=cost(0, 8 * rows * columns),
        name="pack_units",
    )(gate, up)


def heads_back_kernel(normed_ref, grad_ref, weight_ref, out_ref, sums_ref):
    partial = tn(normed_ref[...], grad_ref[...])
    out_ref[...] = partial.astype(out_ref.dtype)
    sums = jnp.sum(partial * weight_ref[...].astype(jnp.float32), axis=1, keepdims=True)
    sums_ref[...] = jnp.broadcast_to(sums, sums_ref.shape)


def heads_back(normed, grads, weight):
    positions, width = normed.shape
    columns = grads.shape[1]
    block = min(512, width)
    return pl.pallas_call(
        heads_back_kernel,
        grid=(width // block,),
        in_specs=[
            pl.BlockSpec((positions, block), lambda j: (0, j)),
            pl.BlockSpec((positions, columns), lambda j: (0, 0)),
            pl.BlockSpec((block, columns), lambda j: (j, 0)),
        ],
        out_specs=[
            pl.BlockSpec((block, columns), lambda j: (j, 0)),
            pl.BlockSpec((block, LANES), lambda j: (j, 0)),
        ],
        out_shape=(
            jax.ShapeDtypeStruct((width, columns), jnp.bfloat16),
            jax.ShapeDtypeStruct((width, LANES), jnp.float32),
        ),
        compiler_params=arbitrary(1, 48),
        cost_estimate=cost(
            2 * positions * width * columns, 2 * positions * (width + columns) + 4 * width * columns
        ),
        name="heads_back",
    )(normed, grads, weight)


def norm_back(value_rows, gain, grads):
    scale = lax.rsqrt(jnp.mean(value_rows * value_rows, axis=-1, keepdims=True) + EPS)
    unit = value_rows * scale
    scaled = grads * gain
    inner = jnp.mean(scaled * unit, axis=-1, keepdims=True)
    return scale * (scaled - unit * inner), jnp.sum(grads * unit, axis=0)


def after(value, *others):
    return lax.optimization_barrier((value, others))[0]


def hop_right(value, count, hop):
    return lax.ppermute(value, "seq", [(i, i + 1) for i in range(hop - 1, count - 1)])


def hop_left(value, count, hop):
    return lax.ppermute(value, "seq", [(i, i - 1) for i in range(1, count - hop + 1)])


def line_scatter(parts, first_before=()):
    count = len(parts)
    right, left = None, None
    for hop in range(count - 1):
        to_right, to_left = parts[count - 1 - hop], parts[hop + 1]
        if hop:
            to_right, to_left = to_right + right, to_left + left
        if hop == 1:
            to_right, to_left = after((to_right, to_left), *first_before)
        right = lax.ppermute(
            to_right.astype(jnp.bfloat16), "seq", [(i, i + 1) for i in range(hop + 1)]
        ).astype(jnp.float32)
        left = lax.ppermute(
            to_left.astype(jnp.bfloat16),
            "seq",
            [(i, i - 1) for i in range(count - 1 - hop, count)],
        ).astype(jnp.float32)
    return parts[0] + right + left


def sum_over(value, axis):
    flat = value.reshape(-1, LANES)
    size = lax.axis_size(axis)
    assert size & (size - 1) == 0
    step = 1
    while step < size:
        flat = flat + lax.ppermute(flat, axis, [(i, i ^ step) for i in range(size)])
        step *= 2
    return flat.reshape(-1)


def swap(value, count):
    return lax.ppermute(value, "seq", [(i, i ^ 1) for i in range(count)])


def fetch(value, count, step):
    return lax.ppermute(value, "seq", [((i + step) % count, i) for i in range(count)])


def give(value, count, step):
    return lax.ppermute(value, "seq", [(i, (i + step) % count) for i in range(count)])


def on_device(
    tokens,
    lengths,
    cotangent,
    w_query,
    key_weight,
    value_weight,
    w_out,
    w_gate,
    w_up,
    w_down,
    norm_attn,
    norm_mlp,
    norm_query,
    norm_key,
):
    slots, rows, width = tokens.shape
    assert slots == 1
    count = lax.axis_size("seq")
    positions = count * rows
    me = lax.axis_index("seq")
    tokens_low = tokens.reshape(rows, width)
    cotangent_low = cotangent.reshape(rows, width)
    length = lengths[0]
    low = jnp.bfloat16
    groups = w_query.shape[1] // key_weight.shape[1]
    kv_count = key_weight.shape[1] // HEAD_SIZE
    units = w_gate.shape[1]
    tile = tile_of(units)
    steps = range(0, count, PAIR)

    def from_groups(both):
        size = HEAD_SIZE
        starts = [h * (groups + 2) * size for h in range(kv_count)]
        ends = (0, groups * size, (groups + 1) * size, (groups + 2) * size)
        return [
            jnp.concatenate([both[:, s + low_end : s + high_end] for s in starts], axis=1)
            for low_end, high_end in zip(ends, ends[1:])
        ]

    weight_rows = w_query.shape[0]
    gain_parts = (norm_attn, norm_mlp, norm_query, norm_key)
    gain_sizes = [part.shape[0] for part in gain_parts]
    own_gains = jnp.concatenate(gain_parts)
    gain_block = jnp.pad(own_gains, (0, weight_rows * LANES - own_gains.shape[0])).reshape(
        weight_rows, LANES
    )
    own_heads = pack_heads(w_query, key_weight, value_weight, gain_block, groups)
    head_columns = own_heads.shape[1] - LANES
    gathered_heads = lax.all_gather(own_heads, "dp", axis=0, tiled=True)
    heads_weight = gathered_heads[:, :head_columns]
    gathered_gains = gathered_heads[:, head_columns:].reshape(-1, weight_rows * LANES)
    rights = [hop_right(tokens_low, count, 1)]
    lefts = [hop_left(tokens_low, count, 1)]
    gains, at = [], 0
    for part_size in gain_sizes:
        gains.append(gathered_gains[:, at : at + part_size].reshape(1, -1).astype(jnp.float32))
        at += part_size
    gain_attn, gain_mlp = gains[:2]
    head_gains = jnp.concatenate(gains[2:], axis=0)
    cosine, sine_table = angles(jnp.arange(positions, dtype=jnp.float32))

    places = [
        jnp.stack([lax.rem(me + k, count), (me + k < count).astype(jnp.int32)])
        for k in range(count)
    ]
    slot_place = jnp.stack([length, me])

    def project_block(k, whole):
        first, second = tokens_low, tokens_low
        if k:
            first, second = lefts[k - 1], rights[count - k - 1]
        return project(
            places[k],
            first,
            second,
            gain_attn,
            heads_weight,
            cosine,
            sine_table,
            head_gains,
            groups,
            whole,
            count,
        )

    own_both = pack_units(w_gate, w_up, tile)
    first_hop = (rights[0], lefts[0])
    both_weights = [lax.all_gather(after(own_both, *first_hop), "dp", axis=0, tiled=True)]
    down_weights = [lax.all_gather(after(w_down, *first_hop), "dp", axis=1, tiled=True)]
    whole = project_block(0, None)
    for hop in range(2, count - 1):
        rights.append(hop_right(rights[-1], count, hop))
        lefts.append(hop_left(lefts[-1], count, hop))
    right, left = after((rights[-1], lefts[-1]), whole[1])
    out_blocks = [w_out] + [
        fetch(after(w_out, rights[-1], lefts[-1]), count, k) for k in range(1, count)
    ]
    rights.append(hop_right(right, count, count - 1))
    lefts.append(hop_left(left, count, count - 1))
    for k in range(2, count - 1):
        whole = project_block(k, whole)
    gathered = (rights[-1], lefts[-1])
    out_weight = lax.all_gather(
        after(
            jnp.concatenate(out_blocks, axis=0), both_weights[0], down_weights[0], *gathered
        ),
        "dp",
        axis=1,
        tiled=True,
    )

    fetched_both = [
        fetch(after(own_both, whole[1], *gathered), count, step) for step in steps[1:]
    ]
    for k in [1, count - 1] if count > 2 else [1]:
        whole = project_block(k, whole)
    normed_attn, heads, raw = whole
    context, totals = attend_forward(slot_place, heads, groups, count)
    sent = after(context, *fetched_both)
    context_pieces = [context[0]] + [give(sent[k], count, k) for k in range(1, count)]
    fetched_down = [fetch(after(w_down, *context_pieces[1:]), count, step) for step in steps[1:]]
    resid, normed_mlp = out_norm(context_pieces, out_weight, tokens_low, gain_mlp)
    away_normed = swap(normed_mlp, count)
    for both, down in zip(fetched_both, fetched_down):
        both_weights.append(lax.all_gather(after(both, context), "dp", axis=0, tiled=True))
        down_weights.append(lax.all_gather(after(down, away_normed), "dp", axis=1, tiled=True))

    place = jnp.arange(rows, dtype=jnp.int32)[:, None] + me * rows
    valid_rows = (place < length).astype(low)
    grad_rows = cotangent_low * valid_rows
    away_grads = swap(after(grad_rows, away_normed), count)
    hidden, boths = None, []
    for at, weight in enumerate(both_weights):
        both, hidden = hidden_units(
            normed_mlp, away_normed, weight, tile, at, len(steps) * units, hidden
        )
        boths.append(both)

    def spread(partial, axis):
        return lax.psum_scatter(partial, "dp", scatter_dimension=axis, tiled=True)

    mlp_own, mlp_away = mlp_out(hidden, down_weights)
    mlp_away = swap(after(mlp_away, away_grads), count)
    hidden = after(hidden, mlp_own)
    down_partial = down_grads(hidden, grad_rows, away_grads)
    grad_rows, away_grads = after((grad_rows, away_grads), down_partial)
    down_sums = spread(down_partial, 1)
    grad_boths = [
        hidden_back(grad_rows, away_grads, down, both, tile)
        for down, both in zip(down_weights, boths)
    ]
    mate_partials = [unit_grads(normed_mlp, away_normed, grad) for grad in grad_boths[1:]]
    mate_sums = [spread(partial, 0) for partial in mate_partials]
    grad_normed_own, grad_normed_away = grad_normed(
        after(grad_boths, *mate_partials), both_weights
    )
    own_partial = unit_grads(normed_mlp, away_normed, grad_boths[0])
    own_sum = spread(own_partial, 0)
    grad_resid, grad_attn_low, gain_mlp_sums, *pieces = resid_back(
        grad_normed_own,
        after(swap(after(grad_normed_away, mlp_away), count), own_partial),
        resid,
        cotangent_low,
        gain_mlp,
        out_weight,
        length,
        me * rows,
        count,
    )
    pieces = [pieces[0]] + [give(pieces[k], count, k) for k in range(1, count)]
    out_partial = out_grads(context_pieces, grad_attn_low)
    out_sums = spread(out_partial, 1)
    pieces = after(pieces, out_partial, down_sums, *mate_sums)
    grad_raw, head_gain_terms = attend_backward(
        slot_place,
        heads,
        raw,
        cosine,
        sine_table,
        head_gains,
        groups,
        context,
        totals,
        pieces,
    )
    given_both = [give(piece, count, step) for step, piece in zip(steps[1:], mate_sums)]
    down_pieces = jnp.split(down_sums, len(steps), axis=0)
    given_down = [give(piece, count, step) for step, piece in zip(steps[1:], down_pieces[1:])]
    grad_raw = after(grad_raw, *given_down)
    shares = [
        nt(
            lax.dynamic_slice_in_dim(grad_raw, lax.rem(me + k, count) * rows, rows, 0),
            heads_weight,
        )
        for k in range(count)
    ]
    heads_partial, gain_attn_sums = heads_back(
        normed_attn, after(grad_raw, shares[1], shares[-1]), heads_weight
    )
    grad_heads = spread(heads_partial, 0)
    grad_normed_attn = line_scatter(shares, (heads_partial, *given_both))
    grad_heads = grad_heads.astype(jnp.float32)
    grad_query, grad_key, grad_value = from_groups(grad_heads)
    layer_output = (
        (valid_rows.astype(jnp.float32) * (resid + mlp_own + mlp_away.astype(jnp.float32)))
        .astype(low)
        .reshape(slots, rows, width)
    )
    grad_input_norm = norm_back(tokens_low.astype(jnp.float32), gain_attn, grad_normed_attn)[0]
    grad_tokens = (grad_resid + grad_input_norm).astype(low).reshape(slots, rows, width)
    gain_attn_term = gain_attn_sums[:, 0] / gain_attn[0]

    out_parts = [
        give(part, count, k) if k else part for k, part in enumerate(jnp.split(out_sums, count))
    ]
    grad_out = sum(part.astype(jnp.float32) for part in out_parts)
    both_total = sum([part.astype(jnp.float32) for part in [own_sum, *given_both]])
    grad_gate, grad_up = separate(both_total, tile)
    grad_down = sum([part.astype(jnp.float32) for part in [down_pieces[0], *given_down]])

    head_gain_sums = jnp.sum(head_gain_terms, axis=0)
    terms = (gain_attn_term, gain_mlp_sums[0], head_gain_sums[0], head_gain_sums[1])
    sums = sum_over(jnp.concatenate(terms), "dp")
    sums = sum_over(after(sums, grad_normed_attn), "seq")
    gain_grads, at = [], 0
    for term, part_size in zip(terms, gain_sizes):
        gain_grads.append(
            lax.dynamic_slice_in_dim(
                sums[at : at + term.shape[0]], lax.axis_index("dp") * part_size, part_size, 0
            )
        )
        at += term.shape[0]
    return (
        layer_output,
        grad_tokens,
        grad_query,
        grad_key,
        grad_value,
        grad_out,
        grad_gate,
        grad_up,
        grad_down,
        *gain_grads,
    )


def solution(mesh):
    return jax.shard_map(
        on_device,
        mesh=mesh,
        in_specs=(
            P("dp", "seq", None),
            P("dp"),
            P("dp", "seq", None),
            P("dp", "seq"),
            P("dp", "seq"),
            P("dp", "seq"),
            P("seq", "dp"),
            P("dp", "seq"),
            P("dp", "seq"),
            P("seq", "dp"),
            P("dp"),
            P("dp"),
            P("dp"),
            P("dp"),
        ),
        out_specs=(
            P("dp", "seq", None),
            P("dp", "seq", None),
            P("dp", "seq"),
            P("dp", "seq"),
            P("dp", "seq"),
            P("seq", "dp"),
            P("dp", "seq"),
            P("dp", "seq"),
            P("seq", "dp"),
            P("dp"),
            P("dp"),
            P("dp"),
            P("dp"),
        ),
        check_vma=False,
    )
```

```python
import functools
import math

import jax
import jax.numpy as jnp
from jax import lax
from jax.experimental import pallas as pl
from jax.experimental.pallas import tpu as pltpu
from jax.sharding import PartitionSpec as P

HEAD_SIZE = 128
EPS = 1e-06
BASE = 1000000.0
MASKED = -1e30
QUERY_SCALE = HEAD_SIZE**-0.5 * math.log2(math.e)
PAIR = 2
LANES = 128
COST_SCALE = 0.05


def norm_rows(value_rows, gain):
    return (
        value_rows
        * lax.rsqrt(jnp.mean(value_rows * value_rows, axis=-1, keepdims=True) + EPS)
        * gain
    )


def angles(positions):
    frequency = BASE ** (-(jnp.arange(HEAD_SIZE // 2, dtype=jnp.float32) * 2.0 / HEAD_SIZE))
    phases = positions[:, None] * frequency[None, :]
    cosine, sine_table = jnp.cos(phases), jnp.sin(phases)
    return (
        jnp.concatenate([cosine, cosine], axis=-1),
        jnp.concatenate([-sine_table, sine_table], axis=-1),
    )


def nn(left, right):
    return lax.dot_general(
        left, right, (((1,), (0,)), ((), ())), preferred_element_type=jnp.float32
    )


def nt(left, right):
    return lax.dot_general(
        left, right, (((1,), (1,)), ((), ())), preferred_element_type=jnp.float32
    )


def tn(left, right):
    return lax.dot_general(
        left, right, (((0,), (0,)), ((), ())), preferred_element_type=jnp.float32
    )


def arbitrary(axes, megabytes):
    return pltpu.CompilerParams(
        dimension_semantics=("arbitrary",) * axes, vmem_limit_bytes=megabytes << 20
    )


def cost(flops, moved, exps=0):
    return pl.CostEstimate(
        flops=int(flops * COST_SCALE),
        bytes_accessed=int(moved * COST_SCALE),
        transcendentals=int(exps * COST_SCALE),
    )


def fixed(shape):
    return pl.BlockSpec(shape, lambda *_: (0,) * len(shape))


def project_kernel(
    groups,
    kv_count,
    place_ref,
    first_ref,
    second_ref,
    gain_ref,
    weight_ref,
    cosine_ref,
    sine_ref,
    head_gain_ref,
    *refs,
):
    normed_ref, heads_ref, raw_ref = refs[-3:]
    size = HEAD_SIZE
    rows = jnp.where(place_ref[1] != 0, first_ref[...], second_ref[...]).astype(jnp.float32)
    scale = lax.rsqrt(jnp.mean(rows * rows, axis=-1, keepdims=True) + EPS)
    normed = (rows * scale * gain_ref[...]).astype(jnp.bfloat16)
    normed_ref[...] = normed
    raw = nn(normed, weight_ref[...])
    cosine, sine_table = cosine_ref[...], sine_ref[...]
    for h in range(kv_count):
        start = h * (groups + 2) * size
        for g in range(groups + 1):
            column = start + g * size
            value = raw[:, column : column + size]
            held = (h * (groups + 1) + g) * size
            raw_ref[:, held : held + size] = value
            which = 0 if g < groups else 1
            value = value * lax.rsqrt(jnp.mean(value * value, axis=-1, keepdims=True) + EPS)
            value = value * head_gain_ref[which : which + 1, :]
            value = value * cosine + pltpu.roll(value, size // 2, 1) * sine_table
            if g < groups:
                value = value * QUERY_SCALE
            heads_ref[:, column : column + size] = value.astype(jnp.bfloat16)
        column = start + (groups + 1) * size
        heads_ref[:, column : column + size] = raw[:, column : column + size].astype(jnp.bfloat16)


def project(
    place, first, second, gain, weight, cosine, sine_table, head_gains, groups, before, count
):
    rows, width = first.shape
    positions = count * rows
    columns = weight.shape[1]
    kv_count = columns // ((groups + 2) * HEAD_SIZE)
    held = kv_count * (groups + 1) * HEAD_SIZE
    block = min(256, rows)
    parts = rows // block
    same = lambda i, s: (0, 0)
    here = lambda i, s: (i, 0)
    there = lambda i, s: (s[0] * parts + i, 0)
    in_specs = [
        pl.BlockSpec((block, width), here),
        pl.BlockSpec((block, width), here),
        pl.BlockSpec((1, width), same),
        pl.BlockSpec((width, columns), same),
        pl.BlockSpec((block, HEAD_SIZE), there),
        pl.BlockSpec((block, HEAD_SIZE), there),
        pl.BlockSpec((2, HEAD_SIZE), same),
    ]
    args = [first, second, gain, weight, cosine, sine_table, head_gains]
    aliases = {}
    if before is not None:
        in_specs += [pl.BlockSpec(memory_space=pl.ANY)] * 3
        aliases = {len(args) + 1 + k: k for k in range(3)}
        args += list(before)
    return pl.pallas_call(
        functools.partial(project_kernel, groups, kv_count),
        grid_spec=pltpu.PrefetchScalarGridSpec(
            num_scalar_prefetch=1,
            grid=(parts,),
            in_specs=in_specs,
            out_specs=[
                pl.BlockSpec((block, width), there),
                pl.BlockSpec((block, columns), there),
                pl.BlockSpec((block, held), there),
            ],
        ),
        out_shape=(
            jax.ShapeDtypeStruct((positions, width), jnp.bfloat16),
            jax.ShapeDtypeStruct((positions, columns), jnp.bfloat16),
            jax.ShapeDtypeStruct((positions, held), jnp.float32),
        ),
        input_output_aliases=aliases,
        compiler_params=arbitrary(1, 40),
        cost_estimate=cost(2 * rows * width * columns, 2 * width * columns + 12 * rows * width),
        name="project",
    )(place, *args)


def forward_kernel(block, groups, place_ref, heads_ref, out_ref, total_ref, wide_ref):
    at_query = pl.program_id(1)
    length = place_ref[0]
    size = HEAD_SIZE
    key_lanes = slice(groups * size, (groups + 1) * size)

    @pl.when(at_query == 0)
    def _():
        wide_ref[:, :size] = heads_ref[:, (groups + 1) * size :]
        wide_ref[:, size:] = jnp.ones((wide_ref.shape[0], size), wide_ref.dtype)

    whole = jnp.minimum(at_query, length // block)
    some = jnp.minimum(at_query + 1, (length + block - 1) // block)
    here = pl.ds(pl.multiple_of(at_query * block, block), block)
    queries = [heads_ref[here, g * size : (g + 1) * size] for g in range(groups)]

    def step(at_key, sums, masked):
        start = pl.multiple_of(at_key * block, block)
        keys = heads_ref[pl.ds(start, block), key_lanes]
        wide = wide_ref[pl.ds(start, block), :]
        if masked:
            rows = at_query * block + lax.broadcasted_iota(jnp.int32, (block, block), 0)
            cols = start + lax.broadcasted_iota(jnp.int32, (block, block), 1)
            allowed = (cols <= rows) & (cols < length)
        after = []
        for g in range(groups):
            scores = nt(queries[g], keys)
            if masked:
                scores = jnp.where(allowed, scores, MASKED)
            after.append(sums[g] + nn(jnp.exp2(scores).astype(jnp.bfloat16), wide))
        return tuple(after)

    sums = tuple(jnp.zeros((block, 2 * size), jnp.float32) for _ in range(groups))
    sums = lax.fori_loop(0, whole, lambda j, c: step(j, c, False), sums)
    sums = lax.fori_loop(whole, some, lambda j, c: step(j, c, True), sums)
    for g in range(groups):
        total = sums[g][:, size:]
        out_ref[:, g * size : (g + 1) * size] = (sums[g][:, :size] / total).astype(out_ref.dtype)
        total_ref[g, :, :] = jnp.transpose(jnp.log2(total))[:8, :]


def attend_forward(place, heads, groups, count):
    positions = heads.shape[0]
    rows = positions // count
    block = min(512, rows)
    parts = rows // block
    group_width = (groups + 2) * HEAD_SIZE
    kv_count = heads.shape[1] // group_width
    size = HEAD_SIZE
    width = kv_count * groups * size
    return pl.pallas_call(
        functools.partial(forward_kernel, block, groups),
        grid_spec=pltpu.PrefetchScalarGridSpec(
            num_scalar_prefetch=1,
            grid=(kv_count, positions // block),
            in_specs=[pl.BlockSpec((positions, group_width), lambda h, i, s: (0, h))],
            out_specs=[
                pl.BlockSpec(
                    (None, block, groups * size),
                    lambda h, i, s: (
                        lax.rem(i // parts + count - s[1], count),
                        lax.rem(i, parts),
                        h,
                    ),
                ),
                pl.BlockSpec((groups, 8, block), lambda h, i, s: (h, 0, i)),
            ],
            scratch_shapes=[pltpu.VMEM((positions, 2 * size), jnp.bfloat16)],
        ),
        out_shape=(
            jax.ShapeDtypeStruct((count, rows, width), jnp.bfloat16),
            jax.ShapeDtypeStruct((kv_count * groups, 8, positions), jnp.float32),
        ),
        compiler_params=arbitrary(2, 48),
        cost_estimate=cost(
            4 * positions * positions * width,
            8 * positions * width,
            positions * positions * width // size // 2,
        ),
        name="attend_forward",
    )(place, heads)


def backward_kernel(
    block,
    groups,
    positions,
    count,
    place_ref,
    heads_ref,
    raw_ref,
    cosine_ref,
    sine_ref,
    head_gain_ref,
    out_ref,
    total_ref,
    *refs,
):
    piece_refs = refs[:count]
    grad_raw_ref, gain_ref, query_sums_ref, key_sums_ref, center_ref, grad_ref = refs[count:]
    length = place_ref[0]
    size = HEAD_SIZE
    rows_each = positions // count
    blocks = positions // block
    key_lanes = slice(groups * size, (groups + 1) * size)
    value_lanes = slice((groups + 1) * size, (groups + 2) * size)
    for k in range(count):
        place = lax.rem(place_ref[1] + k, count) * rows_each
        piece_ref = piece_refs[(count - k) % count]
        grad_ref[pl.ds(pl.multiple_of(place, rows_each), rows_each), :] = piece_ref[...]
        for g in range(groups):
            lanes = slice(g * size, (g + 1) * size)
            terms = piece_ref[:, lanes].astype(jnp.float32) * out_ref[k, :, lanes].astype(
                jnp.float32
            )
            center_ref[g, :, pl.ds(pl.multiple_of(place, rows_each), rows_each)] = (
                jnp.broadcast_to(
                    jnp.sum(jnp.transpose(terms), axis=0, keepdims=True), (8, rows_each)
                )
            )
    query_sums_ref[...] = jnp.zeros_like(query_sums_ref)
    whole = length // block
    some = (length + block - 1) // block

    def key_block(j, _):
        start = pl.multiple_of(j * block, block)
        keys = heads_ref[pl.ds(start, block), key_lanes]
        values = heads_ref[pl.ds(start, block), value_lanes]

        def step(i, carry, masked):
            grad_keys, grad_values = carry
            at = pl.multiple_of(i * block, block)
            if masked:
                key_at = start + lax.broadcasted_iota(jnp.int32, (block, block), 0)
                query_at = at + lax.broadcasted_iota(jnp.int32, (block, block), 1)
                allowed = (key_at <= query_at) & (key_at < length)
            for g in range(groups):
                queries = heads_ref[pl.ds(at, block), g * size : (g + 1) * size]
                grads = grad_ref[pl.ds(at, block), g * size : (g + 1) * size]
                scores = nt(keys, queries) - total_ref[g, 0:1, pl.ds(at, block)]
                if masked:
                    scores = jnp.where(allowed, scores, MASKED)
                probs = jnp.exp2(scores)
                grad_attend = nt(values, grads)
                grad_scores = (
                    probs * (grad_attend - center_ref[g, 0:1, pl.ds(at, block)])
                ).astype(jnp.bfloat16)
                grad_values = grad_values + nn(probs.astype(jnp.bfloat16), grads)
                grad_keys = grad_keys + nn(grad_scores, queries)
                query_sums_ref[g, pl.ds(at, block), :] += tn(grad_scores, keys)
            return grad_keys, grad_values

        zero = jnp.zeros((block, size), jnp.float32)
        first = jnp.where(j < whole, jnp.minimum(j + 1, blocks), blocks)
        carry = lax.fori_loop(j, first, lambda i, c: step(i, c, True), (zero, zero))
        grad_keys, grad_values = lax.fori_loop(
            first, blocks, lambda i, c: step(i, c, False), carry
        )
        key_sums_ref[pl.ds(start, block), :] = grad_keys
        grad_raw_ref[pl.ds(start, block), value_lanes] = grad_values.astype(grad_raw_ref.dtype)
        return 0

    lax.fori_loop(0, some, key_block, 0)

    def padding(j, _):
        start = pl.multiple_of(j * block, block)
        key_sums_ref[pl.ds(start, block), :] = jnp.zeros((block, size), jnp.float32)
        grad_raw_ref[pl.ds(start, block), value_lanes] = jnp.zeros(
            (block, size), grad_raw_ref.dtype
        )
        return 0

    lax.fori_loop(some, blocks, padding, 0)

    def head_back(i, carry):
        rows = pl.ds(pl.multiple_of(i * block, block), block)
        cosine, sine_table = cosine_ref[rows, :], sine_ref[rows, :]
        sums = list(carry)
        for g in range(groups + 1):
            lanes = slice(g * size, (g + 1) * size)
            if g < groups:
                grad = query_sums_ref[g, rows, :] * size**-0.5
            else:
                grad = key_sums_ref[rows, :] * (1.0 / math.log2(math.e))
            which = 0 if g < groups else 1
            grad = grad.astype(jnp.bfloat16).astype(jnp.float32)
            grad = grad * cosine - pltpu.roll(grad, size // 2, 1) * sine_table
            value = raw_ref[rows, lanes]
            scale = lax.rsqrt(jnp.mean(value * value, axis=-1, keepdims=True) + EPS)
            unit = value * scale
            sums[which] = sums[which] + jnp.sum(grad * unit, axis=0, keepdims=True)
            grad = grad * head_gain_ref[which : which + 1, :]
            inner = jnp.mean(grad * unit, axis=-1, keepdims=True)
            grad_raw_ref[rows, lanes] = (scale * (grad - unit * inner)).astype(grad_raw_ref.dtype)
        return tuple(sums)

    zero = jnp.zeros((1, size), jnp.float32)
    sums = lax.fori_loop(0, blocks, head_back, (zero, zero))
    gain_ref[0, 0:1, :] = sums[0]
    gain_ref[0, 1:2, :] = sums[1]


def attend_backward(
    place, heads, raw, cosine, sine_table, head_gains, groups, context, totals, pieces
):
    count = len(pieces)
    positions = heads.shape[0]
    rows = positions // count
    block = min(512, positions)
    size = HEAD_SIZE
    kv_count = heads.shape[1] // ((groups + 2) * size)

    def of_group(lines, columns):
        return pl.BlockSpec((lines, columns * size), lambda h, s: (0, h))

    width = kv_count * groups * size
    return pl.pallas_call(
        functools.partial(backward_kernel, block, groups, positions, count),
        grid_spec=pltpu.PrefetchScalarGridSpec(
            num_scalar_prefetch=1,
            grid=(kv_count,),
            in_specs=[
                of_group(positions, groups + 2),
                of_group(positions, groups + 1),
                fixed(cosine.shape),
                fixed(sine_table.shape),
                fixed(head_gains.shape),
                pl.BlockSpec((count, rows, groups * size), lambda h, s: (0, 0, h)),
                pl.BlockSpec((groups, 8, positions), lambda h, s: (h, 0, 0)),
            ]
            + [of_group(rows, groups)] * count,
            out_specs=[
                of_group(positions, groups + 2),
                pl.BlockSpec((1, 2, size), lambda h, s: (h, 0, 0)),
            ],
            scratch_shapes=[
                pltpu.VMEM((groups, positions, size), jnp.float32),
                pltpu.VMEM((positions, size), jnp.float32),
                pltpu.VMEM((groups, 8, positions), jnp.float32),
                pltpu.VMEM((positions, groups * size), jnp.bfloat16),
            ],
        ),
        out_shape=(
            jax.ShapeDtypeStruct(heads.shape, jnp.bfloat16),
            jax.ShapeDtypeStruct((kv_count, 2, size), jnp.float32),
        ),
        compiler_params=arbitrary(1, 56),
        cost_estimate=cost(
            positions * positions * width,
            2 * positions * width,
            positions * positions * width // size // 20,
        ),
        name="attend_backward",
    )(
        place,
        heads,
        raw,
        cosine,
        sine_table,
        head_gains,
        context,
        totals,
        *pieces,
    )


def tile_of(hidden_units):
    return next(t for t in (512, 384, 256, 128) if hidden_units % t == 0)


def separate(both, tile):
    pieces = [both[:, at : at + tile] for at in range(0, both.shape[1], tile)]
    return jnp.concatenate(pieces[0::2], axis=1), jnp.concatenate(pieces[1::2], axis=1)


def out_norm_kernel(count, weight_ref, rows_ref, gain_ref, *refs):
    resid_ref, normed_ref = refs[count:]
    part = refs[0].shape[-1]
    resid = rows_ref[...].astype(jnp.float32)
    for k in range(count):
        at = (count - k) % count * part
        resid = resid + nn(refs[k][...], weight_ref[at : at + part, :])
    resid_ref[...] = resid
    normed_ref[...] = norm_rows(resid, gain_ref[...]).astype(normed_ref.dtype)


def out_norm(pieces, weight, tokens, gain):
    count = len(pieces)
    rows, part = pieces[0].shape
    width = weight.shape[1]
    block = min(256, rows)
    across = pl.BlockSpec((block, width), lambda i: (i, 0))
    return pl.pallas_call(
        functools.partial(out_norm_kernel, count),
        grid=(rows // block,),
        in_specs=[fixed(weight.shape), across, fixed(gain.shape)]
        + [pl.BlockSpec((block, part), lambda i: (i, 0))] * count,
        out_specs=[across, across],
        out_shape=(
            jax.ShapeDtypeStruct((rows, width), jnp.float32),
            jax.ShapeDtypeStruct((rows, width), jnp.bfloat16),
        ),
        compiler_params=arbitrary(1, 48),
        cost_estimate=cost(2 * rows * count * part * width, 2 * weight.size + 10 * rows * width),
        name="out_norm",
    )(weight, tokens, gain, *pieces)


def hidden_kernel(tile, own_ref, away_ref, weight_ref, *refs):
    both_ref, hidden_ref = refs[-2:]
    rows = own_ref.shape[0]
    for half, rows_ref in enumerate((own_ref, away_ref)):
        here = slice(half * rows, (half + 1) * rows)
        both = nn(rows_ref[...], weight_ref[...])
        both_ref[here, :] = both
        gate, up = both[:, :tile], both[:, tile:]
        hidden_ref[here, :] = (gate * jax.nn.sigmoid(gate) * up).astype(hidden_ref.dtype)


def hidden_units(own, away, weight, tile, at, total, before):
    rows, width = own.shape
    columns = weight.shape[1]
    tiles = columns // (2 * tile)
    in_specs = [
        fixed(own.shape),
        fixed(away.shape),
        pl.BlockSpec((width, 2 * tile), lambda j: (0, j)),
    ]
    args, aliases = [own, away, weight], {}
    if before is not None:
        in_specs.append(pl.BlockSpec(memory_space=pl.ANY))
        args.append(before)
        aliases = {3: 1}
    return pl.pallas_call(
        functools.partial(hidden_kernel, tile),
        grid=(tiles,),
        in_specs=in_specs,
        out_specs=[
            pl.BlockSpec((2 * rows, 2 * tile), lambda j: (0, j)),
            pl.BlockSpec((2 * rows, tile), lambda j: (0, at * tiles + j)),
        ],
        out_shape=(
            jax.ShapeDtypeStruct((2 * rows, columns), jnp.float32),
            jax.ShapeDtypeStruct((2 * rows, total), jnp.bfloat16),
        ),
        input_output_aliases=aliases,
        compiler_params=arbitrary(1, 56),
        cost_estimate=cost(4 * rows * width * columns, 2 * width * columns + 10 * rows * columns),
        name="hidden_units",
    )(*args)


def hidden_back_kernel(tile, own_ref, away_ref, down_ref, both_ref, out_ref):
    rows = own_ref.shape[0]
    for half, grads_ref in enumerate((own_ref, away_ref)):
        here = slice(half * rows, (half + 1) * rows)
        grad_hidden = nt(grads_ref[...], down_ref[...])
        gate, up = both_ref[here, :tile], both_ref[here, tile:]
        sigmoid = jax.nn.sigmoid(gate)
        silu = gate * sigmoid
        out_ref[here, :tile] = (grad_hidden * up * (sigmoid + silu * (1.0 - sigmoid))).astype(
            out_ref.dtype
        )
        out_ref[here, tile:] = (grad_hidden * silu).astype(out_ref.dtype)


def hidden_back(own, away, down, both, tile):
    rows, width = own.shape
    columns = both.shape[1]
    pair = pl.BlockSpec((2 * rows, 2 * tile), lambda j: (0, j))
    return pl.pallas_call(
        functools.partial(hidden_back_kernel, tile),
        grid=(columns // (2 * tile),),
        in_specs=[
            fixed(own.shape),
            fixed(away.shape),
            pl.BlockSpec((tile, width), lambda j: (j, 0)),
            pair,
        ],
        out_specs=pair,
        out_shape=jax.ShapeDtypeStruct((2 * rows, columns), jnp.bfloat16),
        compiler_params=arbitrary(1, 56),
        cost_estimate=cost(2 * rows * width * columns, width * columns + 12 * rows * columns),
        name="hidden_back",
    )(own, away, down, both)


def unit_grads_kernel(own_ref, away_ref, grads_ref, out_ref):
    rows = own_ref.shape[0]
    out_ref[...] = (
        tn(own_ref[...], grads_ref[:rows, :]) + tn(away_ref[...], grads_ref[rows:, :])
    ).astype(out_ref.dtype)


def unit_grads(own, away, grads):
    rows, width = own.shape
    columns = grads.shape[1]
    tile = tile_of(columns)
    return pl.pallas_call(
        unit_grads_kernel,
        grid=(columns // tile,),
        in_specs=[
            fixed(own.shape),
            fixed(away.shape),
            pl.BlockSpec((2 * rows, tile), lambda j: (0, j)),
        ],
        out_specs=pl.BlockSpec((width, tile), lambda j: (0, j)),
        out_shape=jax.ShapeDtypeStruct((width, columns), jnp.bfloat16),
        compiler_params=arbitrary(1, 56),
        cost_estimate=cost(4 * rows * width * columns, 2 * width * columns + 4 * rows * columns),
        name="unit_grads",
    )(own, away, grads)


def down_grads_kernel(hidden_ref, own_ref, away_ref, out_ref):
    rows = own_ref.shape[0]
    out_ref[...] = (
        tn(hidden_ref[:rows, :], own_ref[...]) + tn(hidden_ref[rows:, :], away_ref[...])
    ).astype(out_ref.dtype)


def down_grads(hidden, own, away):
    rows, width = own.shape
    units = hidden.shape[1]
    tile = tile_of(units)
    return pl.pallas_call(
        down_grads_kernel,
        grid=(units // tile,),
        in_specs=[
            pl.BlockSpec((2 * rows, tile), lambda j: (0, j)),
            fixed(own.shape),
            fixed(away.shape),
        ],
        out_specs=pl.BlockSpec((tile, width), lambda j: (j, 0)),
        out_shape=jax.ShapeDtypeStruct((units, width), jnp.bfloat16),
        compiler_params=arbitrary(1, 56),
        cost_estimate=cost(4 * rows * width * units, 2 * width * units + 4 * rows * units),
        name="down_grads",
    )(hidden, own, away)


def grad_normed_kernel(parts, *refs):
    grads, weights = refs[:parts], refs[parts : 2 * parts]
    own_ref, away_ref = refs[2 * parts :]
    rows = own_ref.shape[0]
    for half, out_ref in enumerate((own_ref, away_ref)):
        here = slice(half * rows, (half + 1) * rows)
        total = nt(grads[0][here, :], weights[0][...])
        for grad_ref, weight_ref in zip(grads[1:], weights[1:]):
            total = total + nt(grad_ref[here, :], weight_ref[...])
        out_ref[...] = total.astype(out_ref.dtype)


def grad_normed(grads, weights):
    rows = grads[0].shape[0] // 2
    width = weights[0].shape[0]
    tile = tile_of(width)
    return pl.pallas_call(
        functools.partial(grad_normed_kernel, len(grads)),
        grid=(width // tile,),
        in_specs=[fixed(grad.shape) for grad in grads]
        + [pl.BlockSpec((tile, weight.shape[1]), lambda j: (j, 0)) for weight in weights],
        out_specs=[pl.BlockSpec((rows, tile), lambda j: (0, j))] * 2,
        out_shape=(
            jax.ShapeDtypeStruct((rows, width), jnp.float32),
            jax.ShapeDtypeStruct((rows, width), jnp.bfloat16),
        ),
        compiler_params=arbitrary(1, 60),
        cost_estimate=cost(
            sum(2 * grad.size * width for grad in grads),
            sum(2 * grad.size + 2 * weight.size for grad, weight in zip(grads, weights)),
        ),
        name="grad_normed",
    )(*grads, *weights)


def mlp_out_kernel(hidden_ref, *refs):
    own_ref, away_ref = refs[-2:]
    rows = own_ref.shape[0]
    for half, out_ref in enumerate((own_ref, away_ref)):
        here = slice(half * rows, (half + 1) * rows)
        at, total = 0, None
        for down_ref in refs[:-2]:
            units = down_ref.shape[0]
            part = nn(hidden_ref[here, at : at + units], down_ref[...])
            total = part if total is None else total + part
            at += units
        out_ref[...] = total.astype(out_ref.dtype)


def mlp_out(hidden, downs):
    rows = hidden.shape[0] // 2
    width = downs[0].shape[1]
    tile = tile_of(width)
    return pl.pallas_call(
        mlp_out_kernel,
        grid=(width // tile,),
        in_specs=[fixed(hidden.shape)]
        + [pl.BlockSpec((down.shape[0], tile), lambda j: (0, j)) for down in downs],
        out_specs=[pl.BlockSpec((rows, tile), lambda j: (0, j))] * 2,
        out_shape=(
            jax.ShapeDtypeStruct((rows, width), jnp.float32),
            jax.ShapeDtypeStruct((rows, width), jnp.bfloat16),
        ),
        compiler_params=arbitrary(1, 56),
        cost_estimate=cost(2 * hidden.size * width, 4 * hidden.size + 6 * rows * width),
        name="mlp_out",
    )(hidden, *downs)


def resid_back_kernel(
    place_ref,
    own_ref,
    away_ref,
    resid_ref,
    cotangent_ref,
    gain_ref,
    weight_ref,
    grad_ref,
    low_ref,
    sums_ref,
    *piece_refs,
):
    block = own_ref.shape[0]
    part = piece_refs[0].shape[-1]
    first = place_ref[1] + pl.program_id(0) * block
    at = first + lax.broadcasted_iota(jnp.int32, (block, 1), 0)
    valid = (at < place_ref[0]).astype(jnp.float32)
    grads = own_ref[...] + away_ref[...].astype(jnp.float32)
    back, sums = norm_back(resid_ref[...], gain_ref[...], grads)
    grad_resid = valid * cotangent_ref[...].astype(jnp.float32) + back
    grad_ref[...] = grad_resid
    low = grad_resid.astype(jnp.bfloat16)
    low_ref[...] = low
    for k, piece_ref in enumerate(piece_refs):
        piece_ref[...] = nt(low, weight_ref[k * part : (k + 1) * part, :]).astype(piece_ref.dtype)

    @pl.when(pl.program_id(0) == 0)
    def _():
        sums_ref[...] = jnp.zeros_like(sums_ref)

    sums_ref[...] += sums


def resid_back(own, away, resid, cotangent, gain, weight, length, start, count):
    rows, width = own.shape
    part = weight.shape[0] // count
    block = min(256, rows)
    across = pl.BlockSpec((block, width), lambda i, s: (i, 0))
    return pl.pallas_call(
        resid_back_kernel,
        grid_spec=pltpu.PrefetchScalarGridSpec(
            num_scalar_prefetch=1,
            grid=(rows // block,),
            in_specs=[across] * 4 + [fixed(gain.shape), fixed(weight.shape)],
            out_specs=[across, across, fixed(gain.shape)]
            + [pl.BlockSpec((block, part), lambda i, s: (i, 0))] * count,
        ),
        out_shape=(
            jax.ShapeDtypeStruct((rows, width), jnp.float32),
            jax.ShapeDtypeStruct((rows, width), jnp.bfloat16),
            jax.ShapeDtypeStruct(gain.shape, jnp.float32),
        )
        + (jax.ShapeDtypeStruct((rows, part), jnp.bfloat16),) * count,
        compiler_params=arbitrary(1, 56),
        cost_estimate=cost(2 * rows * weight.size, 2 * weight.size + 20 * rows * width),
        name="resid_back",
    )(jnp.stack([length, start]), own, away, resid, cotangent, gain, weight)


def out_grads_kernel(count, grads_ref, *refs):
    out_ref = refs[count]
    part = refs[0].shape[-1]
    for k in range(count):
        at = (count - k) % count * part
        out_ref[at : at + part, :] = tn(refs[k][...], grads_ref[...]).astype(out_ref.dtype)


def out_grads(pieces, grads):
    count = len(pieces)
    rows, part = pieces[0].shape
    width = grads.shape[1]
    tile = tile_of(width)
    return pl.pallas_call(
        functools.partial(out_grads_kernel, count),
        grid=(width // tile,),
        in_specs=[pl.BlockSpec((rows, tile), lambda j: (0, j))]
        + [fixed(piece.shape) for piece in pieces],
        out_specs=pl.BlockSpec((count * part, tile), lambda j: (0, j)),
        out_shape=jax.ShapeDtypeStruct((count * part, width), jnp.bfloat16),
        compiler_params=arbitrary(1, 48),
        cost_estimate=cost(
            2 * rows * count * part * width, 2 * count * part * (rows + width) + 2 * rows * width
        ),
        name="out_grads",
    )(grads, *pieces)


def pack_heads_kernel(groups, query_ref, key_ref, value_ref, gain_ref, out_ref):
    size = HEAD_SIZE
    at = 0
    for h in range(key_ref.shape[1] // size):
        for ref, start, columns in (
            (query_ref, h * groups * size, groups * size),
            (key_ref, h * size, size),
            (value_ref, h * size, size),
        ):
            out_ref[:, at : at + columns] = ref[:, start : start + columns]
            at += columns
    out_ref[:, at:] = gain_ref[...]


def pack_heads(query, key, value, gain, groups):
    rows = query.shape[0]
    columns = query.shape[1] + key.shape[1] + value.shape[1] + gain.shape[1]
    args = (query, key, value, gain)
    return pl.pallas_call(
        functools.partial(pack_heads_kernel, groups),
        grid=(1,),
        in_specs=[fixed(arg.shape) for arg in args],
        out_specs=fixed((rows, columns)),
        out_shape=jax.ShapeDtypeStruct((rows, columns), jnp.bfloat16),
        compiler_params=arbitrary(1, 16),
        cost_estimate=cost(0, 4 * rows * columns),
        name="pack_heads",
    )(*args)


def pack_units_kernel(tile, gate_ref, up_ref, out_ref):
    for at in range(0, gate_ref.shape[1], tile):
        out_ref[:, 2 * at : 2 * at + tile] = gate_ref[:, at : at + tile]
        out_ref[:, 2 * at + tile : 2 * at + 2 * tile] = up_ref[:, at : at + tile]


def pack_units(gate, up, tile):
    rows, columns = gate.shape
    return pl.pallas_call(
        functools.partial(pack_units_kernel, tile),
        grid=(1,),
        in_specs=[fixed(gate.shape), fixed(up.shape)],
        out_specs=fixed((rows, 2 * columns)),
        out_shape=jax.ShapeDtypeStruct((rows, 2 * columns), jnp.bfloat16),
        compiler_params=arbitrary(1, 16),
        cost_estimate=cost(0, 8 * rows * columns),
        name="pack_units",
    )(gate, up)


def tokens_back_kernel(
    own_ref, right_ref, left_ref, rows_ref, gain_ref, resid_ref, out_ref, beside_ref
):
    width = rows_ref.shape[1]
    total = (
        own_ref[...] + right_ref[...].astype(jnp.float32) + left_ref[...].astype(jnp.float32)
    )
    back = norm_back(rows_ref[...].astype(jnp.float32), gain_ref[...], total[:, :width])[0]
    out_ref[...] = (resid_ref[...] + back).astype(out_ref.dtype)
    beside_ref[...] = total[:, width:]


def tokens_back(parts, tokens, gain, grad_resid):
    rows, width = tokens.shape
    more = parts[0].shape[1] - width
    block = min(256, rows)
    across = pl.BlockSpec((block, width), lambda i: (i, 0))
    both = pl.BlockSpec((block, width + more), lambda i: (i, 0))
    return pl.pallas_call(
        tokens_back_kernel,
        grid=(rows // block,),
        in_specs=[both] * 3 + [across, fixed(gain.shape), across],
        out_specs=[across, pl.BlockSpec((block, more), lambda i: (i, 0))],
        out_shape=(
            jax.ShapeDtypeStruct((rows, width), jnp.bfloat16),
            jax.ShapeDtypeStruct((rows, more), jnp.float32),
        ),
        compiler_params=arbitrary(1, 40),
        cost_estimate=cost(20 * rows * width, 16 * rows * width),
        name="tokens_back",
    )(*parts, tokens, gain, grad_resid)


def share_kernel(slot_ref, grads_ref, weight_ref, beside_ref, out_ref):
    width = weight_ref.shape[0]
    out_ref[:, :width] = nt(grads_ref[...], weight_ref[...]).astype(out_ref.dtype)
    out_ref[:, width:] = beside_ref[...].astype(out_ref.dtype)


def share(slot, grads, weight, beside, k, count, dtype):
    positions, columns = grads.shape
    rows = positions // count
    width, more = weight.shape[0], beside.shape[1]
    block = min(256, rows)
    parts = rows // block
    return pl.pallas_call(
        share_kernel,
        grid_spec=pltpu.PrefetchScalarGridSpec(
            num_scalar_prefetch=1,
            grid=(parts,),
            in_specs=[
                pl.BlockSpec((block, columns), lambda i, s: (s[0] * parts + i, 0)),
                fixed(weight.shape),
                pl.BlockSpec((block, more), lambda i, s: (k * parts + i, 0)),
            ],
            out_specs=pl.BlockSpec((block, width + more), lambda i, s: (i, 0)),
        ),
        out_shape=jax.ShapeDtypeStruct((rows, width + more), dtype),
        compiler_params=arbitrary(1, 40),
        cost_estimate=cost(2 * rows * columns * width, 2 * width * columns),
        name="share",
    )(slot, grads, weight, beside)


def heads_back_kernel(normed_ref, grad_ref, weight_ref, out_ref, sums_ref):
    partial = tn(normed_ref[...], grad_ref[...])
    out_ref[...] = partial.astype(out_ref.dtype)
    sums = jnp.sum(partial * weight_ref[...].astype(jnp.float32), axis=1, keepdims=True)
    sums_ref[...] = jnp.broadcast_to(sums, sums_ref.shape)


def heads_back(normed, grads, weight):
    positions, width = normed.shape
    columns = grads.shape[1]
    block = min(512, width)
    return pl.pallas_call(
        heads_back_kernel,
        grid=(width // block,),
        in_specs=[
            pl.BlockSpec((positions, block), lambda j: (0, j)),
            pl.BlockSpec((positions, columns), lambda j: (0, 0)),
            pl.BlockSpec((block, columns), lambda j: (j, 0)),
        ],
        out_specs=[
            pl.BlockSpec((block, columns), lambda j: (j, 0)),
            pl.BlockSpec((block, LANES), lambda j: (j, 0)),
        ],
        out_shape=(
            jax.ShapeDtypeStruct((width, columns), jnp.bfloat16),
            jax.ShapeDtypeStruct((width, LANES), jnp.float32),
        ),
        compiler_params=arbitrary(1, 48),
        cost_estimate=cost(
            2 * positions * width * columns, 2 * positions * (width + columns) + 4 * width * columns
        ),
        name="heads_back",
    )(normed, grads, weight)


def norm_back(value_rows, gain, grads):
    scale = lax.rsqrt(jnp.mean(value_rows * value_rows, axis=-1, keepdims=True) + EPS)
    unit = value_rows * scale
    scaled = grads * gain
    inner = jnp.mean(scaled * unit, axis=-1, keepdims=True)
    return scale * (scaled - unit * inner), jnp.sum(grads * unit, axis=0)


def after(value, *others):
    return lax.optimization_barrier((value, others))[0]


def hop_right(value, count, hop):
    return lax.ppermute(value, "seq", [(i, i + 1) for i in range(hop - 1, count - 1)])


def hop_left(value, count, hop):
    return lax.ppermute(value, "seq", [(i, i - 1) for i in range(1, count - hop + 1)])


def line_scatter(parts, before):
    count = len(parts)
    right, left = None, None
    for hop in range(count - 1):
        to_right, to_left = parts[count - 1 - hop], parts[hop + 1]
        if hop:
            to_right = to_right.astype(jnp.float32) + right.astype(jnp.float32)
            to_left = to_left.astype(jnp.float32) + left.astype(jnp.float32)
        if hop in before:
            to_right, to_left = after((to_right, to_left), *before[hop])
        right = lax.ppermute(
            to_right.astype(jnp.bfloat16), "seq", [(i, i + 1) for i in range(hop + 1)]
        )
        left = lax.ppermute(
            to_left.astype(jnp.bfloat16),
            "seq",
            [(i, i - 1) for i in range(count - 1 - hop, count)],
        )
    return parts[0], right, left


def sum_over(value, axis):
    flat = value.reshape(-1, LANES)
    size = lax.axis_size(axis)
    assert size & (size - 1) == 0
    step = 1
    while step < size:
        flat = flat + lax.ppermute(flat, axis, [(i, i ^ step) for i in range(size)])
        step *= 2
    return flat.reshape(-1)


def swap(value, count):
    return lax.ppermute(value, "seq", [(i, i ^ 1) for i in range(count)])


def fetch(value, count, step):
    return lax.ppermute(value, "seq", [((i + step) % count, i) for i in range(count)])


def give(value, count, step):
    return lax.ppermute(value, "seq", [(i, (i + step) % count) for i in range(count)])


def on_device(
    tokens,
    lengths,
    cotangent,
    w_query,
    key_weight,
    value_weight,
    w_out,
    w_gate,
    w_up,
    w_down,
    norm_attn,
    norm_mlp,
    norm_query,
    norm_key,
):
    slots, rows, width = tokens.shape
    assert slots == 1
    count = lax.axis_size("seq")
    positions = count * rows
    me = lax.axis_index("seq")
    tokens_low = tokens.reshape(rows, width)
    cotangent_low = cotangent.reshape(rows, width)
    length = lengths[0]
    low = jnp.bfloat16
    groups = w_query.shape[1] // key_weight.shape[1]
    kv_count = key_weight.shape[1] // HEAD_SIZE
    units = w_gate.shape[1]
    tile = tile_of(units)
    steps = range(0, count, PAIR)

    def from_groups(both):
        size = HEAD_SIZE
        starts = [h * (groups + 2) * size for h in range(kv_count)]
        ends = (0, groups * size, (groups + 1) * size, (groups + 2) * size)
        return [
            jnp.concatenate([both[:, s + low_end : s + high_end] for s in starts], axis=1)
            for low_end, high_end in zip(ends, ends[1:])
        ]

    weight_rows = w_query.shape[0]
    gain_parts = (norm_attn, norm_mlp, norm_query, norm_key)
    gain_sizes = [part.shape[0] for part in gain_parts]
    own_gains = jnp.concatenate(gain_parts)
    gain_block = jnp.pad(own_gains, (0, weight_rows * LANES - own_gains.shape[0])).reshape(
        weight_rows, LANES
    )
    own_heads = pack_heads(w_query, key_weight, value_weight, gain_block, groups)
    head_columns = own_heads.shape[1] - LANES
    gathered_heads = lax.all_gather(own_heads, "dp", axis=0, tiled=True)
    heads_weight = gathered_heads[:, :head_columns]
    gathered_gains = gathered_heads[:, head_columns:].reshape(-1, weight_rows * LANES)
    rights = [hop_right(tokens_low, count, 1)]
    lefts = [hop_left(tokens_low, count, 1)]
    gains, at = [], 0
    for part_size in gain_sizes:
        gains.append(gathered_gains[:, at : at + part_size].reshape(1, -1).astype(jnp.float32))
        at += part_size
    gain_attn, gain_mlp = gains[:2]
    head_gains = jnp.concatenate(gains[2:], axis=0)
    cosine, sine_table = angles(jnp.arange(positions, dtype=jnp.float32))

    places = [
        jnp.stack([lax.rem(me + k, count), (me + k < count).astype(jnp.int32)])
        for k in range(count)
    ]
    slot_place = jnp.stack([length, me])

    def project_block(k, whole):
        first, second = tokens_low, tokens_low
        if k:
            first, second = lefts[k - 1], rights[count - k - 1]
        return project(
            places[k],
            first,
            second,
            gain_attn,
            heads_weight,
            cosine,
            sine_table,
            head_gains,
            groups,
            whole,
            count,
        )

    own_both = pack_units(w_gate, w_up, tile)
    first_hop = (rights[0], lefts[0])
    both_weights = [lax.all_gather(after(own_both, *first_hop), "dp", axis=0, tiled=True)]
    down_weights = [lax.all_gather(after(w_down, *first_hop), "dp", axis=1, tiled=True)]
    whole = project_block(0, None)
    for hop in range(2, count - 1):
        rights.append(hop_right(rights[-1], count, hop))
        lefts.append(hop_left(lefts[-1], count, hop))
    right, left = after((rights[-1], lefts[-1]), whole[1])
    before_last = (rights[-1], lefts[-1])
    out_blocks = [w_out] + [
        fetch(after(w_out, *before_last), count, k) for k in range(1, count)
    ]
    fetched_down = [fetch(after(w_down, *before_last), count, step) for step in steps[1:]]
    rights.append(hop_right(right, count, count - 1))
    lefts.append(hop_left(left, count, count - 1))
    for k in range(2, count - 1):
        whole = project_block(k, whole)
    gathered = (rights[-1], lefts[-1])
    out_weight = lax.all_gather(
        after(
            jnp.concatenate(out_blocks, axis=0),
            both_weights[0],
            down_weights[0],
            *gathered,
            *fetched_down,
        ),
        "dp",
        axis=1,
        tiled=True,
    )

    fetched_both = [
        fetch(after(own_both, *gathered), count, step) for step in steps[1:]
    ]
    for k in [1, count - 1] if count > 2 else [1]:
        whole = project_block(k, whole)
    normed_attn, heads, raw = whole
    context, totals = attend_forward(slot_place, heads, groups, count)
    sent = after(context, *fetched_both)
    context_pieces = [context[0]] + [give(sent[k], count, k) for k in range(1, count)]
    resid, normed_mlp = out_norm(context_pieces, out_weight, tokens_low, gain_mlp)
    away_normed = swap(normed_mlp, count)
    for both, down in zip(fetched_both, fetched_down):
        both_weights.append(lax.all_gather(after(both, context), "dp", axis=0, tiled=True))
        down_weights.append(lax.all_gather(after(down, heads), "dp", axis=1, tiled=True))

    place = jnp.arange(rows, dtype=jnp.int32)[:, None] + me * rows
    valid_rows = (place < length).astype(low)
    grad_rows = cotangent_low * valid_rows
    away_grads = swap(after(grad_rows, away_normed), count)
    hidden, boths = None, []
    for at, weight in enumerate(both_weights):
        both, hidden = hidden_units(
            normed_mlp, away_normed, weight, tile, at, len(steps) * units, hidden
        )
        boths.append(both)

    def spread(partial, axis):
        return lax.psum_scatter(partial, "dp", scatter_dimension=axis, tiled=True)

    down_partial = down_grads(hidden, grad_rows, away_grads)
    grad_rows, away_grads = after((grad_rows, away_grads), down_partial)
    down_sums = spread(down_partial, 1)
    grad_boths = [
        hidden_back(grad_rows, away_grads, down, both, tile)
        for down, both in zip(down_weights, boths)
    ]
    mate_partials = [unit_grads(normed_mlp, away_normed, grad) for grad in grad_boths[1:]]
    mate_sums = [spread(partial, 0) for partial in mate_partials]
    grad_normed_own, grad_normed_away = grad_normed(
        after(grad_boths, *mate_partials), both_weights
    )
    own_partial = unit_grads(normed_mlp, away_normed, after(grad_boths[0], grad_normed_away))
    mlp_own, mlp_away = mlp_out(after(hidden, own_partial), down_weights)
    grad_resid, grad_attn_low, gain_mlp_sums, *pieces = resid_back(
        grad_normed_own,
        after(swap(grad_normed_away, count), own_partial, mlp_own, down_sums),
        resid,
        cotangent_low,
        gain_mlp,
        out_weight,
        length,
        me * rows,
        count,
    )
    pieces = [pieces[0]] + [give(pieces[k], count, k) for k in range(1, count)]
    out_partial = out_grads(context_pieces, grad_attn_low)
    out_sums = spread(out_partial, 1)
    own_sum = spread(after(own_partial, *pieces, out_partial), 0)
    pieces = after(pieces, out_partial, down_sums, *mate_sums)
    grad_raw, head_gain_terms = attend_backward(
        slot_place,
        heads,
        raw,
        cosine,
        sine_table,
        head_gains,
        groups,
        context,
        totals,
        pieces,
    )
    away_both, away_down, mlp_away = after((mate_sums, down_sums, mlp_away), *pieces)
    mlp_away = swap(mlp_away, count)
    given_first, given_second = [
        [give(half, count, step) for step, half in zip(steps[1:], halves)]
        for halves in zip(*(jnp.split(piece, 2, axis=0) for piece in away_both))
    ]
    down_pieces = jnp.split(away_down, len(steps), axis=0)
    given_down = [give(piece, count, step) for step, piece in zip(steps[1:], down_pieces[1:])]
    shares = {}
    for k in [count - 1, 1, *range(2, count - 1), 0]:
        shares[k] = share(
            places[k][:1],
            grad_raw,
            heads_weight,
            out_sums,
            k,
            count,
            low if k else jnp.float32,
        )
    shares[1], shares[count - 1] = after(
        (shares[1], shares[count - 1]), *given_down, *given_first, mlp_away
    )
    shares = [shares[k] for k in range(count)]
    heads_partial, gain_attn_sums = heads_back(
        normed_attn, after(grad_raw, shares[1], shares[-1]), heads_weight
    )
    grad_heads = spread(heads_partial, 0)
    gain_attn_term = gain_attn_sums[:, 0] / gain_attn[0]
    head_gain_sums = jnp.sum(head_gain_terms, axis=0)
    terms = (gain_attn_term, gain_mlp_sums[0], head_gain_sums[0], head_gain_sums[1])
    gain_sums = sum_over(jnp.concatenate(terms), "dp").reshape(-1, LANES)
    sums = sum([give(gain_sums, count, k) if k else gain_sums for k in range(count)]).reshape(-1)
    last_parts = line_scatter(
        shares,
        {1: (heads_partial, shares[0], sums, *given_second), 2: (own_sum,)},
    )
    grad_heads = grad_heads.astype(jnp.float32)
    grad_query, grad_key, grad_value = from_groups(grad_heads)
    layer_output = (
        (valid_rows.astype(jnp.float32) * (resid + mlp_own + mlp_away.astype(jnp.float32)))
        .astype(low)
        .reshape(slots, rows, width)
    )
    grad_tokens, grad_out = tokens_back(last_parts, tokens_low, gain_attn, grad_resid)
    grad_tokens = grad_tokens.reshape(slots, rows, width)

    both_total = own_sum.astype(jnp.float32) + sum(
        jnp.concatenate(halves, axis=0).astype(jnp.float32)
        for halves in zip(given_first, given_second)
    )
    grad_gate, grad_up = separate(both_total, tile)
    grad_down = sum([part.astype(jnp.float32) for part in [down_pieces[0], *given_down]])

    gain_grads, at = [], 0
    for term, part_size in zip(terms, gain_sizes):
        gain_grads.append(
            lax.dynamic_slice_in_dim(
                sums[at : at + term.shape[0]], lax.axis_index("dp") * part_size, part_size, 0
            )
        )
        at += term.shape[0]
    return (
        layer_output,
        grad_tokens,
        grad_query,
        grad_key,
        grad_value,
        grad_out,
        grad_gate,
        grad_up,
        grad_down,
        *gain_grads,
    )


def solution(mesh):
    return jax.shard_map(
        on_device,
        mesh=mesh,
        in_specs=(
            P("dp", "seq", None),
            P("dp"),
            P("dp", "seq", None),
            P("dp", "seq"),
            P("dp", "seq"),
            P("dp", "seq"),
            P("seq", "dp"),
            P("dp", "seq"),
            P("dp", "seq"),
            P("seq", "dp"),
            P("dp"),
            P("dp"),
            P("dp"),
            P("dp"),
        ),
        out_specs=(
            P("dp", "seq", None),
            P("dp", "seq", None),
            P("dp", "seq"),
            P("dp", "seq"),
            P("dp", "seq"),
            P("seq", "dp"),
            P("dp", "seq"),
            P("dp", "seq"),
            P("seq", "dp"),
            P("dp"),
            P("dp"),
            P("dp"),
            P("dp"),
        ),
        check_vma=False,
    )
```

```python
import functools
import math

import jax
import jax.numpy as jnp
from jax import lax
from jax.experimental import pallas as pl
from jax.experimental.pallas import tpu as pltpu
from jax.sharding import PartitionSpec as P

HEAD_SIZE = 128
EPS = 1e-06
BASE = 1000000.0
MASKED = -1e30
QUERY_SCALE = HEAD_SIZE**-0.5 * math.log2(math.e)
PAIR = 2
LANES = 128
COST_SCALE = 0.05


def norm_rows(value_rows, gain):
    return (
        value_rows
        * lax.rsqrt(jnp.mean(value_rows * value_rows, axis=-1, keepdims=True) + EPS)
        * gain
    )


def angles(positions):
    frequency = BASE ** (-(jnp.arange(HEAD_SIZE // 2, dtype=jnp.float32) * 2.0 / HEAD_SIZE))
    phases = positions[:, None] * frequency[None, :]
    cosine, sine_table = jnp.cos(phases), jnp.sin(phases)
    return (
        jnp.concatenate([cosine, cosine], axis=-1),
        jnp.concatenate([-sine_table, sine_table], axis=-1),
    )


def nn(left, right):
    return lax.dot_general(
        left, right, (((1,), (0,)), ((), ())), preferred_element_type=jnp.float32
    )


def nt(left, right):
    return lax.dot_general(
        left, right, (((1,), (1,)), ((), ())), preferred_element_type=jnp.float32
    )


def tn(left, right):
    return lax.dot_general(
        left, right, (((0,), (0,)), ((), ())), preferred_element_type=jnp.float32
    )


def arbitrary(axes, megabytes):
    return pltpu.CompilerParams(
        dimension_semantics=("arbitrary",) * axes, vmem_limit_bytes=megabytes << 20
    )


def cost(flops, moved, exps=0):
    return pl.CostEstimate(
        flops=int(flops * COST_SCALE),
        bytes_accessed=int(moved * COST_SCALE),
        transcendentals=int(exps * COST_SCALE),
    )


def fixed(shape):
    return pl.BlockSpec(shape, lambda *_: (0,) * len(shape))


def project_kernel(
    groups,
    kv_count,
    place_ref,
    first_ref,
    second_ref,
    gain_ref,
    weight_ref,
    cosine_ref,
    sine_ref,
    head_gain_ref,
    *refs,
):
    normed_ref, heads_ref, raw_ref = refs[-3:]
    size = HEAD_SIZE
    rows = jnp.where(place_ref[1] != 0, first_ref[...], second_ref[...]).astype(jnp.float32)
    scale = lax.rsqrt(jnp.mean(rows * rows, axis=-1, keepdims=True) + EPS)
    normed = (rows * scale * gain_ref[...]).astype(jnp.bfloat16)
    normed_ref[...] = normed
    raw = nn(normed, weight_ref[...])
    cosine, sine_table = cosine_ref[...], sine_ref[...]
    for h in range(kv_count):
        start = h * (groups + 2) * size
        for g in range(groups + 1):
            column = start + g * size
            value = raw[:, column : column + size]
            held = (h * (groups + 1) + g) * size
            raw_ref[:, held : held + size] = value
            which = 0 if g < groups else 1
            value = value * lax.rsqrt(jnp.mean(value * value, axis=-1, keepdims=True) + EPS)
            value = value * head_gain_ref[which : which + 1, :]
            value = value * cosine + pltpu.roll(value, size // 2, 1) * sine_table
            if g < groups:
                value = value * QUERY_SCALE
            heads_ref[:, column : column + size] = value.astype(jnp.bfloat16)
        column = start + (groups + 1) * size
        heads_ref[:, column : column + size] = raw[:, column : column + size].astype(jnp.bfloat16)


def project(
    place, first, second, gain, weight, cosine, sine_table, head_gains, groups, before, count
):
    rows, width = first.shape
    positions = count * rows
    columns = weight.shape[1]
    kv_count = columns // ((groups + 2) * HEAD_SIZE)
    held = kv_count * (groups + 1) * HEAD_SIZE
    block = min(256, rows)
    parts = rows // block
    same = lambda i, s: (0, 0)
    here = lambda i, s: (i, 0)
    there = lambda i, s: (s[0] * parts + i, 0)
    in_specs = [
        pl.BlockSpec((block, width), here),
        pl.BlockSpec((block, width), here),
        pl.BlockSpec((1, width), same),
        pl.BlockSpec((width, columns), same),
        pl.BlockSpec((block, HEAD_SIZE), there),
        pl.BlockSpec((block, HEAD_SIZE), there),
        pl.BlockSpec((2, HEAD_SIZE), same),
    ]
    args = [first, second, gain, weight, cosine, sine_table, head_gains]
    aliases = {}
    if before is not None:
        in_specs += [pl.BlockSpec(memory_space=pl.ANY)] * 3
        aliases = {len(args) + 1 + k: k for k in range(3)}
        args += list(before)
    return pl.pallas_call(
        functools.partial(project_kernel, groups, kv_count),
        grid_spec=pltpu.PrefetchScalarGridSpec(
            num_scalar_prefetch=1,
            grid=(parts,),
            in_specs=in_specs,
            out_specs=[
                pl.BlockSpec((block, width), there),
                pl.BlockSpec((block, columns), there),
                pl.BlockSpec((block, held), there),
            ],
        ),
        out_shape=(
            jax.ShapeDtypeStruct((positions, width), jnp.bfloat16),
            jax.ShapeDtypeStruct((positions, columns), jnp.bfloat16),
            jax.ShapeDtypeStruct((positions, held), jnp.float32),
        ),
        input_output_aliases=aliases,
        compiler_params=arbitrary(1, 40),
        cost_estimate=cost(2 * rows * width * columns, 2 * width * columns + 12 * rows * width),
        name="project",
    )(place, *args)


def forward_kernel(block, groups, place_ref, heads_ref, out_ref, total_ref, wide_ref):
    at_query = pl.program_id(1)
    length = place_ref[0]
    size = HEAD_SIZE
    key_lanes = slice(groups * size, (groups + 1) * size)

    @pl.when(at_query == 0)
    def _():
        wide_ref[:, :size] = heads_ref[:, (groups + 1) * size :]
        wide_ref[:, size:] = jnp.ones((wide_ref.shape[0], size), wide_ref.dtype)

    whole = jnp.minimum(at_query, length // block)
    some = jnp.minimum(at_query + 1, (length + block - 1) // block)
    here = pl.ds(pl.multiple_of(at_query * block, block), block)
    queries = [heads_ref[here, g * size : (g + 1) * size] for g in range(groups)]

    def step(at_key, sums, masked):
        start = pl.multiple_of(at_key * block, block)
        keys = heads_ref[pl.ds(start, block), key_lanes]
        wide = wide_ref[pl.ds(start, block), :]
        if masked:
            rows = at_query * block + lax.broadcasted_iota(jnp.int32, (block, block), 0)
            cols = start + lax.broadcasted_iota(jnp.int32, (block, block), 1)
            allowed = (cols <= rows) & (cols < length)
        after = []
        for g in range(groups):
            scores = nt(queries[g], keys)
            if masked:
                scores = jnp.where(allowed, scores, MASKED)
            after.append(sums[g] + nn(jnp.exp2(scores).astype(jnp.bfloat16), wide))
        return tuple(after)

    sums = tuple(jnp.zeros((block, 2 * size), jnp.float32) for _ in range(groups))
    sums = lax.fori_loop(0, whole, lambda j, c: step(j, c, False), sums)
    sums = lax.fori_loop(whole, some, lambda j, c: step(j, c, True), sums)
    for g in range(groups):
        total = sums[g][:, size:]
        out_ref[:, g * size : (g + 1) * size] = (sums[g][:, :size] / total).astype(out_ref.dtype)
        total_ref[g, :, :] = jnp.transpose(jnp.log2(total))[:8, :]


def attend_forward(place, heads, groups, count):
    positions = heads.shape[0]
    rows = positions // count
    block = min(512, rows)
    parts = rows // block
    group_width = (groups + 2) * HEAD_SIZE
    kv_count = heads.shape[1] // group_width
    size = HEAD_SIZE
    width = kv_count * groups * size
    return pl.pallas_call(
        functools.partial(forward_kernel, block, groups),
        grid_spec=pltpu.PrefetchScalarGridSpec(
            num_scalar_prefetch=1,
            grid=(kv_count, positions // block),
            in_specs=[pl.BlockSpec((positions, group_width), lambda h, i, s: (0, h))],
            out_specs=[
                pl.BlockSpec(
                    (None, block, groups * size),
                    lambda h, i, s: (
                        lax.rem(i // parts + count - s[1], count),
                        lax.rem(i, parts),
                        h,
                    ),
                ),
                pl.BlockSpec((groups, 8, block), lambda h, i, s: (h, 0, i)),
            ],
            scratch_shapes=[pltpu.VMEM((positions, 2 * size), jnp.bfloat16)],
        ),
        out_shape=(
            jax.ShapeDtypeStruct((count, rows, width), jnp.bfloat16),
            jax.ShapeDtypeStruct((kv_count * groups, 8, positions), jnp.float32),
        ),
        compiler_params=arbitrary(2, 48),
        cost_estimate=cost(
            4 * positions * positions * width,
            8 * positions * width,
            positions * positions * width // size // 2,
        ),
        name="attend_forward",
    )(place, heads)


def backward_kernel(
    block,
    groups,
    positions,
    count,
    place_ref,
    heads_ref,
    raw_ref,
    cosine_ref,
    sine_ref,
    head_gain_ref,
    out_ref,
    total_ref,
    *refs,
):
    piece_refs = refs[:count]
    grad_raw_ref, gain_ref, query_sums_ref, key_sums_ref, center_ref, grad_ref = refs[count:]
    length = place_ref[0]
    size = HEAD_SIZE
    rows_each = positions // count
    blocks = positions // block
    key_lanes = slice(groups * size, (groups + 1) * size)
    value_lanes = slice((groups + 1) * size, (groups + 2) * size)
    for k in range(count):
        place = lax.rem(place_ref[1] + k, count) * rows_each
        piece_ref = piece_refs[(count - k) % count]
        grad_ref[pl.ds(pl.multiple_of(place, rows_each), rows_each), :] = piece_ref[...]
        for g in range(groups):
            lanes = slice(g * size, (g + 1) * size)
            terms = piece_ref[:, lanes].astype(jnp.float32) * out_ref[k, :, lanes].astype(
                jnp.float32
            )
            center_ref[g, :, pl.ds(pl.multiple_of(place, rows_each), rows_each)] = (
                jnp.broadcast_to(
                    jnp.sum(jnp.transpose(terms), axis=0, keepdims=True), (8, rows_each)
                )
            )
    query_sums_ref[...] = jnp.zeros_like(query_sums_ref)
    whole = length // block
    some = (length + block - 1) // block

    def key_block(j, _):
        start = pl.multiple_of(j * block, block)
        keys = heads_ref[pl.ds(start, block), key_lanes]
        values = heads_ref[pl.ds(start, block), value_lanes]

        def step(i, carry, masked):
            grad_keys, grad_values = carry
            at = pl.multiple_of(i * block, block)
            if masked:
                key_at = start + lax.broadcasted_iota(jnp.int32, (block, block), 0)
                query_at = at + lax.broadcasted_iota(jnp.int32, (block, block), 1)
                allowed = (key_at <= query_at) & (key_at < length)
            for g in range(groups):
                queries = heads_ref[pl.ds(at, block), g * size : (g + 1) * size]
                grads = grad_ref[pl.ds(at, block), g * size : (g + 1) * size]
                scores = nt(keys, queries) - total_ref[g, 0:1, pl.ds(at, block)]
                if masked:
                    scores = jnp.where(allowed, scores, MASKED)
                probs = jnp.exp2(scores)
                grad_attend = nt(values, grads)
                grad_scores = (
                    probs * (grad_attend - center_ref[g, 0:1, pl.ds(at, block)])
                ).astype(jnp.bfloat16)
                grad_values = grad_values + nn(probs.astype(jnp.bfloat16), grads)
                grad_keys = grad_keys + nn(grad_scores, queries)
                query_sums_ref[g, pl.ds(at, block), :] += tn(grad_scores, keys)
            return grad_keys, grad_values

        zero = jnp.zeros((block, size), jnp.float32)
        first = jnp.where(j < whole, jnp.minimum(j + 1, blocks), blocks)
        carry = lax.fori_loop(j, first, lambda i, c: step(i, c, True), (zero, zero))
        grad_keys, grad_values = lax.fori_loop(
            first, blocks, lambda i, c: step(i, c, False), carry
        )
        key_sums_ref[pl.ds(start, block), :] = grad_keys
        grad_raw_ref[pl.ds(start, block), value_lanes] = grad_values.astype(grad_raw_ref.dtype)
        return 0

    lax.fori_loop(0, some, key_block, 0)

    def padding(j, _):
        start = pl.multiple_of(j * block, block)
        key_sums_ref[pl.ds(start, block), :] = jnp.zeros((block, size), jnp.float32)
        grad_raw_ref[pl.ds(start, block), value_lanes] = jnp.zeros(
            (block, size), grad_raw_ref.dtype
        )
        return 0

    lax.fori_loop(some, blocks, padding, 0)

    def head_back(i, carry):
        rows = pl.ds(pl.multiple_of(i * block, block), block)
        cosine, sine_table = cosine_ref[rows, :], sine_ref[rows, :]
        sums = list(carry)
        for g in range(groups + 1):
            lanes = slice(g * size, (g + 1) * size)
            if g < groups:
                grad = query_sums_ref[g, rows, :] * size**-0.5
            else:
                grad = key_sums_ref[rows, :] * (1.0 / math.log2(math.e))
            which = 0 if g < groups else 1
            grad = grad.astype(jnp.bfloat16).astype(jnp.float32)
            grad = grad * cosine - pltpu.roll(grad, size // 2, 1) * sine_table
            value = raw_ref[rows, lanes]
            scale = lax.rsqrt(jnp.mean(value * value, axis=-1, keepdims=True) + EPS)
            unit = value * scale
            sums[which] = sums[which] + jnp.sum(grad * unit, axis=0, keepdims=True)
            grad = grad * head_gain_ref[which : which + 1, :]
            inner = jnp.mean(grad * unit, axis=-1, keepdims=True)
            grad_raw_ref[rows, lanes] = (scale * (grad - unit * inner)).astype(grad_raw_ref.dtype)
        return tuple(sums)

    zero = jnp.zeros((1, size), jnp.float32)
    sums = lax.fori_loop(0, blocks, head_back, (zero, zero))
    gain_ref[0, 0:1, :] = sums[0]
    gain_ref[0, 1:2, :] = sums[1]


def attend_backward(
    place, heads, raw, cosine, sine_table, head_gains, groups, context, totals, pieces
):
    count = len(pieces)
    positions = heads.shape[0]
    rows = positions // count
    block = min(512, positions)
    size = HEAD_SIZE
    kv_count = heads.shape[1] // ((groups + 2) * size)

    def of_group(lines, columns):
        return pl.BlockSpec((lines, columns * size), lambda h, s: (0, h))

    width = kv_count * groups * size
    return pl.pallas_call(
        functools.partial(backward_kernel, block, groups, positions, count),
        grid_spec=pltpu.PrefetchScalarGridSpec(
            num_scalar_prefetch=1,
            grid=(kv_count,),
            in_specs=[
                of_group(positions, groups + 2),
                of_group(positions, groups + 1),
                fixed(cosine.shape),
                fixed(sine_table.shape),
                fixed(head_gains.shape),
                pl.BlockSpec((count, rows, groups * size), lambda h, s: (0, 0, h)),
                pl.BlockSpec((groups, 8, positions), lambda h, s: (h, 0, 0)),
            ]
            + [of_group(rows, groups)] * count,
            out_specs=[
                of_group(positions, groups + 2),
                pl.BlockSpec((1, 2, size), lambda h, s: (h, 0, 0)),
            ],
            scratch_shapes=[
                pltpu.VMEM((groups, positions, size), jnp.float32),
                pltpu.VMEM((positions, size), jnp.float32),
                pltpu.VMEM((groups, 8, positions), jnp.float32),
                pltpu.VMEM((positions, groups * size), jnp.bfloat16),
            ],
        ),
        out_shape=(
            jax.ShapeDtypeStruct(heads.shape, jnp.bfloat16),
            jax.ShapeDtypeStruct((kv_count, 2, size), jnp.float32),
        ),
        compiler_params=arbitrary(1, 56),
        cost_estimate=cost(
            positions * positions * width,
            2 * positions * width,
            positions * positions * width // size // 20,
        ),
        name="attend_backward",
    )(
        place,
        heads,
        raw,
        cosine,
        sine_table,
        head_gains,
        context,
        totals,
        *pieces,
    )


def tile_of(hidden_units):
    return next(t for t in (512, 384, 256, 128) if hidden_units % t == 0)


def separate(both, tile):
    pieces = [both[:, at : at + tile] for at in range(0, both.shape[1], tile)]
    return jnp.concatenate(pieces[0::2], axis=1), jnp.concatenate(pieces[1::2], axis=1)


def out_norm_kernel(count, weight_ref, rows_ref, gain_ref, *refs):
    resid_ref, normed_ref = refs[count:]
    part = refs[0].shape[-1]
    resid = rows_ref[...].astype(jnp.float32)
    for k in range(count):
        at = (count - k) % count * part
        resid = resid + nn(refs[k][...], weight_ref[at : at + part, :])
    resid_ref[...] = resid
    normed_ref[...] = norm_rows(resid, gain_ref[...]).astype(normed_ref.dtype)


def out_norm(pieces, weight, tokens, gain):
    count = len(pieces)
    rows, part = pieces[0].shape
    width = weight.shape[1]
    block = min(256, rows)
    across = pl.BlockSpec((block, width), lambda i: (i, 0))
    return pl.pallas_call(
        functools.partial(out_norm_kernel, count),
        grid=(rows // block,),
        in_specs=[fixed(weight.shape), across, fixed(gain.shape)]
        + [pl.BlockSpec((block, part), lambda i: (i, 0))] * count,
        out_specs=[across, across],
        out_shape=(
            jax.ShapeDtypeStruct((rows, width), jnp.float32),
            jax.ShapeDtypeStruct((rows, width), jnp.bfloat16),
        ),
        compiler_params=arbitrary(1, 48),
        cost_estimate=cost(2 * rows * count * part * width, 2 * weight.size + 10 * rows * width),
        name="out_norm",
    )(weight, tokens, gain, *pieces)


def hidden_kernel(tile, own_ref, away_ref, weight_ref, *refs):
    both_ref, hidden_ref = refs[-2:]
    rows = own_ref.shape[0]
    for half, rows_ref in enumerate((own_ref, away_ref)):
        here = slice(half * rows, (half + 1) * rows)
        both = nn(rows_ref[...], weight_ref[...])
        both_ref[here, :] = both.astype(both_ref.dtype)
        gate, up = both[:, :tile], both[:, tile:]
        hidden_ref[here, :] = (gate * jax.nn.sigmoid(gate) * up).astype(hidden_ref.dtype)


def hidden_units(own, away, weight, tile, at, total, before):
    rows, width = own.shape
    columns = weight.shape[1]
    tiles = columns // (2 * tile)
    in_specs = [
        fixed(own.shape),
        fixed(away.shape),
        pl.BlockSpec((width, 2 * tile), lambda j: (0, j)),
    ]
    args, aliases = [own, away, weight], {}
    if before is not None:
        in_specs.append(pl.BlockSpec(memory_space=pl.ANY))
        args.append(before)
        aliases = {3: 1}
    return pl.pallas_call(
        functools.partial(hidden_kernel, tile),
        grid=(tiles,),
        in_specs=in_specs,
        out_specs=[
            pl.BlockSpec((2 * rows, 2 * tile), lambda j: (0, j)),
            pl.BlockSpec((2 * rows, tile), lambda j: (0, at * tiles + j)),
        ],
        out_shape=(
            jax.ShapeDtypeStruct((2 * rows, columns), jnp.bfloat16),
            jax.ShapeDtypeStruct((2 * rows, total), jnp.bfloat16),
        ),
        input_output_aliases=aliases,
        compiler_params=arbitrary(1, 56),
        cost_estimate=cost(4 * rows * width * columns, 2 * width * columns + 10 * rows * columns),
        name="hidden_units",
    )(*args)


def hidden_back_kernel(tile, own_ref, away_ref, down_ref, both_ref, out_ref):
    rows = own_ref.shape[0]
    for half, grads_ref in enumerate((own_ref, away_ref)):
        here = slice(half * rows, (half + 1) * rows)
        grad_hidden = nt(grads_ref[...], down_ref[...])
        gate = both_ref[here, :tile].astype(jnp.float32)
        up = both_ref[here, tile:].astype(jnp.float32)
        sigmoid = jax.nn.sigmoid(gate)
        silu = gate * sigmoid
        out_ref[here, :tile] = (grad_hidden * up * (sigmoid + silu * (1.0 - sigmoid))).astype(
            out_ref.dtype
        )
        out_ref[here, tile:] = (grad_hidden * silu).astype(out_ref.dtype)


def hidden_back(own, away, down, both, tile):
    rows, width = own.shape
    columns = both.shape[1]
    pair = pl.BlockSpec((2 * rows, 2 * tile), lambda j: (0, j))
    return pl.pallas_call(
        functools.partial(hidden_back_kernel, tile),
        grid=(columns // (2 * tile),),
        in_specs=[
            fixed(own.shape),
            fixed(away.shape),
            pl.BlockSpec((tile, width), lambda j: (j, 0)),
            pair,
        ],
        out_specs=pair,
        out_shape=jax.ShapeDtypeStruct((2 * rows, columns), jnp.bfloat16),
        compiler_params=arbitrary(1, 56),
        cost_estimate=cost(2 * rows * width * columns, width * columns + 12 * rows * columns),
        name="hidden_back",
    )(own, away, down, both)


def unit_grads_kernel(own_ref, away_ref, grads_ref, out_ref):
    rows = own_ref.shape[0]
    out_ref[...] = (
        tn(own_ref[...], grads_ref[:rows, :]) + tn(away_ref[...], grads_ref[rows:, :])
    ).astype(out_ref.dtype)


def unit_grads(own, away, grads):
    rows, width = own.shape
    columns = grads.shape[1]
    tile = tile_of(columns)
    return pl.pallas_call(
        unit_grads_kernel,
        grid=(columns // tile,),
        in_specs=[
            fixed(own.shape),
            fixed(away.shape),
            pl.BlockSpec((2 * rows, tile), lambda j: (0, j)),
        ],
        out_specs=pl.BlockSpec((width, tile), lambda j: (0, j)),
        out_shape=jax.ShapeDtypeStruct((width, columns), jnp.bfloat16),
        compiler_params=arbitrary(1, 56),
        cost_estimate=cost(4 * rows * width * columns, 2 * width * columns + 4 * rows * columns),
        name="unit_grads",
    )(own, away, grads)


def down_grads_kernel(hidden_ref, own_ref, away_ref, out_ref):
    rows = own_ref.shape[0]
    out_ref[...] = (
        tn(hidden_ref[:rows, :], own_ref[...]) + tn(hidden_ref[rows:, :], away_ref[...])
    ).astype(out_ref.dtype)


def down_grads(hidden, own, away):
    rows, width = own.shape
    units = hidden.shape[1]
    tile = tile_of(units)
    return pl.pallas_call(
        down_grads_kernel,
        grid=(units // tile,),
        in_specs=[
            pl.BlockSpec((2 * rows, tile), lambda j: (0, j)),
            fixed(own.shape),
            fixed(away.shape),
        ],
        out_specs=pl.BlockSpec((tile, width), lambda j: (j, 0)),
        out_shape=jax.ShapeDtypeStruct((units, width), jnp.bfloat16),
        compiler_params=arbitrary(1, 56),
        cost_estimate=cost(4 * rows * width * units, 2 * width * units + 4 * rows * units),
        name="down_grads",
    )(hidden, own, away)


def grad_normed_kernel(parts, *refs):
    grads, weights = refs[:parts], refs[parts : 2 * parts]
    own_ref, away_ref = refs[2 * parts :]
    rows = own_ref.shape[0]
    for half, out_ref in enumerate((own_ref, away_ref)):
        here = slice(half * rows, (half + 1) * rows)
        total = nt(grads[0][here, :], weights[0][...])
        for grad_ref, weight_ref in zip(grads[1:], weights[1:]):
            total = total + nt(grad_ref[here, :], weight_ref[...])
        out_ref[...] = total.astype(out_ref.dtype)


def grad_normed(grads, weights):
    rows = grads[0].shape[0] // 2
    width = weights[0].shape[0]
    tile = tile_of(width)
    return pl.pallas_call(
        functools.partial(grad_normed_kernel, len(grads)),
        grid=(width // tile,),
        in_specs=[fixed(grad.shape) for grad in grads]
        + [pl.BlockSpec((tile, weight.shape[1]), lambda j: (j, 0)) for weight in weights],
        out_specs=[pl.BlockSpec((rows, tile), lambda j: (0, j))] * 2,
        out_shape=(
            jax.ShapeDtypeStruct((rows, width), jnp.float32),
            jax.ShapeDtypeStruct((rows, width), jnp.bfloat16),
        ),
        compiler_params=arbitrary(1, 60),
        cost_estimate=cost(
            sum(2 * grad.size * width for grad in grads),
            sum(2 * grad.size + 2 * weight.size for grad, weight in zip(grads, weights)),
        ),
        name="grad_normed",
    )(*grads, *weights)


def mlp_out_kernel(hidden_ref, *refs):
    own_ref, away_ref = refs[-2:]
    rows = own_ref.shape[0]
    for half, out_ref in enumerate((own_ref, away_ref)):
        here = slice(half * rows, (half + 1) * rows)
        at, total = 0, None
        for down_ref in refs[:-2]:
            units = down_ref.shape[0]
            part = nn(hidden_ref[here, at : at + units], down_ref[...])
            total = part if total is None else total + part
            at += units
        out_ref[...] = total.astype(out_ref.dtype)


def mlp_out(hidden, downs):
    rows = hidden.shape[0] // 2
    width = downs[0].shape[1]
    tile = tile_of(width)
    return pl.pallas_call(
        mlp_out_kernel,
        grid=(width // tile,),
        in_specs=[fixed(hidden.shape)]
        + [pl.BlockSpec((down.shape[0], tile), lambda j: (0, j)) for down in downs],
        out_specs=[pl.BlockSpec((rows, tile), lambda j: (0, j))] * 2,
        out_shape=(
            jax.ShapeDtypeStruct((rows, width), jnp.float32),
            jax.ShapeDtypeStruct((rows, width), jnp.bfloat16),
        ),
        compiler_params=arbitrary(1, 56),
        cost_estimate=cost(2 * hidden.size * width, 4 * hidden.size + 6 * rows * width),
        name="mlp_out",
    )(hidden, *downs)


def resid_back_kernel(
    place_ref,
    own_ref,
    away_ref,
    resid_ref,
    cotangent_ref,
    gain_ref,
    weight_ref,
    grad_ref,
    low_ref,
    sums_ref,
    *piece_refs,
):
    block = own_ref.shape[0]
    part = piece_refs[0].shape[-1]
    first = place_ref[1] + pl.program_id(0) * block
    at = first + lax.broadcasted_iota(jnp.int32, (block, 1), 0)
    valid = (at < place_ref[0]).astype(jnp.float32)
    grads = own_ref[...] + away_ref[...].astype(jnp.float32)
    back, sums = norm_back(resid_ref[...], gain_ref[...], grads)
    grad_resid = valid * cotangent_ref[...].astype(jnp.float32) + back
    grad_ref[...] = grad_resid
    low = grad_resid.astype(jnp.bfloat16)
    low_ref[...] = low
    for k, piece_ref in enumerate(piece_refs):
        piece_ref[...] = nt(low, weight_ref[k * part : (k + 1) * part, :]).astype(piece_ref.dtype)

    @pl.when(pl.program_id(0) == 0)
    def _():
        sums_ref[...] = jnp.zeros_like(sums_ref)

    sums_ref[...] += sums


def resid_back(own, away, resid, cotangent, gain, weight, length, start, count):
    rows, width = own.shape
    part = weight.shape[0] // count
    block = min(256, rows)
    across = pl.BlockSpec((block, width), lambda i, s: (i, 0))
    return pl.pallas_call(
        resid_back_kernel,
        grid_spec=pltpu.PrefetchScalarGridSpec(
            num_scalar_prefetch=1,
            grid=(rows // block,),
            in_specs=[across] * 4 + [fixed(gain.shape), fixed(weight.shape)],
            out_specs=[across, across, fixed(gain.shape)]
            + [pl.BlockSpec((block, part), lambda i, s: (i, 0))] * count,
        ),
        out_shape=(
            jax.ShapeDtypeStruct((rows, width), jnp.float32),
            jax.ShapeDtypeStruct((rows, width), jnp.bfloat16),
            jax.ShapeDtypeStruct(gain.shape, jnp.float32),
        )
        + (jax.ShapeDtypeStruct((rows, part), jnp.bfloat16),) * count,
        compiler_params=arbitrary(1, 56),
        cost_estimate=cost(2 * rows * weight.size, 2 * weight.size + 20 * rows * width),
        name="resid_back",
    )(jnp.stack([length, start]), own, away, resid, cotangent, gain, weight)


def out_grads_kernel(count, grads_ref, *refs):
    out_ref = refs[count]
    part = refs[0].shape[-1]
    for k in range(count):
        at = (count - k) % count * part
        out_ref[at : at + part, :] = tn(refs[k][...], grads_ref[...]).astype(out_ref.dtype)


def out_grads(pieces, grads):
    count = len(pieces)
    rows, part = pieces[0].shape
    width = grads.shape[1]
    tile = tile_of(width)
    return pl.pallas_call(
        functools.partial(out_grads_kernel, count),
        grid=(width // tile,),
        in_specs=[pl.BlockSpec((rows, tile), lambda j: (0, j))]
        + [fixed(piece.shape) for piece in pieces],
        out_specs=pl.BlockSpec((count * part, tile), lambda j: (0, j)),
        out_shape=jax.ShapeDtypeStruct((count * part, width), jnp.bfloat16),
        compiler_params=arbitrary(1, 48),
        cost_estimate=cost(
            2 * rows * count * part * width, 2 * count * part * (rows + width) + 2 * rows * width
        ),
        name="out_grads",
    )(grads, *pieces)


def pack_heads_kernel(groups, query_ref, key_ref, value_ref, gain_ref, out_ref):
    size = HEAD_SIZE
    at = 0
    for h in range(key_ref.shape[1] // size):
        for ref, start, columns in (
            (query_ref, h * groups * size, groups * size),
            (key_ref, h * size, size),
            (value_ref, h * size, size),
        ):
            out_ref[:, at : at + columns] = ref[:, start : start + columns]
            at += columns
    out_ref[:, at:] = gain_ref[...]


def pack_heads(query, key, value, gain, groups):
    rows = query.shape[0]
    columns = query.shape[1] + key.shape[1] + value.shape[1] + gain.shape[1]
    args = (query, key, value, gain)
    return pl.pallas_call(
        functools.partial(pack_heads_kernel, groups),
        grid=(1,),
        in_specs=[fixed(arg.shape) for arg in args],
        out_specs=fixed((rows, columns)),
        out_shape=jax.ShapeDtypeStruct((rows, columns), jnp.bfloat16),
        compiler_params=arbitrary(1, 16),
        cost_estimate=cost(0, 4 * rows * columns),
        name="pack_heads",
    )(*args)


def pack_units_kernel(tile, gate_ref, up_ref, out_ref):
    for at in range(0, gate_ref.shape[1], tile):
        out_ref[:, 2 * at : 2 * at + tile] = gate_ref[:, at : at + tile]
        out_ref[:, 2 * at + tile : 2 * at + 2 * tile] = up_ref[:, at : at + tile]


def pack_units(gate, up, tile):
    rows, columns = gate.shape
    return pl.pallas_call(
        functools.partial(pack_units_kernel, tile),
        grid=(1,),
        in_specs=[fixed(gate.shape), fixed(up.shape)],
        out_specs=fixed((rows, 2 * columns)),
        out_shape=jax.ShapeDtypeStruct((rows, 2 * columns), jnp.bfloat16),
        compiler_params=arbitrary(1, 16),
        cost_estimate=cost(0, 8 * rows * columns),
        name="pack_units",
    )(gate, up)


def tokens_back_kernel(
    own_ref, right_ref, left_ref, rows_ref, gain_ref, resid_ref, out_ref, beside_ref
):
    width = rows_ref.shape[1]
    total = (
        own_ref[...] + right_ref[...].astype(jnp.float32) + left_ref[...].astype(jnp.float32)
    )
    back = norm_back(rows_ref[...].astype(jnp.float32), gain_ref[...], total[:, :width])[0]
    out_ref[...] = (resid_ref[...] + back).astype(out_ref.dtype)
    beside_ref[...] = total[:, width:]


def tokens_back(parts, tokens, gain, grad_resid):
    rows, width = tokens.shape
    more = parts[0].shape[1] - width
    block = min(256, rows)
    across = pl.BlockSpec((block, width), lambda i: (i, 0))
    both = pl.BlockSpec((block, width + more), lambda i: (i, 0))
    return pl.pallas_call(
        tokens_back_kernel,
        grid=(rows // block,),
        in_specs=[both] * 3 + [across, fixed(gain.shape), across],
        out_specs=[across, pl.BlockSpec((block, more), lambda i: (i, 0))],
        out_shape=(
            jax.ShapeDtypeStruct((rows, width), jnp.bfloat16),
            jax.ShapeDtypeStruct((rows, more), jnp.float32),
        ),
        compiler_params=arbitrary(1, 40),
        cost_estimate=cost(20 * rows * width, 16 * rows * width),
        name="tokens_back",
    )(*parts, tokens, gain, grad_resid)


def share_kernel(slot_ref, grads_ref, weight_ref, beside_ref, out_ref):
    width = weight_ref.shape[0]
    out_ref[:, :width] = nt(grads_ref[...], weight_ref[...]).astype(out_ref.dtype)
    out_ref[:, width:] = beside_ref[...].astype(out_ref.dtype)


def share(slot, grads, weight, beside, k, count, dtype):
    positions, columns = grads.shape
    rows = positions // count
    width, more = weight.shape[0], beside.shape[1]
    block = min(256, rows)
    parts = rows // block
    return pl.pallas_call(
        share_kernel,
        grid_spec=pltpu.PrefetchScalarGridSpec(
            num_scalar_prefetch=1,
            grid=(parts,),
            in_specs=[
                pl.BlockSpec((block, columns), lambda i, s: (s[0] * parts + i, 0)),
                fixed(weight.shape),
                pl.BlockSpec((block, more), lambda i, s: (k * parts + i, 0)),
            ],
            out_specs=pl.BlockSpec((block, width + more), lambda i, s: (i, 0)),
        ),
        out_shape=jax.ShapeDtypeStruct((rows, width + more), dtype),
        compiler_params=arbitrary(1, 40),
        cost_estimate=cost(2 * rows * columns * width, 2 * width * columns),
        name="share",
    )(slot, grads, weight, beside)


def heads_back_kernel(normed_ref, grad_ref, weight_ref, out_ref, sums_ref):
    partial = tn(normed_ref[...], grad_ref[...])
    out_ref[...] = partial.astype(out_ref.dtype)
    sums = jnp.sum(partial * weight_ref[...].astype(jnp.float32), axis=1, keepdims=True)
    sums_ref[...] = jnp.broadcast_to(sums, sums_ref.shape)


def heads_back(normed, grads, weight):
    positions, width = normed.shape
    columns = grads.shape[1]
    block = min(512, width)
    return pl.pallas_call(
        heads_back_kernel,
        grid=(width // block,),
        in_specs=[
            pl.BlockSpec((positions, block), lambda j: (0, j)),
            pl.BlockSpec((positions, columns), lambda j: (0, 0)),
            pl.BlockSpec((block, columns), lambda j: (j, 0)),
        ],
        out_specs=[
            pl.BlockSpec((block, columns), lambda j: (j, 0)),
            pl.BlockSpec((block, LANES), lambda j: (j, 0)),
        ],
        out_shape=(
            jax.ShapeDtypeStruct((width, columns), jnp.bfloat16),
            jax.ShapeDtypeStruct((width, LANES), jnp.float32),
        ),
        compiler_params=arbitrary(1, 48),
        cost_estimate=cost(
            2 * positions * width * columns, 2 * positions * (width + columns) + 4 * width * columns
        ),
        name="heads_back",
    )(normed, grads, weight)


def norm_back(value_rows, gain, grads):
    scale = lax.rsqrt(jnp.mean(value_rows * value_rows, axis=-1, keepdims=True) + EPS)
    unit = value_rows * scale
    scaled = grads * gain
    inner = jnp.mean(scaled * unit, axis=-1, keepdims=True)
    return scale * (scaled - unit * inner), jnp.sum(grads * unit, axis=0)


def after(value, *others):
    return lax.optimization_barrier((value, others))[0]


def hop_right(value, count, hop):
    return lax.ppermute(value, "seq", [(i, i + 1) for i in range(hop - 1, count - 1)])


def hop_left(value, count, hop):
    return lax.ppermute(value, "seq", [(i, i - 1) for i in range(1, count - hop + 1)])


def line_scatter(parts, before):
    count = len(parts)
    right, left = None, None
    hops = []
    for hop in range(count - 1):
        to_right, to_left = parts[count - 1 - hop], parts[hop + 1]
        if hop:
            to_right = to_right.astype(jnp.float32) + right.astype(jnp.float32)
            to_left = to_left.astype(jnp.float32) + left.astype(jnp.float32)
        if hop in before:
            to_right, to_left = after((to_right, to_left), *before[hop])
        right = lax.ppermute(
            to_right.astype(jnp.bfloat16), "seq", [(i, i + 1) for i in range(hop + 1)]
        )
        left = lax.ppermute(
            to_left.astype(jnp.bfloat16),
            "seq",
            [(i, i - 1) for i in range(count - 1 - hop, count)],
        )
        hops.append((right, left))
    return (parts[0], right, left), hops


def sum_over(value, axis):
    flat = value.reshape(-1, LANES)
    size = lax.axis_size(axis)
    assert size & (size - 1) == 0
    step = 1
    while step < size:
        flat = flat + lax.ppermute(flat, axis, [(i, i ^ step) for i in range(size)])
        step *= 2
    return flat.reshape(-1)


def swap(value, count):
    return lax.ppermute(value, "seq", [(i, i ^ 1) for i in range(count)])


def fetch(value, count, step):
    return lax.ppermute(value, "seq", [((i + step) % count, i) for i in range(count)])


def give(value, count, step):
    return lax.ppermute(value, "seq", [(i, (i + step) % count) for i in range(count)])


def on_device(
    tokens,
    lengths,
    cotangent,
    w_query,
    key_weight,
    value_weight,
    w_out,
    w_gate,
    w_up,
    w_down,
    norm_attn,
    norm_mlp,
    norm_query,
    norm_key,
):
    slots, rows, width = tokens.shape
    assert slots == 1
    count = lax.axis_size("seq")
    positions = count * rows
    me = lax.axis_index("seq")
    tokens_low = tokens.reshape(rows, width)
    cotangent_low = cotangent.reshape(rows, width)
    length = lengths[0]
    low = jnp.bfloat16
    groups = w_query.shape[1] // key_weight.shape[1]
    kv_count = key_weight.shape[1] // HEAD_SIZE
    units = w_gate.shape[1]
    tile = tile_of(units)
    steps = range(0, count, PAIR)

    def from_groups(both):
        size = HEAD_SIZE
        starts = [h * (groups + 2) * size for h in range(kv_count)]
        ends = (0, groups * size, (groups + 1) * size, (groups + 2) * size)
        return [
            jnp.concatenate([both[:, s + low_end : s + high_end] for s in starts], axis=1)
            for low_end, high_end in zip(ends, ends[1:])
        ]

    weight_rows = w_query.shape[0]
    gain_parts = (norm_attn, norm_mlp, norm_query, norm_key)
    gain_sizes = [part.shape[0] for part in gain_parts]
    own_gains = jnp.concatenate(gain_parts)
    gain_block = jnp.pad(own_gains, (0, weight_rows * LANES - own_gains.shape[0])).reshape(
        weight_rows, LANES
    )
    own_heads = pack_heads(w_query, key_weight, value_weight, gain_block, groups)
    head_columns = own_heads.shape[1] - LANES
    gathered_heads = lax.all_gather(own_heads, "dp", axis=0, tiled=True)
    heads_weight = gathered_heads[:, :head_columns]
    gathered_gains = gathered_heads[:, head_columns:].reshape(-1, weight_rows * LANES)
    rights = [hop_right(tokens_low, count, 1)]
    lefts = [hop_left(tokens_low, count, 1)]
    gains, at = [], 0
    for part_size in gain_sizes:
        gains.append(gathered_gains[:, at : at + part_size].reshape(1, -1).astype(jnp.float32))
        at += part_size
    gain_attn, gain_mlp = gains[:2]
    head_gains = jnp.concatenate(gains[2:], axis=0)
    cosine, sine_table = angles(jnp.arange(positions, dtype=jnp.float32))

    places = [
        jnp.stack([lax.rem(me + k, count), (me + k < count).astype(jnp.int32)])
        for k in range(count)
    ]
    slot_place = jnp.stack([length, me])

    def project_block(k, whole):
        first, second = tokens_low, tokens_low
        if k:
            first, second = lefts[k - 1], rights[count - k - 1]
        return project(
            places[k],
            first,
            second,
            gain_attn,
            heads_weight,
            cosine,
            sine_table,
            head_gains,
            groups,
            whole,
            count,
        )

    own_both = pack_units(w_gate, w_up, tile)
    first_hop = (rights[0], lefts[0])
    both_weights = [lax.all_gather(after(own_both, *first_hop), "dp", axis=0, tiled=True)]
    down_weights = [lax.all_gather(after(w_down, *first_hop), "dp", axis=1, tiled=True)]
    whole = project_block(0, None)
    for hop in range(2, count - 1):
        rights.append(hop_right(rights[-1], count, hop))
        lefts.append(hop_left(lefts[-1], count, hop))
    right, left = after((rights[-1], lefts[-1]), whole[1])
    before_last = (rights[-1], lefts[-1])
    fetched_down = [fetch(after(w_down, *before_last), count, step) for step in steps[1:]]
    rights.append(hop_right(right, count, count - 1))
    lefts.append(hop_left(left, count, count - 1))
    for k in range(2, count - 1):
        whole = project_block(k, whole)
    out_blocks = [w_out] + [
        fetch(after(w_out, *before_last, whole[1]), count, k) for k in range(1, count)
    ]
    gathered = (rights[-1], lefts[-1])
    out_weight = lax.all_gather(
        after(
            jnp.concatenate(out_blocks, axis=0),
            both_weights[0],
            down_weights[0],
            *gathered,
            *fetched_down,
        ),
        "dp",
        axis=1,
        tiled=True,
    )

    fetched_both = [
        fetch(after(own_both, *gathered), count, step) for step in steps[1:]
    ]
    for k in [1, count - 1] if count > 2 else [1]:
        whole = project_block(k, whole)
    normed_attn, heads, raw = whole
    context, totals = attend_forward(slot_place, heads, groups, count)
    sent = context
    context_pieces = [context[0]] + [give(sent[k], count, k) for k in range(1, count)]
    resid, normed_mlp = out_norm(context_pieces, out_weight, tokens_low, gain_mlp)
    away_normed = swap(normed_mlp, count)
    for both, down in zip(fetched_both, fetched_down):
        both_weights.append(lax.all_gather(after(both, context), "dp", axis=0, tiled=True))
        down_weights.append(lax.all_gather(after(down, heads), "dp", axis=1, tiled=True))

    place = jnp.arange(rows, dtype=jnp.int32)[:, None] + me * rows
    valid_rows = (place < length).astype(low)
    grad_rows = cotangent_low * valid_rows
    away_grads = swap(after(grad_rows, away_normed), count)
    hidden, boths = None, []
    for at, weight in enumerate(both_weights):
        both, hidden = hidden_units(
            normed_mlp, away_normed, weight, tile, at, len(steps) * units, hidden
        )
        boths.append(both)

    def spread(partial, axis):
        return lax.psum_scatter(partial, "dp", scatter_dimension=axis, tiled=True)

    down_partial = down_grads(hidden, grad_rows, away_grads)
    grad_rows, away_grads = after((grad_rows, away_grads), down_partial)
    down_sums = spread(down_partial, 1)
    grad_boths = [
        hidden_back(grad_rows, away_grads, down, both, tile)
        for down, both in zip(down_weights, boths)
    ]
    mate_partials = [unit_grads(normed_mlp, away_normed, grad) for grad in grad_boths[1:]]
    mate_sums = [spread(partial, 0) for partial in mate_partials]
    grad_normed_own, grad_normed_away = grad_normed(
        after(grad_boths, *mate_partials), both_weights
    )
    own_partial = unit_grads(normed_mlp, away_normed, after(grad_boths[0], grad_normed_away))
    mlp_own, mlp_away = mlp_out(after(hidden, own_partial), down_weights)
    grad_resid, grad_attn_low, gain_mlp_sums, *pieces = resid_back(
        grad_normed_own,
        after(swap(grad_normed_away, count), own_partial, mlp_own, down_sums),
        resid,
        cotangent_low,
        gain_mlp,
        out_weight,
        length,
        me * rows,
        count,
    )
    pieces = [pieces[0]] + [give(pieces[k], count, k) for k in range(1, count)]
    out_partial = out_grads(context_pieces, grad_attn_low)
    out_sums = spread(out_partial, 1)
    own_sum = spread(after(own_partial, *pieces, out_partial), 0)
    pieces = after(pieces, out_partial, down_sums, *mate_sums)
    grad_raw, head_gain_terms = attend_backward(
        slot_place,
        heads,
        raw,
        cosine,
        sine_table,
        head_gains,
        groups,
        context,
        totals,
        pieces,
    )
    away_both, away_down, mlp_away = after((mate_sums, down_sums, mlp_away), *pieces)
    mlp_away = swap(mlp_away, count)
    given_first, given_second = [
        [give(half, count, step) for step, half in zip(steps[1:], halves)]
        for halves in zip(*(jnp.split(piece, 2, axis=0) for piece in away_both))
    ]
    down_pieces = jnp.split(away_down, len(steps), axis=0)
    given_down = [give(piece, count, step) for step, piece in zip(steps[1:], down_pieces[1:])]
    shares = {}
    for k in [count - 1, 1, *range(2, count - 1), 0]:
        shares[k] = share(
            places[k][:1],
            grad_raw,
            heads_weight,
            out_sums,
            k,
            count,
            low if k else jnp.float32,
        )
    shares[1], shares[count - 1] = after(
        (shares[1], shares[count - 1]), *given_down, *given_first, mlp_away
    )
    shares = [shares[k] for k in range(count)]
    heads_partial, gain_attn_sums = heads_back(
        normed_attn, after(grad_raw, shares[1], shares[-1]), heads_weight
    )
    grad_heads = spread(heads_partial, 0)
    gain_attn_term = gain_attn_sums[:, 0] / gain_attn[0]
    head_gain_sums = jnp.sum(head_gain_terms, axis=0)
    terms = (gain_attn_term, gain_mlp_sums[0], head_gain_sums[0], head_gain_sums[1])
    gain_sums = sum_over(jnp.concatenate(terms), "dp").reshape(-1, LANES)
    gain_parts = [gain_sums] + [give(gain_sums, count, k) for k in range(1, count)]
    last_parts, hops = line_scatter(
        shares,
        {1: (heads_partial, shares[0], *gain_parts[1:], *given_second), 2: (own_sum,)},
    )
    grad_heads = grad_heads.astype(jnp.float32)
    grad_query, grad_key, grad_value = from_groups(grad_heads)
    layer_output = (
        (valid_rows.astype(jnp.float32) * (resid + mlp_own + mlp_away.astype(jnp.float32)))
        .astype(low)
        .reshape(slots, rows, width)
    )
    grad_tokens, grad_out = tokens_back(last_parts, tokens_low, gain_attn, grad_resid)
    grad_tokens = grad_tokens.reshape(slots, rows, width)

    sums = sum(gain_parts).reshape(-1)
    both_total = own_sum.astype(jnp.float32) + sum(
        jnp.concatenate(halves, axis=0).astype(jnp.float32)
        for halves in zip(given_first, given_second)
    )
    grad_gate, grad_up = separate(both_total, tile)
    grad_down = sum([part.astype(jnp.float32) for part in [down_pieces[0], *given_down]])

    gain_grads, at = [], 0
    for term, part_size in zip(terms, gain_sizes):
        gain_grads.append(
            lax.dynamic_slice_in_dim(
                sums[at : at + term.shape[0]], lax.axis_index("dp") * part_size, part_size, 0
            )
        )
        at += term.shape[0]
    return (
        layer_output,
        grad_tokens,
        grad_query,
        grad_key,
        grad_value,
        grad_out,
        grad_gate,
        grad_up,
        grad_down,
        *gain_grads,
    )


def solution(mesh):
    return jax.shard_map(
        on_device,
        mesh=mesh,
        in_specs=(
            P("dp", "seq", None),
            P("dp"),
            P("dp", "seq", None),
            P("dp", "seq"),
            P("dp", "seq"),
            P("dp", "seq"),
            P("seq", "dp"),
            P("dp", "seq"),
            P("dp", "seq"),
            P("seq", "dp"),
            P("dp"),
            P("dp"),
            P("dp"),
            P("dp"),
        ),
        out_specs=(
            P("dp", "seq", None),
            P("dp", "seq", None),
            P("dp", "seq"),
            P("dp", "seq"),
            P("dp", "seq"),
            P("seq", "dp"),
            P("dp", "seq"),
            P("dp", "seq"),
            P("seq", "dp"),
            P("dp"),
            P("dp"),
            P("dp"),
            P("dp"),
        ),
        check_vma=False,
    )
```

```python
import functools
import math

import jax
import jax.numpy as jnp
from jax import lax
from jax.experimental import pallas as pl
from jax.experimental.pallas import tpu as pltpu
from jax.sharding import PartitionSpec as P

HEAD_SIZE = 128
EPS = 1e-06
BASE = 1000000.0
MASKED = -1e30
QUERY_SCALE = HEAD_SIZE**-0.5 * math.log2(math.e)
PAIR = 2
LANES = 128
COST_SCALE = 0.05


def norm_rows(value_rows, gain):
    return (
        value_rows
        * lax.rsqrt(jnp.mean(value_rows * value_rows, axis=-1, keepdims=True) + EPS)
        * gain
    )


def angles(positions):
    frequency = BASE ** (-(jnp.arange(HEAD_SIZE // 2, dtype=jnp.float32) * 2.0 / HEAD_SIZE))
    phases = positions[:, None] * frequency[None, :]
    cosine, sine_table = jnp.cos(phases), jnp.sin(phases)
    return (
        jnp.concatenate([cosine, cosine], axis=-1),
        jnp.concatenate([-sine_table, sine_table], axis=-1),
    )


def nn(left, right):
    return lax.dot_general(
        left, right, (((1,), (0,)), ((), ())), preferred_element_type=jnp.float32
    )


def nt(left, right):
    return lax.dot_general(
        left, right, (((1,), (1,)), ((), ())), preferred_element_type=jnp.float32
    )


def tn(left, right):
    return lax.dot_general(
        left, right, (((0,), (0,)), ((), ())), preferred_element_type=jnp.float32
    )


def arbitrary(axes, megabytes):
    return pltpu.CompilerParams(
        dimension_semantics=("arbitrary",) * axes, vmem_limit_bytes=megabytes << 20
    )


def cost(flops, moved, exps=0):
    return pl.CostEstimate(
        flops=int(flops * COST_SCALE),
        bytes_accessed=int(moved * COST_SCALE),
        transcendentals=int(exps * COST_SCALE),
    )


def fixed(shape):
    return pl.BlockSpec(shape, lambda *_: (0,) * len(shape))


def project_kernel(
    groups,
    kv_count,
    place_ref,
    first_ref,
    second_ref,
    gain_ref,
    weight_ref,
    cosine_ref,
    sine_ref,
    head_gain_ref,
    *refs,
):
    normed_ref, heads_ref, raw_ref = refs[-3:]
    size = HEAD_SIZE
    rows = jnp.where(place_ref[1] != 0, first_ref[...], second_ref[...]).astype(jnp.float32)
    scale = lax.rsqrt(jnp.mean(rows * rows, axis=-1, keepdims=True) + EPS)
    normed = (rows * scale * gain_ref[...]).astype(jnp.bfloat16)
    normed_ref[...] = normed
    raw = nn(normed, weight_ref[...])
    cosine, sine_table = cosine_ref[...], sine_ref[...]
    for h in range(kv_count):
        start = h * (groups + 2) * size
        for g in range(groups + 1):
            column = start + g * size
            value = raw[:, column : column + size]
            held = (h * (groups + 1) + g) * size
            raw_ref[:, held : held + size] = value.astype(raw_ref.dtype)
            which = 0 if g < groups else 1
            value = value * lax.rsqrt(jnp.mean(value * value, axis=-1, keepdims=True) + EPS)
            value = value * head_gain_ref[which : which + 1, :]
            value = value * cosine + pltpu.roll(value, size // 2, 1) * sine_table
            if g < groups:
                value = value * QUERY_SCALE
            heads_ref[:, column : column + size] = value.astype(jnp.bfloat16)
        column = start + (groups + 1) * size
        heads_ref[:, column : column + size] = raw[:, column : column + size].astype(jnp.bfloat16)


def project(
    place, first, second, gain, weight, cosine, sine_table, head_gains, groups, before, count
):
    rows, width = first.shape
    positions = count * rows
    columns = weight.shape[1]
    kv_count = columns // ((groups + 2) * HEAD_SIZE)
    held = kv_count * (groups + 1) * HEAD_SIZE
    block = min(256, rows)
    parts = rows // block
    same = lambda i, s: (0, 0)
    here = lambda i, s: (i, 0)
    there = lambda i, s: (s[0] * parts + i, 0)
    in_specs = [
        pl.BlockSpec((block, width), here),
        pl.BlockSpec((block, width), here),
        pl.BlockSpec((1, width), same),
        pl.BlockSpec((width, columns), same),
        pl.BlockSpec((block, HEAD_SIZE), there),
        pl.BlockSpec((block, HEAD_SIZE), there),
        pl.BlockSpec((2, HEAD_SIZE), same),
    ]
    args = [first, second, gain, weight, cosine, sine_table, head_gains]
    aliases = {}
    if before is not None:
        in_specs += [pl.BlockSpec(memory_space=pl.ANY)] * 3
        aliases = {len(args) + 1 + k: k for k in range(3)}
        args += list(before)
    return pl.pallas_call(
        functools.partial(project_kernel, groups, kv_count),
        grid_spec=pltpu.PrefetchScalarGridSpec(
            num_scalar_prefetch=1,
            grid=(parts,),
            in_specs=in_specs,
            out_specs=[
                pl.BlockSpec((block, width), there),
                pl.BlockSpec((block, columns), there),
                pl.BlockSpec((block, held), there),
            ],
        ),
        out_shape=(
            jax.ShapeDtypeStruct((positions, width), jnp.bfloat16),
            jax.ShapeDtypeStruct((positions, columns), jnp.bfloat16),
            jax.ShapeDtypeStruct((positions, held), jnp.bfloat16),
        ),
        input_output_aliases=aliases,
        compiler_params=arbitrary(1, 40),
        cost_estimate=cost(2 * rows * width * columns, 2 * width * columns + 12 * rows * width),
        name="project",
    )(place, *args)


def forward_kernel(block, groups, place_ref, heads_ref, out_ref, total_ref, wide_ref):
    at_query = pl.program_id(1)
    length = place_ref[0]
    size = HEAD_SIZE
    key_lanes = slice(groups * size, (groups + 1) * size)

    @pl.when(at_query == 0)
    def _():
        wide_ref[:, :size] = heads_ref[:, (groups + 1) * size :]
        wide_ref[:, size:] = jnp.ones((wide_ref.shape[0], size), wide_ref.dtype)

    whole = jnp.minimum(at_query, length // block)
    some = jnp.minimum(at_query + 1, (length + block - 1) // block)
    here = pl.ds(pl.multiple_of(at_query * block, block), block)
    queries = [heads_ref[here, g * size : (g + 1) * size] for g in range(groups)]

    def step(at_key, sums, masked):
        start = pl.multiple_of(at_key * block, block)
        keys = heads_ref[pl.ds(start, block), key_lanes]
        wide = wide_ref[pl.ds(start, block), :]
        if masked:
            rows = at_query * block + lax.broadcasted_iota(jnp.int32, (block, block), 0)
            cols = start + lax.broadcasted_iota(jnp.int32, (block, block), 1)
            allowed = (cols <= rows) & (cols < length)
        after = []
        for g in range(groups):
            scores = nt(queries[g], keys)
            if masked:
                scores = jnp.where(allowed, scores, MASKED)
            after.append(sums[g] + nn(jnp.exp2(scores).astype(jnp.bfloat16), wide))
        return tuple(after)

    sums = tuple(jnp.zeros((block, 2 * size), jnp.float32) for _ in range(groups))
    sums = lax.fori_loop(0, whole, lambda j, c: step(j, c, False), sums)
    sums = lax.fori_loop(whole, some, lambda j, c: step(j, c, True), sums)
    for g in range(groups):
        total = sums[g][:, size:]
        out_ref[:, g * size : (g + 1) * size] = (sums[g][:, :size] / total).astype(out_ref.dtype)
        total_ref[g, :, :] = jnp.transpose(jnp.log2(total))[:8, :]


def attend_forward(place, heads, groups, count):
    positions = heads.shape[0]
    rows = positions // count
    block = min(512, rows)
    parts = rows // block
    group_width = (groups + 2) * HEAD_SIZE
    kv_count = heads.shape[1] // group_width
    size = HEAD_SIZE
    width = kv_count * groups * size
    return pl.pallas_call(
        functools.partial(forward_kernel, block, groups),
        grid_spec=pltpu.PrefetchScalarGridSpec(
            num_scalar_prefetch=1,
            grid=(kv_count, positions // block),
            in_specs=[pl.BlockSpec((positions, group_width), lambda h, i, s: (0, h))],
            out_specs=[
                pl.BlockSpec(
                    (None, block, groups * size),
                    lambda h, i, s: (
                        lax.rem(i // parts + count - s[1], count),
                        lax.rem(i, parts),
                        h,
                    ),
                ),
                pl.BlockSpec((groups, 8, block), lambda h, i, s: (h, 0, i)),
            ],
            scratch_shapes=[pltpu.VMEM((positions, 2 * size), jnp.bfloat16)],
        ),
        out_shape=(
            jax.ShapeDtypeStruct((count, rows, width), jnp.bfloat16),
            jax.ShapeDtypeStruct((kv_count * groups, 8, positions), jnp.float32),
        ),
        compiler_params=arbitrary(2, 48),
        cost_estimate=cost(
            4 * positions * positions * width,
            8 * positions * width,
            positions * positions * width // size // 2,
        ),
        name="attend_forward",
    )(place, heads)


def backward_kernel(
    block,
    groups,
    positions,
    count,
    place_ref,
    heads_ref,
    raw_ref,
    cosine_ref,
    sine_ref,
    head_gain_ref,
    out_ref,
    total_ref,
    *refs,
):
    piece_refs = refs[:count]
    grad_raw_ref, gain_ref, query_sums_ref, key_sums_ref, center_ref, grad_ref = refs[count:]
    length = place_ref[0]
    size = HEAD_SIZE
    rows_each = positions // count
    blocks = positions // block
    key_lanes = slice(groups * size, (groups + 1) * size)
    value_lanes = slice((groups + 1) * size, (groups + 2) * size)
    for k in range(count):
        place = lax.rem(place_ref[1] + k, count) * rows_each
        piece_ref = piece_refs[(count - k) % count]
        grad_ref[pl.ds(pl.multiple_of(place, rows_each), rows_each), :] = piece_ref[...]
        for g in range(groups):
            lanes = slice(g * size, (g + 1) * size)
            terms = piece_ref[:, lanes].astype(jnp.float32) * out_ref[k, :, lanes].astype(
                jnp.float32
            )
            center_ref[g, :, pl.ds(pl.multiple_of(place, rows_each), rows_each)] = (
                jnp.broadcast_to(
                    jnp.sum(jnp.transpose(terms), axis=0, keepdims=True), (8, rows_each)
                )
            )
    query_sums_ref[...] = jnp.zeros_like(query_sums_ref)
    whole = length // block
    some = (length + block - 1) // block

    def key_block(j, _):
        start = pl.multiple_of(j * block, block)
        keys = heads_ref[pl.ds(start, block), key_lanes]
        values = heads_ref[pl.ds(start, block), value_lanes]

        def step(i, carry, masked):
            grad_keys, grad_values = carry
            at = pl.multiple_of(i * block, block)
            if masked:
                key_at = start + lax.broadcasted_iota(jnp.int32, (block, block), 0)
                query_at = at + lax.broadcasted_iota(jnp.int32, (block, block), 1)
                allowed = (key_at <= query_at) & (key_at < length)
            for g in range(groups):
                queries = heads_ref[pl.ds(at, block), g * size : (g + 1) * size]
                grads = grad_ref[pl.ds(at, block), g * size : (g + 1) * size]
                scores = nt(keys, queries) - total_ref[g, 0:1, pl.ds(at, block)]
                if masked:
                    scores = jnp.where(allowed, scores, MASKED)
                probs = jnp.exp2(scores)
                grad_attend = nt(values, grads)
                grad_scores = (
                    probs * (grad_attend - center_ref[g, 0:1, pl.ds(at, block)])
                ).astype(jnp.bfloat16)
                grad_values = grad_values + nn(probs.astype(jnp.bfloat16), grads)
                grad_keys = grad_keys + nn(grad_scores, queries)
                query_sums_ref[g, pl.ds(at, block), :] += tn(grad_scores, keys)
            return grad_keys, grad_values

        zero = jnp.zeros((block, size), jnp.float32)
        first = jnp.where(j < whole, jnp.minimum(j + 1, blocks), blocks)
        carry = lax.fori_loop(j, first, lambda i, c: step(i, c, True), (zero, zero))
        grad_keys, grad_values = lax.fori_loop(
            first, blocks, lambda i, c: step(i, c, False), carry
        )
        key_sums_ref[pl.ds(start, block), :] = grad_keys
        grad_raw_ref[pl.ds(start, block), value_lanes] = grad_values.astype(grad_raw_ref.dtype)
        return 0

    lax.fori_loop(0, some, key_block, 0)

    def padding(j, _):
        start = pl.multiple_of(j * block, block)
        key_sums_ref[pl.ds(start, block), :] = jnp.zeros((block, size), jnp.float32)
        grad_raw_ref[pl.ds(start, block), value_lanes] = jnp.zeros(
            (block, size), grad_raw_ref.dtype
        )
        return 0

    lax.fori_loop(some, blocks, padding, 0)

    def head_back(i, carry):
        rows = pl.ds(pl.multiple_of(i * block, block), block)
        cosine, sine_table = cosine_ref[rows, :], sine_ref[rows, :]
        sums = list(carry)
        for g in range(groups + 1):
            lanes = slice(g * size, (g + 1) * size)
            if g < groups:
                grad = query_sums_ref[g, rows, :] * size**-0.5
            else:
                grad = key_sums_ref[rows, :] * (1.0 / math.log2(math.e))
            which = 0 if g < groups else 1
            grad = grad.astype(jnp.bfloat16).astype(jnp.float32)
            grad = grad * cosine - pltpu.roll(grad, size // 2, 1) * sine_table
            value = raw_ref[rows, lanes].astype(jnp.float32)
            scale = lax.rsqrt(jnp.mean(value * value, axis=-1, keepdims=True) + EPS)
            unit = value * scale
            sums[which] = sums[which] + jnp.sum(grad * unit, axis=0, keepdims=True)
            grad = grad * head_gain_ref[which : which + 1, :]
            inner = jnp.mean(grad * unit, axis=-1, keepdims=True)
            grad_raw_ref[rows, lanes] = (scale * (grad - unit * inner)).astype(grad_raw_ref.dtype)
        return tuple(sums)

    zero = jnp.zeros((1, size), jnp.float32)
    sums = lax.fori_loop(0, blocks, head_back, (zero, zero))
    gain_ref[0, 0:1, :] = sums[0]
    gain_ref[0, 1:2, :] = sums[1]


def attend_backward(
    place, heads, raw, cosine, sine_table, head_gains, groups, context, totals, pieces
):
    count = len(pieces)
    positions = heads.shape[0]
    rows = positions // count
    block = min(512, positions)
    size = HEAD_SIZE
    kv_count = heads.shape[1] // ((groups + 2) * size)

    def of_group(lines, columns):
        return pl.BlockSpec((lines, columns * size), lambda h, s: (0, h))

    width = kv_count * groups * size
    return pl.pallas_call(
        functools.partial(backward_kernel, block, groups, positions, count),
        grid_spec=pltpu.PrefetchScalarGridSpec(
            num_scalar_prefetch=1,
            grid=(kv_count,),
            in_specs=[
                of_group(positions, groups + 2),
                of_group(positions, groups + 1),
                fixed(cosine.shape),
                fixed(sine_table.shape),
                fixed(head_gains.shape),
                pl.BlockSpec((count, rows, groups * size), lambda h, s: (0, 0, h)),
                pl.BlockSpec((groups, 8, positions), lambda h, s: (h, 0, 0)),
            ]
            + [of_group(rows, groups)] * count,
            out_specs=[
                of_group(positions, groups + 2),
                pl.BlockSpec((1, 2, size), lambda h, s: (h, 0, 0)),
            ],
            scratch_shapes=[
                pltpu.VMEM((groups, positions, size), jnp.float32),
                pltpu.VMEM((positions, size), jnp.float32),
                pltpu.VMEM((groups, 8, positions), jnp.float32),
                pltpu.VMEM((positions, groups * size), jnp.bfloat16),
            ],
        ),
        out_shape=(
            jax.ShapeDtypeStruct(heads.shape, jnp.bfloat16),
            jax.ShapeDtypeStruct((kv_count, 2, size), jnp.float32),
        ),
        compiler_params=arbitrary(1, 56),
        cost_estimate=cost(
            positions * positions * width,
            2 * positions * width,
            positions * positions * width // size // 20,
        ),
        name="attend_backward",
    )(
        place,
        heads,
        raw,
        cosine,
        sine_table,
        head_gains,
        context,
        totals,
        *pieces,
    )


def tile_of(hidden_units):
    return next(t for t in (512, 384, 256, 128) if hidden_units % t == 0)


def separate(both, tile):
    pieces = [both[:, at : at + tile] for at in range(0, both.shape[1], tile)]
    return jnp.concatenate(pieces[0::2], axis=1), jnp.concatenate(pieces[1::2], axis=1)


def out_norm_kernel(count, weight_ref, rows_ref, gain_ref, *refs):
    resid_ref, normed_ref = refs[count:]
    part = refs[0].shape[-1]
    resid = rows_ref[...].astype(jnp.float32)
    for k in range(count):
        at = (count - k) % count * part
        resid = resid + nn(refs[k][...], weight_ref[at : at + part, :])
    resid_ref[...] = resid
    normed_ref[...] = norm_rows(resid, gain_ref[...]).astype(normed_ref.dtype)


def out_norm(pieces, weight, tokens, gain):
    count = len(pieces)
    rows, part = pieces[0].shape
    width = weight.shape[1]
    block = min(256, rows)
    across = pl.BlockSpec((block, width), lambda i: (i, 0))
    return pl.pallas_call(
        functools.partial(out_norm_kernel, count),
        grid=(rows // block,),
        in_specs=[fixed(weight.shape), across, fixed(gain.shape)]
        + [pl.BlockSpec((block, part), lambda i: (i, 0))] * count,
        out_specs=[across, across],
        out_shape=(
            jax.ShapeDtypeStruct((rows, width), jnp.float32),
            jax.ShapeDtypeStruct((rows, width), jnp.bfloat16),
        ),
        compiler_params=arbitrary(1, 48),
        cost_estimate=cost(2 * rows * count * part * width, 2 * weight.size + 10 * rows * width),
        name="out_norm",
    )(weight, tokens, gain, *pieces)


def hidden_kernel(tile, own_ref, away_ref, weight_ref, *refs):
    both_ref, hidden_ref = refs[-2:]
    rows = own_ref.shape[0]
    for half, rows_ref in enumerate((own_ref, away_ref)):
        here = slice(half * rows, (half + 1) * rows)
        both = nn(rows_ref[...], weight_ref[...])
        both_ref[here, :] = both.astype(both_ref.dtype)
        gate, up = both[:, :tile], both[:, tile:]
        hidden_ref[here, :] = (gate * jax.nn.sigmoid(gate) * up).astype(hidden_ref.dtype)


def hidden_units(own, away, weight, tile, at, total, before):
    rows, width = own.shape
    columns = weight.shape[1]
    tiles = columns // (2 * tile)
    in_specs = [
        fixed(own.shape),
        fixed(away.shape),
        pl.BlockSpec((width, 2 * tile), lambda j: (0, j)),
    ]
    args, aliases = [own, away, weight], {}
    if before is not None:
        in_specs.append(pl.BlockSpec(memory_space=pl.ANY))
        args.append(before)
        aliases = {3: 1}
    return pl.pallas_call(
        functools.partial(hidden_kernel, tile),
        grid=(tiles,),
        in_specs=in_specs,
        out_specs=[
            pl.BlockSpec((2 * rows, 2 * tile), lambda j: (0, j)),
            pl.BlockSpec((2 * rows, tile), lambda j: (0, at * tiles + j)),
        ],
        out_shape=(
            jax.ShapeDtypeStruct((2 * rows, columns), jnp.bfloat16),
            jax.ShapeDtypeStruct((2 * rows, total), jnp.bfloat16),
        ),
        input_output_aliases=aliases,
        compiler_params=arbitrary(1, 56),
        cost_estimate=cost(4 * rows * width * columns, 2 * width * columns + 10 * rows * columns),
        name="hidden_units",
    )(*args)


def hidden_back_kernel(tile, own_ref, away_ref, down_ref, both_ref, out_ref):
    rows = own_ref.shape[0]
    for half, grads_ref in enumerate((own_ref, away_ref)):
        here = slice(half * rows, (half + 1) * rows)
        grad_hidden = nt(grads_ref[...], down_ref[...])
        gate = both_ref[here, :tile].astype(jnp.float32)
        up = both_ref[here, tile:].astype(jnp.float32)
        sigmoid = jax.nn.sigmoid(gate)
        silu = gate * sigmoid
        out_ref[here, :tile] = (grad_hidden * up * (sigmoid + silu * (1.0 - sigmoid))).astype(
            out_ref.dtype
        )
        out_ref[here, tile:] = (grad_hidden * silu).astype(out_ref.dtype)


def hidden_back(own, away, down, both, tile):
    rows, width = own.shape
    columns = both.shape[1]
    pair = pl.BlockSpec((2 * rows, 2 * tile), lambda j: (0, j))
    return pl.pallas_call(
        functools.partial(hidden_back_kernel, tile),
        grid=(columns // (2 * tile),),
        in_specs=[
            fixed(own.shape),
            fixed(away.shape),
            pl.BlockSpec((tile, width), lambda j: (j, 0)),
            pair,
        ],
        out_specs=pair,
        out_shape=jax.ShapeDtypeStruct((2 * rows, columns), jnp.bfloat16),
        compiler_params=arbitrary(1, 56),
        cost_estimate=cost(2 * rows * width * columns, width * columns + 12 * rows * columns),
        name="hidden_back",
    )(own, away, down, both)


def unit_grads_kernel(own_ref, away_ref, grads_ref, out_ref):
    rows = own_ref.shape[0]
    out_ref[...] = (
        tn(own_ref[...], grads_ref[:rows, :]) + tn(away_ref[...], grads_ref[rows:, :])
    ).astype(out_ref.dtype)


def unit_grads(own, away, grads):
    rows, width = own.shape
    columns = grads.shape[1]
    tile = tile_of(columns)
    return pl.pallas_call(
        unit_grads_kernel,
        grid=(columns // tile,),
        in_specs=[
            fixed(own.shape),
            fixed(away.shape),
            pl.BlockSpec((2 * rows, tile), lambda j: (0, j)),
        ],
        out_specs=pl.BlockSpec((width, tile), lambda j: (0, j)),
        out_shape=jax.ShapeDtypeStruct((width, columns), jnp.bfloat16),
        compiler_params=arbitrary(1, 56),
        cost_estimate=cost(4 * rows * width * columns, 2 * width * columns + 4 * rows * columns),
        name="unit_grads",
    )(own, away, grads)


def down_grads_kernel(hidden_ref, own_ref, away_ref, out_ref):
    rows = own_ref.shape[0]
    out_ref[...] = (
        tn(hidden_ref[:rows, :], own_ref[...]) + tn(hidden_ref[rows:, :], away_ref[...])
    ).astype(out_ref.dtype)


def down_grads(hidden, own, away):
    rows, width = own.shape
    units = hidden.shape[1]
    tile = tile_of(units)
    return pl.pallas_call(
        down_grads_kernel,
        grid=(units // tile,),
        in_specs=[
            pl.BlockSpec((2 * rows, tile), lambda j: (0, j)),
            fixed(own.shape),
            fixed(away.shape),
        ],
        out_specs=pl.BlockSpec((tile, width), lambda j: (j, 0)),
        out_shape=jax.ShapeDtypeStruct((units, width), jnp.bfloat16),
        compiler_params=arbitrary(1, 56),
        cost_estimate=cost(4 * rows * width * units, 2 * width * units + 4 * rows * units),
        name="down_grads",
    )(hidden, own, away)


def grad_normed_kernel(parts, *refs):
    grads, weights = refs[:parts], refs[parts : 2 * parts]
    own_ref, away_ref = refs[2 * parts :]
    rows = own_ref.shape[0]
    for half, out_ref in enumerate((own_ref, away_ref)):
        here = slice(half * rows, (half + 1) * rows)
        total = nt(grads[0][here, :], weights[0][...])
        for grad_ref, weight_ref in zip(grads[1:], weights[1:]):
            total = total + nt(grad_ref[here, :], weight_ref[...])
        out_ref[...] = total.astype(out_ref.dtype)


def grad_normed(grads, weights):
    rows = grads[0].shape[0] // 2
    width = weights[0].shape[0]
    tile = tile_of(width)
    return pl.pallas_call(
        functools.partial(grad_normed_kernel, len(grads)),
        grid=(width // tile,),
        in_specs=[fixed(grad.shape) for grad in grads]
        + [pl.BlockSpec((tile, weight.shape[1]), lambda j: (j, 0)) for weight in weights],
        out_specs=[pl.BlockSpec((rows, tile), lambda j: (0, j))] * 2,
        out_shape=(
            jax.ShapeDtypeStruct((rows, width), jnp.float32),
            jax.ShapeDtypeStruct((rows, width), jnp.bfloat16),
        ),
        compiler_params=arbitrary(1, 60),
        cost_estimate=cost(
            sum(2 * grad.size * width for grad in grads),
            sum(2 * grad.size + 2 * weight.size for grad, weight in zip(grads, weights)),
        ),
        name="grad_normed",
    )(*grads, *weights)


def mlp_out_kernel(hidden_ref, *refs):
    own_ref, away_ref = refs[-2:]
    rows = own_ref.shape[0]
    for half, out_ref in enumerate((own_ref, away_ref)):
        here = slice(half * rows, (half + 1) * rows)
        at, total = 0, None
        for down_ref in refs[:-2]:
            units = down_ref.shape[0]
            part = nn(hidden_ref[here, at : at + units], down_ref[...])
            total = part if total is None else total + part
            at += units
        out_ref[...] = total.astype(out_ref.dtype)


def mlp_out(hidden, downs):
    rows = hidden.shape[0] // 2
    width = downs[0].shape[1]
    tile = tile_of(width)
    return pl.pallas_call(
        mlp_out_kernel,
        grid=(width // tile,),
        in_specs=[fixed(hidden.shape)]
        + [pl.BlockSpec((down.shape[0], tile), lambda j: (0, j)) for down in downs],
        out_specs=[pl.BlockSpec((rows, tile), lambda j: (0, j))] * 2,
        out_shape=(
            jax.ShapeDtypeStruct((rows, width), jnp.float32),
            jax.ShapeDtypeStruct((rows, width), jnp.bfloat16),
        ),
        compiler_params=arbitrary(1, 56),
        cost_estimate=cost(2 * hidden.size * width, 4 * hidden.size + 6 * rows * width),
        name="mlp_out",
    )(hidden, *downs)


def resid_back_kernel(
    place_ref,
    own_ref,
    away_ref,
    resid_ref,
    cotangent_ref,
    gain_ref,
    weight_ref,
    grad_ref,
    low_ref,
    sums_ref,
    *piece_refs,
):
    block = own_ref.shape[0]
    part = piece_refs[0].shape[-1]
    first = place_ref[1] + pl.program_id(0) * block
    at = first + lax.broadcasted_iota(jnp.int32, (block, 1), 0)
    valid = (at < place_ref[0]).astype(jnp.float32)
    grads = own_ref[...] + away_ref[...].astype(jnp.float32)
    back, sums = norm_back(resid_ref[...], gain_ref[...], grads)
    grad_resid = valid * cotangent_ref[...].astype(jnp.float32) + back
    grad_ref[...] = grad_resid
    low = grad_resid.astype(jnp.bfloat16)
    low_ref[...] = low
    for k, piece_ref in enumerate(piece_refs):
        piece_ref[...] = nt(low, weight_ref[k * part : (k + 1) * part, :]).astype(piece_ref.dtype)

    @pl.when(pl.program_id(0) == 0)
    def _():
        sums_ref[...] = jnp.zeros_like(sums_ref)

    sums_ref[...] += sums


def resid_back(own, away, resid, cotangent, gain, weight, length, start, count):
    rows, width = own.shape
    part = weight.shape[0] // count
    block = min(256, rows)
    across = pl.BlockSpec((block, width), lambda i, s: (i, 0))
    return pl.pallas_call(
        resid_back_kernel,
        grid_spec=pltpu.PrefetchScalarGridSpec(
            num_scalar_prefetch=1,
            grid=(rows // block,),
            in_specs=[across] * 4 + [fixed(gain.shape), fixed(weight.shape)],
            out_specs=[across, across, fixed(gain.shape)]
            + [pl.BlockSpec((block, part), lambda i, s: (i, 0))] * count,
        ),
        out_shape=(
            jax.ShapeDtypeStruct((rows, width), jnp.float32),
            jax.ShapeDtypeStruct((rows, width), jnp.bfloat16),
            jax.ShapeDtypeStruct(gain.shape, jnp.float32),
        )
        + (jax.ShapeDtypeStruct((rows, part), jnp.bfloat16),) * count,
        compiler_params=arbitrary(1, 56),
        cost_estimate=cost(2 * rows * weight.size, 2 * weight.size + 20 * rows * width),
        name="resid_back",
    )(jnp.stack([length, start]), own, away, resid, cotangent, gain, weight)


def out_grads_kernel(count, grads_ref, *refs):
    out_ref = refs[count]
    part = refs[0].shape[-1]
    for k in range(count):
        at = (count - k) % count * part
        out_ref[at : at + part, :] = tn(refs[k][...], grads_ref[...]).astype(out_ref.dtype)


def out_grads(pieces, grads):
    count = len(pieces)
    rows, part = pieces[0].shape
    width = grads.shape[1]
    tile = tile_of(width)
    return pl.pallas_call(
        functools.partial(out_grads_kernel, count),
        grid=(width // tile,),
        in_specs=[pl.BlockSpec((rows, tile), lambda j: (0, j))]
        + [fixed(piece.shape) for piece in pieces],
        out_specs=pl.BlockSpec((count * part, tile), lambda j: (0, j)),
        out_shape=jax.ShapeDtypeStruct((count * part, width), jnp.bfloat16),
        compiler_params=arbitrary(1, 48),
        cost_estimate=cost(
            2 * rows * count * part * width, 2 * count * part * (rows + width) + 2 * rows * width
        ),
        name="out_grads",
    )(grads, *pieces)


def pack_heads_kernel(groups, query_ref, key_ref, value_ref, gain_ref, out_ref):
    size = HEAD_SIZE
    at = 0
    for h in range(key_ref.shape[1] // size):
        for ref, start, columns in (
            (query_ref, h * groups * size, groups * size),
            (key_ref, h * size, size),
            (value_ref, h * size, size),
        ):
            out_ref[:, at : at + columns] = ref[:, start : start + columns]
            at += columns
    out_ref[:, at:] = gain_ref[...]


def pack_heads(query, key, value, gain, groups):
    rows = query.shape[0]
    columns = query.shape[1] + key.shape[1] + value.shape[1] + gain.shape[1]
    args = (query, key, value, gain)
    return pl.pallas_call(
        functools.partial(pack_heads_kernel, groups),
        grid=(1,),
        in_specs=[fixed(arg.shape) for arg in args],
        out_specs=fixed((rows, columns)),
        out_shape=jax.ShapeDtypeStruct((rows, columns), jnp.bfloat16),
        compiler_params=arbitrary(1, 16),
        cost_estimate=cost(0, 4 * rows * columns),
        name="pack_heads",
    )(*args)


def pack_units_kernel(tile, gate_ref, up_ref, out_ref):
    for at in range(0, gate_ref.shape[1], tile):
        out_ref[:, 2 * at : 2 * at + tile] = gate_ref[:, at : at + tile]
        out_ref[:, 2 * at + tile : 2 * at + 2 * tile] = up_ref[:, at : at + tile]


def pack_units(gate, up, tile):
    rows, columns = gate.shape
    return pl.pallas_call(
        functools.partial(pack_units_kernel, tile),
        grid=(1,),
        in_specs=[fixed(gate.shape), fixed(up.shape)],
        out_specs=fixed((rows, 2 * columns)),
        out_shape=jax.ShapeDtypeStruct((rows, 2 * columns), jnp.bfloat16),
        compiler_params=arbitrary(1, 16),
        cost_estimate=cost(0, 8 * rows * columns),
        name="pack_units",
    )(gate, up)


def tokens_back_kernel(
    own_ref, right_ref, left_ref, rows_ref, gain_ref, resid_ref, out_ref, beside_ref
):
    width = rows_ref.shape[1]
    total = (
        own_ref[...] + right_ref[...].astype(jnp.float32) + left_ref[...].astype(jnp.float32)
    )
    back = norm_back(rows_ref[...].astype(jnp.float32), gain_ref[...], total[:, :width])[0]
    out_ref[...] = (resid_ref[...] + back).astype(out_ref.dtype)
    beside_ref[...] = total[:, width:]


def tokens_back(parts, tokens, gain, grad_resid):
    rows, width = tokens.shape
    more = parts[0].shape[1] - width
    block = min(256, rows)
    across = pl.BlockSpec((block, width), lambda i: (i, 0))
    both = pl.BlockSpec((block, width + more), lambda i: (i, 0))
    return pl.pallas_call(
        tokens_back_kernel,
        grid=(rows // block,),
        in_specs=[both] * 3 + [across, fixed(gain.shape), across],
        out_specs=[across, pl.BlockSpec((block, more), lambda i: (i, 0))],
        out_shape=(
            jax.ShapeDtypeStruct((rows, width), jnp.bfloat16),
            jax.ShapeDtypeStruct((rows, more), jnp.float32),
        ),
        compiler_params=arbitrary(1, 40),
        cost_estimate=cost(20 * rows * width, 16 * rows * width),
        name="tokens_back",
    )(*parts, tokens, gain, grad_resid)


def share_kernel(slot_ref, grads_ref, weight_ref, beside_ref, out_ref):
    width = weight_ref.shape[0]
    out_ref[:, :width] = nt(grads_ref[...], weight_ref[...]).astype(out_ref.dtype)
    out_ref[:, width:] = beside_ref[...].astype(out_ref.dtype)


def share(slot, grads, weight, beside, k, count, dtype):
    positions, columns = grads.shape
    rows = positions // count
    width, more = weight.shape[0], beside.shape[1]
    block = min(256, rows)
    parts = rows // block
    return pl.pallas_call(
        share_kernel,
        grid_spec=pltpu.PrefetchScalarGridSpec(
            num_scalar_prefetch=1,
            grid=(parts,),
            in_specs=[
                pl.BlockSpec((block, columns), lambda i, s: (s[0] * parts + i, 0)),
                fixed(weight.shape),
                pl.BlockSpec((block, more), lambda i, s: (k * parts + i, 0)),
            ],
            out_specs=pl.BlockSpec((block, width + more), lambda i, s: (i, 0)),
        ),
        out_shape=jax.ShapeDtypeStruct((rows, width + more), dtype),
        compiler_params=arbitrary(1, 40),
        cost_estimate=cost(2 * rows * columns * width, 2 * width * columns),
        name="share",
    )(slot, grads, weight, beside)


def heads_back_kernel(normed_ref, grad_ref, weight_ref, out_ref, sums_ref):
    partial = tn(normed_ref[...], grad_ref[...])
    out_ref[...] = partial.astype(out_ref.dtype)
    sums = jnp.sum(partial * weight_ref[...].astype(jnp.float32), axis=1, keepdims=True)
    sums_ref[...] = jnp.broadcast_to(sums, sums_ref.shape)


def heads_back(normed, grads, weight):
    positions, width = normed.shape
    columns = grads.shape[1]
    block = min(512, width)
    return pl.pallas_call(
        heads_back_kernel,
        grid=(width // block,),
        in_specs=[
            pl.BlockSpec((positions, block), lambda j: (0, j)),
            pl.BlockSpec((positions, columns), lambda j: (0, 0)),
            pl.BlockSpec((block, columns), lambda j: (j, 0)),
        ],
        out_specs=[
            pl.BlockSpec((block, columns), lambda j: (j, 0)),
            pl.BlockSpec((block, LANES), lambda j: (j, 0)),
        ],
        out_shape=(
            jax.ShapeDtypeStruct((width, columns), jnp.bfloat16),
            jax.ShapeDtypeStruct((width, LANES), jnp.float32),
        ),
        compiler_params=arbitrary(1, 48),
        cost_estimate=cost(
            2 * positions * width * columns, 2 * positions * (width + columns) + 4 * width * columns
        ),
        name="heads_back",
    )(normed, grads, weight)


def norm_back(value_rows, gain, grads):
    scale = lax.rsqrt(jnp.mean(value_rows * value_rows, axis=-1, keepdims=True) + EPS)
    unit = value_rows * scale
    scaled = grads * gain
    inner = jnp.mean(scaled * unit, axis=-1, keepdims=True)
    return scale * (scaled - unit * inner), jnp.sum(grads * unit, axis=0)


def after(value, *others):
    return lax.optimization_barrier((value, others))[0]


def hop_right(value, count, hop):
    return lax.ppermute(value, "seq", [(i, i + 1) for i in range(hop - 1, count - 1)])


def hop_left(value, count, hop):
    return lax.ppermute(value, "seq", [(i, i - 1) for i in range(1, count - hop + 1)])


def line_scatter(parts, before):
    count = len(parts)
    right, left = None, None
    hops = []
    for hop in range(count - 1):
        to_right, to_left = parts[count - 1 - hop], parts[hop + 1]
        if hop:
            to_right = to_right.astype(jnp.float32) + right.astype(jnp.float32)
            to_left = to_left.astype(jnp.float32) + left.astype(jnp.float32)
        if hop in before:
            to_right, to_left = after((to_right, to_left), *before[hop])
        right = lax.ppermute(
            to_right.astype(jnp.bfloat16), "seq", [(i, i + 1) for i in range(hop + 1)]
        )
        left = lax.ppermute(
            to_left.astype(jnp.bfloat16),
            "seq",
            [(i, i - 1) for i in range(count - 1 - hop, count)],
        )
        hops.append((right, left))
    return (parts[0], right, left), hops


def sum_over(value, axis):
    flat = value.reshape(-1, LANES)
    size = lax.axis_size(axis)
    assert size & (size - 1) == 0
    step = 1
    while step < size:
        flat = flat + lax.ppermute(flat, axis, [(i, i ^ step) for i in range(size)])
        step *= 2
    return flat.reshape(-1)


def swap(value, count):
    return lax.ppermute(value, "seq", [(i, i ^ 1) for i in range(count)])


def fetch(value, count, step):
    return lax.ppermute(value, "seq", [((i + step) % count, i) for i in range(count)])


def give(value, count, step):
    return lax.ppermute(value, "seq", [(i, (i + step) % count) for i in range(count)])


def on_device(
    tokens,
    lengths,
    cotangent,
    w_query,
    key_weight,
    value_weight,
    w_out,
    w_gate,
    w_up,
    w_down,
    norm_attn,
    norm_mlp,
    norm_query,
    norm_key,
):
    slots, rows, width = tokens.shape
    assert slots == 1
    count = lax.axis_size("seq")
    positions = count * rows
    me = lax.axis_index("seq")
    tokens_low = tokens.reshape(rows, width)
    cotangent_low = cotangent.reshape(rows, width)
    length = lengths[0]
    low = jnp.bfloat16
    groups = w_query.shape[1] // key_weight.shape[1]
    kv_count = key_weight.shape[1] // HEAD_SIZE
    units = w_gate.shape[1]
    tile = tile_of(units)
    steps = range(0, count, PAIR)

    def from_groups(both):
        size = HEAD_SIZE
        starts = [h * (groups + 2) * size for h in range(kv_count)]
        ends = (0, groups * size, (groups + 1) * size, (groups + 2) * size)
        return [
            jnp.concatenate([both[:, s + low_end : s + high_end] for s in starts], axis=1)
            for low_end, high_end in zip(ends, ends[1:])
        ]

    weight_rows = w_query.shape[0]
    gain_parts = (norm_attn, norm_mlp, norm_query, norm_key)
    gain_sizes = [part.shape[0] for part in gain_parts]
    own_gains = jnp.concatenate(gain_parts)
    gain_block = jnp.pad(own_gains, (0, weight_rows * LANES - own_gains.shape[0])).reshape(
        weight_rows, LANES
    )
    own_heads = pack_heads(w_query, key_weight, value_weight, gain_block, groups)
    head_columns = own_heads.shape[1] - LANES
    gathered_heads = lax.all_gather(own_heads, "dp", axis=0, tiled=True)
    heads_weight = gathered_heads[:, :head_columns]
    gathered_gains = gathered_heads[:, head_columns:].reshape(-1, weight_rows * LANES)
    rights = [hop_right(tokens_low, count, 1)]
    lefts = [hop_left(tokens_low, count, 1)]
    gains, at = [], 0
    for part_size in gain_sizes:
        gains.append(gathered_gains[:, at : at + part_size].reshape(1, -1).astype(jnp.float32))
        at += part_size
    gain_attn, gain_mlp = gains[:2]
    head_gains = jnp.concatenate(gains[2:], axis=0)
    cosine, sine_table = angles(jnp.arange(positions, dtype=jnp.float32))

    places = [
        jnp.stack([lax.rem(me + k, count), (me + k < count).astype(jnp.int32)])
        for k in range(count)
    ]
    slot_place = jnp.stack([length, me])

    def project_block(k, whole):
        first, second = tokens_low, tokens_low
        if k:
            first, second = lefts[k - 1], rights[count - k - 1]
        return project(
            places[k],
            first,
            second,
            gain_attn,
            heads_weight,
            cosine,
            sine_table,
            head_gains,
            groups,
            whole,
            count,
        )

    own_both = pack_units(w_gate, w_up, tile)
    first_hop = (rights[0], lefts[0])
    both_weights = [lax.all_gather(after(own_both, *first_hop), "dp", axis=0, tiled=True)]
    down_weights = [lax.all_gather(after(w_down, *first_hop), "dp", axis=1, tiled=True)]
    whole = project_block(0, None)
    for hop in range(2, count - 1):
        rights.append(hop_right(rights[-1], count, hop))
        lefts.append(hop_left(lefts[-1], count, hop))
    right, left = after((rights[-1], lefts[-1]), whole[1])
    before_last = (rights[-1], lefts[-1])
    fetched_down = [fetch(after(w_down, *before_last), count, step) for step in steps[1:]]
    rights.append(hop_right(right, count, count - 1))
    lefts.append(hop_left(left, count, count - 1))
    for k in range(2, count - 1):
        whole = project_block(k, whole)
    out_blocks = [w_out] + [
        fetch(after(w_out, *before_last, whole[1]), count, k) for k in range(1, count)
    ]
    gathered = (rights[-1], lefts[-1])
    out_weight = lax.all_gather(
        after(
            jnp.concatenate(out_blocks, axis=0),
            both_weights[0],
            down_weights[0],
            *gathered,
            *fetched_down,
        ),
        "dp",
        axis=1,
        tiled=True,
    )

    fetched_both = [
        fetch(after(own_both, *gathered), count, step) for step in steps[1:]
    ]
    for k in [1, count - 1] if count > 2 else [1]:
        whole = project_block(k, whole)
    normed_attn, heads, raw = whole
    context, totals = attend_forward(slot_place, heads, groups, count)
    sent = context
    context_pieces = [context[0]] + [give(sent[k], count, k) for k in range(1, count)]
    resid, normed_mlp = out_norm(context_pieces, out_weight, tokens_low, gain_mlp)
    away_normed = swap(normed_mlp, count)
    for both, down in zip(fetched_both, fetched_down):
        both_weights.append(lax.all_gather(after(both, context), "dp", axis=0, tiled=True))
        down_weights.append(lax.all_gather(after(down, heads), "dp", axis=1, tiled=True))

    place = jnp.arange(rows, dtype=jnp.int32)[:, None] + me * rows
    valid_rows = (place < length).astype(low)
    grad_rows = cotangent_low * valid_rows
    away_grads = swap(after(grad_rows, away_normed), count)
    hidden, boths = None, []
    for at, weight in enumerate(both_weights):
        both, hidden = hidden_units(
            normed_mlp, away_normed, weight, tile, at, len(steps) * units, hidden
        )
        boths.append(both)

    def spread(partial, axis):
        return lax.psum_scatter(partial, "dp", scatter_dimension=axis, tiled=True)

    down_partial = down_grads(hidden, grad_rows, away_grads)
    grad_rows, away_grads = after((grad_rows, away_grads), down_partial)
    down_sums = spread(down_partial, 1)
    grad_boths = [
        hidden_back(grad_rows, away_grads, down, both, tile)
        for down, both in zip(down_weights, boths)
    ]
    mate_partials = [unit_grads(normed_mlp, away_normed, grad) for grad in grad_boths[1:]]
    mate_sums = [spread(partial, 0) for partial in mate_partials]
    grad_normed_own, grad_normed_away = grad_normed(
        after(grad_boths, *mate_partials), both_weights
    )
    own_partial = unit_grads(normed_mlp, away_normed, after(grad_boths[0], grad_normed_away))
    mlp_own, mlp_away = mlp_out(after(hidden, own_partial), down_weights)
    grad_resid, grad_attn_low, gain_mlp_sums, *pieces = resid_back(
        grad_normed_own,
        after(swap(grad_normed_away, count), own_partial, mlp_own, down_sums),
        resid,
        cotangent_low,
        gain_mlp,
        out_weight,
        length,
        me * rows,
        count,
    )
    pieces = [pieces[0]] + [give(pieces[k], count, k) for k in range(1, count)]
    out_partial = out_grads(context_pieces, grad_attn_low)
    out_sums = spread(out_partial, 1)
    own_sum = spread(after(own_partial, *pieces, out_partial), 0)
    pieces = after(pieces, out_partial, down_sums, *mate_sums)
    grad_raw, head_gain_terms = attend_backward(
        slot_place,
        heads,
        raw,
        cosine,
        sine_table,
        head_gains,
        groups,
        context,
        totals,
        pieces,
    )
    away_both, away_down, mlp_away = after((mate_sums, down_sums, mlp_away), *pieces)
    mlp_away = swap(mlp_away, count)
    given_first, given_second = [
        [give(half, count, step) for step, half in zip(steps[1:], halves)]
        for halves in zip(*(jnp.split(piece, 2, axis=0) for piece in away_both))
    ]
    down_pieces = jnp.split(away_down, len(steps), axis=0)
    given_down = [give(piece, count, step) for step, piece in zip(steps[1:], down_pieces[1:])]
    shares = {}
    for k in [count - 1, 1, *range(2, count - 1), 0]:
        shares[k] = share(
            places[k][:1],
            grad_raw,
            heads_weight,
            out_sums,
            k,
            count,
            low if k else jnp.float32,
        )
    shares[1], shares[count - 1] = after(
        (shares[1], shares[count - 1]), *given_down, *given_first, mlp_away
    )
    shares = [shares[k] for k in range(count)]
    heads_partial, gain_attn_sums = heads_back(
        normed_attn, after(grad_raw, shares[1], shares[-1]), heads_weight
    )
    grad_heads = spread(heads_partial, 0)
    gain_attn_term = gain_attn_sums[:, 0] / gain_attn[0]
    head_gain_sums = jnp.sum(head_gain_terms, axis=0)
    terms = (gain_attn_term, gain_mlp_sums[0], head_gain_sums[0], head_gain_sums[1])
    gain_sums = sum_over(jnp.concatenate(terms), "dp").reshape(-1, LANES)
    gain_parts = [gain_sums] + [give(gain_sums, count, k) for k in range(1, count)]
    last_parts, hops = line_scatter(
        shares,
        {1: (heads_partial, shares[0], *gain_parts[1:], *given_second), 2: (own_sum,)},
    )
    grad_heads = grad_heads.astype(jnp.float32)
    grad_query, grad_key, grad_value = from_groups(grad_heads)
    layer_output = (
        (valid_rows.astype(jnp.float32) * (resid + mlp_own + mlp_away.astype(jnp.float32)))
        .astype(low)
        .reshape(slots, rows, width)
    )
    grad_tokens, grad_out = tokens_back(last_parts, tokens_low, gain_attn, grad_resid)
    grad_tokens = grad_tokens.reshape(slots, rows, width)

    sums = sum(gain_parts).reshape(-1)
    both_total = own_sum.astype(jnp.float32) + sum(
        jnp.concatenate(halves, axis=0).astype(jnp.float32)
        for halves in zip(given_first, given_second)
    )
    grad_gate, grad_up = separate(both_total, tile)
    grad_down = sum([part.astype(jnp.float32) for part in [down_pieces[0], *given_down]])

    gain_grads, at = [], 0
    for term, part_size in zip(terms, gain_sizes):
        gain_grads.append(
            lax.dynamic_slice_in_dim(
                sums[at : at + term.shape[0]], lax.axis_index("dp") * part_size, part_size, 0
            )
        )
        at += term.shape[0]
    return (
        layer_output,
        grad_tokens,
        grad_query,
        grad_key,
        grad_value,
        grad_out,
        grad_gate,
        grad_up,
        grad_down,
        *gain_grads,
    )


def solution(mesh):
    return jax.shard_map(
        on_device,
        mesh=mesh,
        in_specs=(
            P("dp", "seq", None),
            P("dp"),
            P("dp", "seq", None),
            P("dp", "seq"),
            P("dp", "seq"),
            P("dp", "seq"),
            P("seq", "dp"),
            P("dp", "seq"),
            P("dp", "seq"),
            P("seq", "dp"),
            P("dp"),
            P("dp"),
            P("dp"),
            P("dp"),
        ),
        out_specs=(
            P("dp", "seq", None),
            P("dp", "seq", None),
            P("dp", "seq"),
            P("dp", "seq"),
            P("dp", "seq"),
            P("seq", "dp"),
            P("dp", "seq"),
            P("dp", "seq"),
            P("seq", "dp"),
            P("dp"),
            P("dp"),
            P("dp"),
            P("dp"),
        ),
        check_vma=False,
    )
```
